256 devices in a mesh: slab: 64 (over x, z, core), quad: 4 (over y).
Axes of the slice: x: 4, y: 4, z: 8, core: 2. Of those that a mesh axis runs over, the one named last changes fastest.
Arguments:
- right_side: float32 [256, 64, 1024], P('slab', 'quad'), may hold values from -16 to 16
- phase_label: int32 [256, 64, 1024], P('slab', 'quad'), may hold values 0 or 1
- density_gain: float32 [256, 64, 1024], P('slab', 'quad'), may hold values from 0.25 to 1.75
- subdomain: int32 [256, 64, 1024], P('slab', 'quad'), may hold values from 0 to 63, as said below
- block_factor: float32 [64, 256, 256], P('slab', 'quad'), may hold values from -0.03125 to 0.03125
- coupling: float32 [64, 256, 64], P('slab', 'quad'), may hold values from -0.75 to 0.75
Outputs:
- solution_field: float32 [256, 64, 1024], P('slab', 'quad')
- residual: float32 [256, 64, 1024], P('slab', 'quad')
The draws below stay inside these ranges and needn't reach their ends.
Inputs may be any that keep to these rules, and one draw needn't show every extreme that they name: `subdomain`: within each device the subdomains are 8 x 8 contiguous tiles with jagged edges, each spanning the device's z-planes.
All inputs are finite; a program needn't handle non-finite values. No bound on the sum of `phase_label` on one device may be relied on, other than what follows from the above.
Results may differ from the reference program's by a relative error of at most 0.0075.
Values sent between devices are 32-bit elements; how exact they have to be, the bound alone decides.
No kernel may reach another device: no remote copies, remote signals or barrier semaphores. Data moves between devices by JAX's collectives and lax.ppermute only.
A program may use at most 64 MiB of HBM per device.

```python
import jax
import jax.numpy as jnp
from jax import lax

CZ = 4
CY = 16
NX = 1024
LINE = 4
SUB_Y = 8
SUB_X = 8
ITERS = 2
SUBS = 64
COARSE = 256
SLABS = 64
NZ = 256
NY = 64
N_QUAD = 4


def draw_subdomain(key, part):
    keyed = jax.random.fold_in(key, 11)
    key_y, key_x = jax.random.split(keyed)
    jitter_y = jax.random.randint(key_y, (NZ, 1, NX), 0, CY // 2 + 1)
    jitter_x = jax.random.randint(key_x, (NZ, NY, 1), 0, NX // 2 + 1)
    ypos = lax.broadcasted_iota(jnp.int32, (NZ, NY, NX), 1) % CY
    xpos = lax.broadcasted_iota(jnp.int32, (NZ, NY, NX), 2)
    tile_y = jnp.minimum((ypos * SUB_Y + jitter_y) // CY, SUB_Y - 1)
    tile_x = jnp.minimum((xpos * SUB_X + jitter_x) // NX, SUB_X - 1)
    return (tile_y * SUB_X + tile_x).astype(jnp.int32)


def draw_right_side(key, part):
    keyed = jax.random.fold_in(key, 23)
    zpos = lax.broadcasted_iota(jnp.float32, (NZ, NY, NX), 0)
    rising = jnp.exp(jnp.log(3.0) * zpos / max(NZ - 1, 1))
    values = jax.random.truncated_normal(keyed, -5.0, 5.0, (NZ, NY, NX), jnp.float32) * rising
    return values.astype(jnp.float32)


def set_ends(array, own_key, least, top_value):
    shape = array.shape
    spot = [jax.random.randint(jax.random.fold_in(own_key, axis), (), 0, shape[axis]) for axis in range(len(shape))]
    array = array.at[tuple(spot)].set(least)
    longest = shape.index(max(shape))
    spot[longest] = (spot[longest] + 1) % shape[longest]
    return array.at[tuple(spot)].set(top_value)


def level_of(rng, dims, cuts, least, top_value):
    def one(axis_at, parts):
        heights = jax.random.uniform(jax.random.fold_in(jax.random.fold_in(rng, 6), axis_at), (parts,), jnp.float32, least / len(cuts), top_value / len(cuts))
        return jnp.repeat(jnp.exp(heights), dims[axis_at] // parts).reshape((-1,) + (1,) * (len(dims) - axis_at - 1))

    factor_of = one(*cuts[0])
    for cut in cuts[1:]:
        factor_of = factor_of * one(*cut)
    return factor_of


def normal_values(rng, shape, width, reach, cuts=(), dtype=jnp.bfloat16):
    result = width * jax.random.normal(rng, shape, jnp.float32)
    if cuts:
        result = result * level_of(rng, shape, cuts, -0.22, 0.18)
    return jnp.clip(result, -reach, reach).astype(dtype)


def setup_inputs(seed: int = 0) -> dict:
    key_of = jax.random.split(jax.random.key(seed), 7)
    return {
        "right_side": draw_right_side(jax.random.fold_in(key_of[6], 71), 0),
        "phase_label": set_ends((jax.random.randint(key_of[1], (NZ, NY, NX), 0, 4) < 3).astype(jnp.int32), jax.random.fold_in(key_of[1], 1), 0, 1),
        "density_gain": jnp.clip(1.0 + 0.15 * jax.random.normal(key_of[2], (NZ, NY, NX), jnp.float32), 0.25, 1.75),
        "subdomain": draw_subdomain(jax.random.fold_in(key_of[6], 71), 0),
        "block_factor": normal_values(key_of[4], (SLABS, COARSE, COARSE), (0.5 / COARSE), 0.03125, ((0, 64), (1, 4)), jnp.float32),
        "coupling": normal_values(key_of[5], (SLABS, COARSE, SUBS), (1.1 * SUBS) ** -0.5, 0.75, ((0, 64), (1, 4)), jnp.float32),
    }


HIGH = lax.Precision.HIGHEST


def harmonic(here, there):
    return jnp.where(there > 0, 2.0 * here * there / (here + there), here)


def solve_along_line(diag, lower, upper, rhs):
    shape = rhs.shape
    dd = diag.reshape(-1, LINE, shape[1], shape[2])
    lo = lower.reshape(-1, LINE, shape[1], shape[2])
    up = upper.reshape(-1, LINE, shape[1], shape[2])
    rr = rhs.reshape(-1, LINE, shape[1], shape[2])
    gammas = []
    rhos = []
    denom = dd[:, 0]
    gammas.append(-up[:, 0] / denom)
    rhos.append(rr[:, 0] / denom)
    for j in range(1, LINE):
        denom = dd[:, j] + lo[:, j] * gammas[j - 1]
        gammas.append(-up[:, j] / denom)
        rhos.append((rr[:, j] + lo[:, j] * rhos[j - 1]) / denom)
    values = [None] * LINE
    values[LINE - 1] = rhos[LINE - 1]
    for j in range(LINE - 2, -1, -1):
        values[j] = rhos[j] - gammas[j] * values[j + 1]
    return jnp.stack(values, axis=1).reshape(shape)


def reference(right_side, phase_label, density_gain, subdomain, block_factor, coupling):
    mobility = 1.0 / (density_gain * (0.001 + 0.999 * phase_label.astype(jnp.float32)))
    mpad = jnp.pad(mobility, 1)
    kz_lo = harmonic(mobility, mpad[:-2, 1:-1, 1:-1])
    kz_hi = harmonic(mobility, mpad[2:, 1:-1, 1:-1])
    ky_lo = harmonic(mobility, mpad[1:-1, :-2, 1:-1])
    ky_hi = harmonic(mobility, mpad[1:-1, 2:, 1:-1])
    kx_lo = harmonic(mobility, mpad[1:-1, 1:-1, :-2])
    kx_hi = harmonic(mobility, mpad[1:-1, 1:-1, 2:])
    diag = kz_lo + kz_hi + ky_lo + ky_hi + kx_lo + kx_hi

    def apply_a(field):
        vp = jnp.pad(field, 1)
        return (diag * field - kz_lo * vp[:-2, 1:-1, 1:-1] - kz_hi * vp[2:, 1:-1, 1:-1]
                - ky_lo * vp[1:-1, :-2, 1:-1] - ky_hi * vp[1:-1, 2:, 1:-1]
                - kx_lo * vp[1:-1, 1:-1, :-2] - kx_hi * vp[1:-1, 1:-1, 2:])

    zpos = lax.broadcasted_iota(jnp.int32, right_side.shape, 0)
    ypos = lax.broadcasted_iota(jnp.int32, right_side.shape, 1)
    global_id = ((zpos // CZ) * COARSE + (ypos // CY) * SUBS + subdomain).astype(jnp.int32)
    flat_id = global_id.reshape(-1)
    mats = coupling.reshape(SLABS, N_QUAD, SUBS, SUBS)

    def precondition(resid):
        block_part = solve_along_line(diag, kz_lo, kz_hi, resid)
        coarse_in = jax.ops.segment_sum(resid.reshape(-1), flat_id, num_segments=SLABS * COARSE).reshape(SLABS, COARSE)
        coarse_rhs = jnp.einsum("kij,kj->ki", block_factor, coarse_in, precision=HIGH).reshape(SLABS, N_QUAD, SUBS)

        def upward(prev, pair):
            mat, vec = pair
            now = jnp.einsum("qij,qj->qi", mat, prev, precision=HIGH) + vec
            return now, now

        start = jnp.zeros((N_QUAD, SUBS), jnp.float32)
        unused, u_all = lax.scan(upward, start, (mats, coarse_rhs))

        def downward(s_next, pair):
            mat, uval = pair
            wval = uval + s_next
            return jnp.einsum("qji,qj->qi", mat, wval, precision=HIGH), wval

        unused2, w_all = lax.scan(downward, start, (mats, u_all), reverse=True)
        coarse_out = jnp.einsum("kji,kj->ki", block_factor, w_all.reshape(SLABS, COARSE), precision=HIGH)
        return block_part + coarse_out.reshape(-1)[flat_id].reshape(resid.shape)

    solution_field = jnp.zeros_like(right_side)
    residual = right_side
    precond = precondition(residual)
    search_direction = precond
    rz = jnp.sum(residual * precond)
    for step in range(ITERS):
        image = apply_a(search_direction)
        alpha = rz / jnp.sum(search_direction * image)
        solution_field = solution_field + alpha * search_direction
        residual = residual - alpha * image
        if step + 1 < ITERS:
            precond = precondition(residual)
            residual_precond_next = jnp.sum(residual * precond)
            search_direction = precond + (residual_precond_next / rz) * search_direction
            rz = residual_precond_next
    return solution_field, residual
```

```python
import jax
import jax.numpy as jnp
from jax import lax
from jax.experimental import pallas as pl
from jax.experimental.pallas import tpu as pltpu
from jax.sharding import PartitionSpec as P

F32 = jnp.float32
HIGH = lax.Precision.HIGHEST
BOTH = ("slab", "quad")


def sds(*shape):
    return jax.ShapeDtypeStruct(shape, F32)


def call(kernel, outs, scratch=()):
    return pl.pallas_call(kernel, out_shape=outs, scratch_shapes=list(scratch), name=kernel.__name__)


def harmonic(here, there):
    return jnp.where(there > 0, 2.0 * here * there / (here + there), here)


def x_before(plane):
    lane = lax.broadcasted_iota(jnp.int32, plane.shape, 1)
    return jnp.where(lane == 0, 0.0, pltpu.roll(plane, 1, 1))


def x_after(plane):
    width = plane.shape[1]
    lane = lax.broadcasted_iota(jnp.int32, plane.shape, 1)
    return jnp.where(lane == width - 1, 0.0, pltpu.roll(plane, width - 1, 1))


def y_before(plane, halo):
    row = lax.broadcasted_iota(jnp.int32, plane.shape, 0)
    return jnp.where(row == 0, halo, pltpu.roll(plane, 1, 0))


def y_after(plane, halo):
    height = plane.shape[0]
    row = lax.broadcasted_iota(jnp.int32, plane.shape, 0)
    return jnp.where(row == height - 1, halo, pltpu.roll(plane, height - 1, 0))


def lane_of(shape):
    return lax.broadcasted_iota(jnp.int32, shape, len(shape) - 1)


def restrict(sub_ref, field_ref, rows_ref):
    def group(g, unused):
        def tile(t, totals):
            rows = pl.ds(pl.multiple_of((t % 2) * 8, 8), 8)
            sub = sub_ref[t // 2, rows, :]
            field = field_ref[t // 2, rows, :]
            out = []
            for label in range(8):
                picked = jnp.where(sub == g * 8 + label, field, 0.0)
                total = totals[label]
                for j in range(8):
                    total = total + picked[:, j * 128 : (j + 1) * 128]
                out.append(total)
            return tuple(out)

        totals = lax.fori_loop(0, 8, tile, tuple(jnp.zeros((8, 128), F32) for _ in range(8)))
        stacked = jnp.concatenate([jnp.sum(t, axis=0, keepdims=True) for t in totals], axis=0)
        rows_ref[pl.ds(pl.multiple_of(g * 8, 8), 8), :] = stacked
        return unused

    lax.fori_loop(0, 8, group, 0)
    return jnp.sum(rows_ref[...].T, axis=0, keepdims=True)


def look_up(table, index):
    wide = jnp.broadcast_to(table, (8, 128))
    rows = []
    for r in range(index.shape[0] // 8):
        parts = []
        for c in range(index.shape[1] // 128):
            part = index[r * 8 : (r + 1) * 8, c * 128 : (c + 1) * 128]
            parts.append(jnp.take_along_axis(wide, part, axis=1, mode="promise_in_bounds"))
        rows.append(jnp.concatenate(parts, axis=1))
    return jnp.concatenate(rows, axis=0)


def solve_lines(kz, inv, gam, rhs):
    rho = [rhs[0] * inv[0]]
    for j in range(1, 4):
        rho.append((rhs[j] + kz[j] * rho[j - 1]) * inv[j])
    out = [None] * 4
    out[3] = rho[3]
    for j in (2, 1, 0):
        out[j] = rho[j] - gam[j] * out[j + 1]
    return out


def begin(rs, ph, gain, sub, fac, mob, zup, zdn, yup, ydn, pay, rows):
    for z in range(4):
        m = 1.0 / (gain[z] * (0.001 + 0.999 * ph[z].astype(F32)))
        s = (sub[z] + 1).astype(F32)
        mob[z] = m
        yup[z : z + 1, :] = m[15:16, :]
        yup[z + 4 : z + 5, :] = s[15:16, :]
        ydn[z : z + 1, :] = m[0:1, :]
        ydn[z + 4 : z + 5, :] = s[0:1, :]
        if z == 0:
            zdn[0] = m
            zdn[1] = s
        if z == 3:
            zup[0] = m
            zup[1] = s
    cin = restrict(sub, rs, rows)
    both = jnp.concatenate([cin, cin], axis=1)
    lane = lane_of((64, 128))
    row = lax.broadcasted_iota(jnp.int32, (64, 128), 0)
    tail = jnp.where(row == 0, both, 0.0)
    for q in range(4):
        block = fac[:, (q // 2) * 128 : (q // 2 + 1) * 128]
        if q % 2:
            block = pltpu.roll(block, 64, 1)
        pay[q] = jnp.where(lane < 64, block, tail)


def setup(rs, mob, zlo, zhi, ylo, yhi, fac, cou, got, kz, kyl, kyh, kxl, kxh, diag, inv, gam, bj, bzu, bzd, byu, byd, pay):
    odd = lax.axis_index("slab") % 2
    planes = [mob[z] for z in range(4)]
    below = [zlo[0]] + planes[:3]
    above = planes[1:] + [zhi[0]]
    faces = [harmonic(planes[z], below[z]) for z in range(4)]
    faces.append(harmonic(planes[3], above[3]))
    for z in range(5):
        kz[z] = faces[z]
    diags = []
    for z in range(4):
        m = planes[z]
        a = harmonic(m, y_before(m, ylo[z : z + 1, :]))
        b = harmonic(m, y_after(m, yhi[z : z + 1, :]))
        c = harmonic(m, x_before(m))
        d = harmonic(m, x_after(m))
        kyl[z] = a
        kyh[z] = b
        kxl[z] = c
        kxh[z] = d
        total = faces[z] + faces[z + 1] + a + b + c + d
        diag[z] = total
        diags.append(total)
    invs = [1.0 / diags[0]]
    gams = [-faces[1] * invs[0]]
    for j in range(1, 4):
        invs.append(1.0 / (diags[j] + faces[j] * gams[j - 1]))
        gams.append(-faces[j + 1] * invs[j])
    for j in range(4):
        inv[j] = invs[j]
    for j in range(3):
        gam[j] = gams[j]
    out = solve_lines(faces, invs, gams, [rs[z] for z in range(4)])
    for z in range(4):
        bj[z] = out[z]
        byu[z : z + 1, :] = out[z][15:16, :]
        byd[z : z + 1, :] = out[z][0:1, :]
    bzu[0] = out[3]
    bzd[0] = out[0]
    cins = [pltpu.roll(got[q][0:8, :], 64, 1)[0:1, :64] for q in range(4)]
    cin = jnp.concatenate(cins, axis=1)
    rhs = lax.dot_general(
        jnp.broadcast_to(cin, (8, 256)), fac[...], (((1,), (1,)), ((), ())), precision=HIGH, preferred_element_type=F32
    )
    flag = jnp.broadcast_to(odd, (64, 64)) == 1
    mat = jnp.where(flag, cou[...], cou[...].T)
    packed = jnp.concatenate([mat[:32, :], mat[32:, :]], axis=1)
    tail = jnp.concatenate([rhs, rhs], axis=1)
    for m in range(32):
        pay[m, 0:32, :] = packed
        pay[m, 32:40, :] = tail


def chain(own, other, rhs_ref, fac, facm, facp, out, mats, us, uc, ws, wc, core):
    odd = lax.axis_index("slab") % 2
    lane = lane_of((32, 128))
    low = lane < 64
    for m in range(32):
        for j, src in ((0, own), (1, other)):
            packed = src[m, 0:32, :]
            at = 2 * m + (odd if j == 0 else 1 - odd)
            mats[at, 0:32, :] = jnp.where(low, packed, 0.0)
            mats[at, 32:64, :] = jnp.where(low, pltpu.roll(packed, 64, 1), 0.0)
    cols = rhs_ref[...].T
    row = rhs_ref[0:1, :]
    us[0:1, :] = row
    col = None
    for k in range(1, 64):
        if k % 2:
            col = jnp.sum(mats[k] * row, axis=1, keepdims=True) + cols[:64, k : k + 1]
            uc[k] = jnp.broadcast_to(col, (64, 128))
        else:
            row = jnp.sum(mats[k] * col, axis=0, keepdims=True) + rhs_ref[k : k + 1, :]
            us[k : k + 1, :] = row
    ws[0:8, :] = jnp.zeros((8, 128), F32)
    wc[0] = jnp.zeros((64, 128), F32)
    wc[65] = jnp.zeros((64, 128), F32)
    wc[64] = jnp.broadcast_to(col, (64, 128))
    for k in range(63, 0, -1):
        if k % 2:
            row = jnp.sum(mats[k] * col, axis=0, keepdims=True) + us[k - 1 : k, :]
            ws[k : k + 1, :] = row
        else:
            col = jnp.sum(mats[k] * row, axis=1, keepdims=True) + uc[k - 1][:, 0:1]
            wc[k] = jnp.broadcast_to(col, (64, 128))
    slab = lax.axis_index("slab")
    for j, (shift, table) in enumerate(((0, fac), (-1, facm), (1, facp))):
        at = slab + shift + 1
        from_row = ws[pl.ds(jnp.minimum(at, 63), 1), :]
        from_col = wc[at].T[0:1, :]
        is_row = jnp.broadcast_to(at % 2, (1, 64)) == 1
        w = jnp.where(is_row, from_row[:, :64], from_col)
        part = jnp.dot(jnp.broadcast_to(w, (8, 64)), table[...], precision=HIGH, preferred_element_type=F32)
        for q in range(4):
            out[q, 2 * j : 2 * j + 1, :] = part[0:1, :128]
            out[q, 2 * j + 1 : 2 * j + 2, :] = part[0:1, 128:]
    for q in range(4):
        out[q, 6:8, :] = jnp.zeros((2, 128), F32)


def chain_first(own, other, fac, facm, facp, out, mats, us, uc, ws, wc, rhs):
    odd = lax.axis_index("slab") % 2
    lane = lane_of((1, 128))
    for m in range(32):
        for j, src in ((0, own), (1, other)):
            at = 2 * m + (odd if j == 0 else 1 - odd)
            rhs[pl.ds(at, 1), :] = jnp.where(lane < 64, src[m, 32:33, :], 0.0)
    chain(own, other, rhs, fac, facm, facp, out, mats, us, uc, ws, wc, None)


def chain_second(own, other, got, fac, facm, facp, out, dots, mats, us, uc, ws, wc, rhs):
    total = got[pl.ds(0, 64, 4), :]
    for q in range(1, 4):
        total = total + got[pl.ds(q, 64, 4), :]
    rhs[...] = jnp.where(lane_of((64, 128)) < 64, total, 0.0)
    dots[...] = jnp.broadcast_to(jnp.sum(total, axis=0, keepdims=True), (8, 128))
    chain(own, other, rhs, fac, facm, facp, out, mats, us, uc, ws, wc, None)


def tables(got):
    quad = lax.axis_index("quad")
    total = got[0] + got[1] + got[2] + got[3]
    near = pltpu.roll(total, 1, 1)
    far = pltpu.roll(total, 65, 1)
    lane = lane_of((1, 128))
    valid = (lane >= 1) & (lane <= 64)

    def table(base, q):
        first = jnp.where(jnp.broadcast_to(q % 2, (1, 128)) == 1, far[base : base + 1, :], near[base : base + 1, :])
        second = jnp.where(
            jnp.broadcast_to(q % 2, (1, 128)) == 1, far[base + 1 : base + 2, :], near[base + 1 : base + 2, :]
        )
        picked = jnp.where(jnp.broadcast_to(q, (1, 128)) >= 2, second, first)
        return jnp.where(valid, picked, 0.0)

    return (
        table(0, quad),
        table(0, jnp.maximum(quad - 1, 0)),
        table(0, jnp.minimum(quad + 1, 3)),
        table(2, quad),
        table(4, quad),
    )


def apply(got, bj, zlo, zhi, ylo, yhi, bzl, bzh, byl, byh, sub, kz, kyl, kyh, kxl, kxh, diag):
    own, t_yl, t_yh, t_zl, t_zh = tables(got)
    planes = [bj[z] + look_up(own, sub[z] + 1) for z in range(4)]
    below = bzl[0] + look_up(t_zl, zlo[1].astype(jnp.int32))
    above = bzh[0] + look_up(t_zh, zhi[1].astype(jnp.int32))
    before = byl[...] + look_up(t_yl, jnp.minimum(ylo[...], 64.0).astype(jnp.int32))[4:8, :]
    after = byh[...] + look_up(t_yh, jnp.minimum(yhi[...], 64.0).astype(jnp.int32))[4:8, :]
    lower = [below] + planes[:3]
    upper = planes[1:] + [above]
    images = []
    for z in range(4):
        v = planes[z]
        images.append(
            diag[z] * v
            - kz[z] * lower[z]
            - kz[z + 1] * upper[z]
            - kyl[z] * y_before(v, before[z : z + 1, :])
            - kyh[z] * y_after(v, after[z : z + 1, :])
            - kxl[z] * x_before(v)
            - kxh[z] * x_after(v)
        )
    return planes, images


def total_of(lefts, rights):
    acc = lefts[0] * rights[0]
    for a, b in zip(lefts[1:], rights[1:]):
        acc = acc + a * b
    return jnp.sum(jnp.sum(acc, axis=0, keepdims=True), axis=1, keepdims=True)


def first(
    got, bj, zlo, zhi, ylo, yhi, bzl, bzh, byl, byh, sub, kz, kyl, kyh, kxl, kxh, diag, rs, inv, gam, cols,
    z_out, q_out, bj_out, bzu, bzd, byu, byd, pay, rows,
):
    planes, images = apply(got, bj, zlo, zhi, ylo, yhi, bzl, bzh, byl, byh, sub, kz, kyl, kyh, kxl, kxh, diag)
    for z in range(4):
        z_out[z] = planes[z]
        q_out[z] = images[z]
    rz = total_of([rs[z] for z in range(4)], planes)
    pq = total_of(planes, images)
    out = solve_lines([kz[z] for z in range(4)], [inv[z] for z in range(4)], [gam[z] for z in range(3)], images)
    for z in range(4):
        bj_out[z] = out[z]
        byu[z : z + 1, :] = out[z][15:16, :]
        byd[z : z + 1, :] = out[z][0:1, :]
    bzu[0] = out[3]
    bzd[0] = out[0]
    cin = jnp.broadcast_to(restrict(sub, q_out, rows), (8, 64))
    lane = lane_of((1, 128))
    parts = []
    for q in range(4):
        part = lax.dot_general(
            cin, cols[q][:, :64], (((1,), (1,)), ((), ())), precision=HIGH, preferred_element_type=F32
        )[0:1, :]
        part = jnp.concatenate([part, part], axis=1)
        parts.append(jnp.where(lane < 64, part, jnp.where(lane == 64, rz, jnp.where(lane == 65, pq, 0.0))))
    tile = jnp.concatenate(parts + parts, axis=0)
    for j in range(32):
        pay[j * 8 : (j + 1) * 8, :] = tile


def second(
    got, bj, zlo, zhi, ylo, yhi, bzl, bzh, byl, byh, sub, kz, kyl, kyh, kxl, kxh, diag, rs, z0, q0, dots,
    z_out, g_out, r_out, pay,
):
    planes, images = apply(got, bj, zlo, zhi, ylo, yhi, bzl, bzh, byl, byh, sub, kz, kyl, kyh, kxl, kxh, diag)
    alpha = dots[0:1, 64:65] / dots[0:1, 65:66]
    zs, gs, rr = [], [], []
    for z in range(4):
        rr.append(rs[z] - alpha * q0[z])
        zs.append(z0[z] - alpha * planes[z])
        gs.append(q0[z] - alpha * images[z])
        z_out[z] = zs[z]
        g_out[z] = gs[z]
        r_out[z] = rr[z]
    new = total_of(rr, zs)
    own = total_of(zs, gs)
    cross = total_of([z0[z] for z in range(4)], gs)
    lane = lane_of((8, 128))
    tile = jnp.where(lane == 0, new, jnp.where(lane == 1, own, jnp.where(lane == 2, cross, 0.0)))
    for j in range(32):
        pay[j * 8 : (j + 1) * 8, :] = tile


def last(got, dots, z0, q0, z1, g1, r1, x_out, r_out):
    total = jnp.sum(got[...], axis=0, keepdims=True)
    new, own, cross = total[:, 0:1], total[:, 1:2], total[:, 2:3]
    rz, pq = dots[0:1, 64:65], dots[0:1, 65:66]
    alpha = rz / pq
    beta = new / rz
    step = new / (own + 2.0 * beta * cross + beta * beta * pq)
    for z in range(4):
        x_out[z] = alpha * z0[z] + step * (z1[z] + beta * z0[z])
        r_out[z] = r1[z] - step * (g1[z] + beta * q0[z])


def body(right_side, phase_label, density_gain, subdomain, block_factor, coupling):
    slabs, quads = lax.axis_size("slab"), lax.axis_size("quad")
    fac, cou = block_factor[0], coupling[0]
    grid = sds(4, 16, 1024)
    up = [(i, i + 1) for i in range(slabs - 1)]
    down = [(j, i) for i, j in up]
    forth = [(i, i + 1) for i in range(quads - 1)]
    back = [(j, i) for i, j in forth]
    cores = [[i for i in range(slabs) if i % 2 == c] for c in range(2)]

    def exchange(value, axis, groups=None):
        return lax.all_to_all(value, axis, 0, 0, tiled=True, axis_index_groups=groups)

    def halo(zu, zd, yu, yd):
        return (
            lax.ppermute(zu, "slab", up),
            lax.ppermute(zd, "slab", down),
            lax.ppermute(yu, "quad", forth),
            lax.ppermute(yd, "quad", back),
        )

    facm = lax.ppermute(fac, "slab", up)
    facp = lax.ppermute(fac, "slab", down)
    mob, *faces, pay = call(
        begin,
        (grid, sds(2, 16, 1024), sds(2, 16, 1024), sds(8, 1024), sds(8, 1024), sds(4, 64, 128)),
        [pltpu.VMEM((64, 128), F32)],
    )(right_side, phase_label, density_gain, subdomain, fac)
    sides = halo(*faces)
    got = exchange(pay, "quad")
    kz, kyl, kyh, kxl, kxh, diag, inv, gam, bj, *ends, pay = call(
        setup,
        (sds(5, 16, 1024), grid, grid, grid, grid, grid, grid, sds(3, 16, 1024), grid)
        + (sds(1, 16, 1024), sds(1, 16, 1024), sds(4, 1024), sds(4, 1024), sds(32, 40, 128)),
    )(right_side, mob, *sides, fac, cou, got)
    bjs = halo(*ends)
    own = exchange(pay, "slab", cores)
    other = lax.ppermute(own, "slab", [(i, i ^ 1) for i in range(slabs)])
    work = [
        pltpu.VMEM((64, 64, 128), F32),
        pltpu.VMEM((64, 128), F32),
        pltpu.VMEM((64, 64, 128), F32),
        pltpu.VMEM((64, 128), F32),
        pltpu.VMEM((66, 64, 128), F32),
        pltpu.VMEM((64, 128), F32),
    ]
    part = call(chain_first, sds(4, 8, 128), work)(own, other, fac, facm, facp)
    coarse = exchange(part, "quad")
    stencil = (kz, kyl, kyh, kxl, kxh, diag)
    z0, q0, bj1, *ends, pay = call(
        first,
        (grid, grid, grid, sds(1, 16, 1024), sds(1, 16, 1024), sds(4, 1024), sds(4, 1024), sds(256, 128)),
        [pltpu.VMEM((64, 128), F32)],
    )(coarse, bj, *sides, *bjs, subdomain, *stencil, right_side, inv, gam, got)
    bjs = halo(*ends)
    everyone = exchange(pay.reshape(256, 1, 128), BOTH).reshape(256, 128)
    part, dots = call(chain_second, (sds(4, 8, 128), sds(8, 128)), work)(own, other, everyone, fac, facm, facp)
    coarse = exchange(part, "quad")
    z1, g1, r1, pay = call(second, (grid, grid, grid, sds(256, 128)))(
        coarse, bj1, *sides, *bjs, subdomain, *stencil, right_side, z0, q0, dots
    )
    everyone = exchange(pay.reshape(256, 1, 128), BOTH).reshape(256, 128)
    return tuple(call(last, (grid, grid))(everyone, dots, z0, q0, z1, g1, r1))


def solution(mesh):
    spec = P("slab", "quad", None)
    return jax.shard_map(body, mesh=mesh, in_specs=(spec,) * 6, out_specs=(spec, spec), check_vma=False)
```

```python
import jax
import jax.numpy as jnp
from jax import lax
from jax.experimental import pallas as pl
from jax.experimental.pallas import tpu as pltpu
from jax.sharding import PartitionSpec as P

F32 = jnp.float32
HIGH = lax.Precision.HIGHEST
BOTH = ("slab", "quad")


def sds(*shape):
    return jax.ShapeDtypeStruct(shape, F32)


def call(kernel, outs, scratch=()):
    return pl.pallas_call(kernel, out_shape=outs, scratch_shapes=list(scratch), name=kernel.__name__)


def harmonic(here, there):
    return jnp.where(there > 0, 2.0 * here * there / (here + there), here)


def x_before(plane):
    lane = lax.broadcasted_iota(jnp.int32, plane.shape, 1)
    return jnp.where(lane == 0, 0.0, pltpu.roll(plane, 1, 1))


def x_after(plane):
    width = plane.shape[1]
    lane = lax.broadcasted_iota(jnp.int32, plane.shape, 1)
    return jnp.where(lane == width - 1, 0.0, pltpu.roll(plane, width - 1, 1))


def y_before(plane, halo):
    row = lax.broadcasted_iota(jnp.int32, plane.shape, 0)
    return jnp.where(row == 0, halo, pltpu.roll(plane, 1, 0))


def y_after(plane, halo):
    height = plane.shape[0]
    row = lax.broadcasted_iota(jnp.int32, plane.shape, 0)
    return jnp.where(row == height - 1, halo, pltpu.roll(plane, height - 1, 0))


def lane_of(shape):
    return lax.broadcasted_iota(jnp.int32, shape, len(shape) - 1)


def restrict(sub_ref, field_ref, rows_ref):
    def group(g, unused):
        def tile(t, totals):
            rows = pl.ds(pl.multiple_of((t % 2) * 8, 8), 8)
            sub = sub_ref[t // 2, rows, :]
            field = field_ref[t // 2, rows, :]
            out = []
            for label in range(8):
                picked = jnp.where(sub == g * 8 + label, field, 0.0)
                total = totals[label]
                for j in range(8):
                    total = total + picked[:, j * 128 : (j + 1) * 128]
                out.append(total)
            return tuple(out)

        totals = lax.fori_loop(0, 8, tile, tuple(jnp.zeros((8, 128), F32) for _ in range(8)))
        stacked = jnp.concatenate([jnp.sum(t, axis=0, keepdims=True) for t in totals], axis=0)
        rows_ref[pl.ds(pl.multiple_of(g * 8, 8), 8), :] = stacked
        return unused

    lax.fori_loop(0, 8, group, 0)
    return jnp.sum(rows_ref[...].T, axis=0, keepdims=True)


def look_up(table, index):
    wide = jnp.broadcast_to(table, (8, 128))
    rows = []
    for r in range(index.shape[0] // 8):
        parts = []
        for c in range(index.shape[1] // 128):
            part = index[r * 8 : (r + 1) * 8, c * 128 : (c + 1) * 128]
            parts.append(jnp.take_along_axis(wide, part, axis=1, mode="promise_in_bounds"))
        rows.append(jnp.concatenate(parts, axis=1))
    return jnp.concatenate(rows, axis=0)


def solve_lines(kz, inv, gam, rhs):
    rho = [rhs[0] * inv[0]]
    for j in range(1, 4):
        rho.append((rhs[j] + kz[j] * rho[j - 1]) * inv[j])
    out = [None] * 4
    out[3] = rho[3]
    for j in (2, 1, 0):
        out[j] = rho[j] - gam[j] * out[j + 1]
    return out


def parity():
    return lax.axis_index("slab") % 2


def choose(flag, a, b):
    return jnp.where(jnp.broadcast_to(flag, a.shape) == 1, a, b)


def spread(out, at, plane):
    h = plane.shape[0]
    for c in range(8):
        out[at + c * h : at + (c + 1) * h, :] = plane[:, c * 128 : (c + 1) * 128]


def gather_rows(block, at, h):
    return jnp.concatenate([block[at + c * h : at + (c + 1) * h, :] for c in range(8)], axis=1)


def face_for(dest, upward, downward):
    return choose((lax.axis_index("quad") + 1 == dest).astype(jnp.int32), upward, downward)


def begin(rs, ph, gain, sub, fac, mob, core, near, pay, rows):
    odd = parity()
    ms, ss = [], []
    for z in range(4):
        m = 1.0 / (gain[z] * (0.001 + 0.999 * ph[z].astype(F32)))
        mob[z] = m
        ms.append(m)
        ss.append((sub[z] + 1).astype(F32))
    spread(core, 0, choose(odd, ms[0], ms[3]))
    spread(core, 128, choose(odd, ss[0], ss[3]))
    spread(near, 0, choose(odd, ms[3], ms[0]))
    spread(near, 128, choose(odd, ss[3], ss[0]))
    for part in (core, near):
        part[256:320, :] = fac[:, :128]
        part[320:384, :] = fac[:, 128:]
    upward = jnp.concatenate([m[15:16, :] for m in ms] + [s[15:16, :] for s in ss], axis=0)
    downward = jnp.concatenate([m[0:1, :] for m in ms] + [s[0:1, :] for s in ss], axis=0)
    cin = restrict(sub, rs, rows)
    both = jnp.concatenate([cin, cin], axis=1)
    lane = lane_of((64, 128))
    row = lax.broadcasted_iota(jnp.int32, (64, 128), 0)
    tail = jnp.where(row == 0, both, 0.0)
    for q in range(4):
        block = fac[:, (q // 2) * 128 : (q // 2 + 1) * 128]
        if q % 2:
            block = pltpu.roll(block, 64, 1)
        pay[q, 0:64, :] = jnp.where(lane < 64, block, tail)
        spread(pay.at[q], 64, face_for(q, upward, downward))


def send_faces(out, to_core, to_near, ups, downs):
    odd = parity()
    to_core[...] = choose(odd, out[0], out[3])
    to_near[...] = choose(odd, out[3], out[0])
    for z in range(4):
        ups[z : z + 1, :] = out[z][15:16, :]
        downs[z : z + 1, :] = out[z][0:1, :]


def setup(
    rs, mob, core, near, fac, cou, got, kz, kyl, kyh, kxl, kxh, diag, inv, gam, bj, to_core, to_near, ups, downs, zsub, ysub, pay
):
    odd = parity()
    quad = lax.axis_index("quad")
    planes = [mob[z] for z in range(4)]
    c_mob, n_mob = gather_rows(core, 0, 16), gather_rows(near, 0, 16)
    c_sub, n_sub = gather_rows(core, 128, 16), gather_rows(near, 128, 16)
    below = [choose(odd, c_mob, n_mob)] + planes[:3]
    above = planes[1:] + [choose(odd, n_mob, c_mob)]
    zsub[0] = choose(odd, c_sub, n_sub).astype(jnp.int32)
    zsub[1] = choose(odd, n_sub, c_sub).astype(jnp.int32)
    before = gather_rows(got[jnp.maximum(quad - 1, 0)], 64, 8)
    after = gather_rows(got[jnp.minimum(quad + 1, 3)], 64, 8)
    ylo = jnp.where(jnp.broadcast_to(quad, before.shape) > 0, before, 0.0)
    yhi = jnp.where(jnp.broadcast_to(quad, after.shape) < 3, after, 0.0)
    ysub[...] = jnp.concatenate([ylo[4:8, :], yhi[4:8, :]], axis=0).astype(jnp.int32)
    faces = [harmonic(planes[z], below[z]) for z in range(4)]
    faces.append(harmonic(planes[3], above[3]))
    for z in range(5):
        kz[z] = faces[z]
    diags = []
    for z in range(4):
        m = planes[z]
        a = harmonic(m, y_before(m, ylo[z : z + 1, :]))
        b = harmonic(m, y_after(m, yhi[z : z + 1, :]))
        c = harmonic(m, x_before(m))
        d = harmonic(m, x_after(m))
        kyl[z] = a
        kyh[z] = b
        kxl[z] = c
        kxh[z] = d
        total = faces[z] + faces[z + 1] + a + b + c + d
        diag[z] = total
        diags.append(total)
    invs = [1.0 / diags[0]]
    gams = [-faces[1] * invs[0]]
    for j in range(1, 4):
        invs.append(1.0 / (diags[j] + faces[j] * gams[j - 1]))
        gams.append(-faces[j + 1] * invs[j])
    for j in range(4):
        inv[j] = invs[j]
    for j in range(3):
        gam[j] = gams[j]
    out = solve_lines(faces, invs, gams, [rs[z] for z in range(4)])
    for z in range(4):
        bj[z] = out[z]
    send_faces(out, to_core, to_near, ups, downs)
    cins = [pltpu.roll(got[q][0:8, :], 64, 1)[0:1, :64] for q in range(4)]
    cin = jnp.concatenate(cins, axis=1)
    rhs = lax.dot_general(
        jnp.broadcast_to(cin, (8, 256)), fac[...], (((1,), (1,)), ((), ())), precision=HIGH, preferred_element_type=F32
    )
    flag = jnp.broadcast_to(odd, (64, 64)) == 1
    mat = jnp.where(flag, cou[...], cou[...].T)
    packed = jnp.concatenate([mat[:32, :], mat[32:, :]], axis=1)
    tail = jnp.concatenate([rhs, rhs], axis=1)
    for m in range(32):
        pay[m, 0:32, :] = packed
        pay[m, 32:40, :] = tail


def chain(own, other, rhs_ref, fac, core, near, ups, downs, out, mats, us, uc, ws, wc):
    odd = lax.axis_index("slab") % 2
    lane = lane_of((32, 128))
    low = lane < 64
    for m in range(32):
        for j, src in ((0, own), (1, other)):
            packed = src[m, 0:32, :]
            at = 2 * m + (odd if j == 0 else 1 - odd)
            mats[at, 0:32, :] = jnp.where(low, packed, 0.0)
            mats[at, 32:64, :] = jnp.where(low, pltpu.roll(packed, 64, 1), 0.0)
    cols = rhs_ref[...].T
    row = rhs_ref[0:1, :]
    us[0:1, :] = row
    col = None
    for k in range(1, 64):
        if k % 2:
            col = jnp.sum(mats[k] * row, axis=1, keepdims=True) + cols[:64, k : k + 1]
            uc[k] = jnp.broadcast_to(col, (64, 128))
        else:
            row = jnp.sum(mats[k] * col, axis=0, keepdims=True) + rhs_ref[k : k + 1, :]
            us[k : k + 1, :] = row
    ws[0:8, :] = jnp.zeros((8, 128), F32)
    wc[0] = jnp.zeros((64, 128), F32)
    wc[65] = jnp.zeros((64, 128), F32)
    wc[64] = jnp.broadcast_to(col, (64, 128))
    for k in range(63, 0, -1):
        if k % 2:
            row = jnp.sum(mats[k] * col, axis=0, keepdims=True) + us[k - 1 : k, :]
            ws[k : k + 1, :] = row
        else:
            col = jnp.sum(mats[k] * row, axis=1, keepdims=True) + uc[k - 1][:, 0:1]
            wc[k] = jnp.broadcast_to(col, (64, 128))
    slab = lax.axis_index("slab")
    c_fac = jnp.concatenate([core[256:320, :], core[320:384, :]], axis=1)
    n_fac = jnp.concatenate([near[256:320, :], near[320:384, :]], axis=1)
    shares = ((0, fac[...]), (-1, choose(odd, c_fac, n_fac)), (1, choose(odd, n_fac, c_fac)))
    for j, (shift, table) in enumerate(shares):
        at = slab + shift + 1
        from_row = ws[pl.ds(jnp.minimum(at, 63), 1), :]
        from_col = wc[at].T[0:1, :]
        is_row = jnp.broadcast_to(at % 2, (1, 64)) == 1
        w = jnp.where(is_row, from_row[:, :64], from_col)
        part = jnp.dot(jnp.broadcast_to(w, (8, 64)), table, precision=HIGH, preferred_element_type=F32)
        for q in range(4):
            out[q, 2 * j : 2 * j + 1, :] = part[0:1, :128]
            out[q, 2 * j + 1 : 2 * j + 2, :] = part[0:1, 128:]
    for q in range(4):
        out[q, 6:8, :] = jnp.zeros((2, 128), F32)
        spread(out.at[q], 8, face_for(q, ups[...], downs[...]))


def chain_first(own, other, fac, core, near, ups, downs, out, mats, us, uc, ws, wc, rhs):
    odd = lax.axis_index("slab") % 2
    lane = lane_of((1, 128))
    for m in range(32):
        for j, src in ((0, own), (1, other)):
            at = 2 * m + (odd if j == 0 else 1 - odd)
            rhs[pl.ds(at, 1), :] = jnp.where(lane < 64, src[m, 32:33, :], 0.0)
    chain(own, other, rhs, fac, core, near, ups, downs, out, mats, us, uc, ws, wc)


def chain_second(own, other, got, fac, core, near, ups, downs, out, dots, mats, us, uc, ws, wc, rhs):
    total = got[pl.ds(0, 64, 4), :]
    for q in range(1, 4):
        total = total + got[pl.ds(q, 64, 4), :]
    rhs[...] = jnp.where(lane_of((64, 128)) < 64, total, 0.0)
    dots[...] = jnp.broadcast_to(jnp.sum(total, axis=0, keepdims=True), (8, 128))
    chain(own, other, rhs, fac, core, near, ups, downs, out, mats, us, uc, ws, wc)


def tables(got):
    quad = lax.axis_index("quad")
    total = got[0, 0:8, :] + got[1, 0:8, :] + got[2, 0:8, :] + got[3, 0:8, :]
    near = pltpu.roll(total, 1, 1)
    far = pltpu.roll(total, 65, 1)
    lane = lane_of((1, 128))
    valid = (lane >= 1) & (lane <= 64)

    def table(base, q):
        first = jnp.where(jnp.broadcast_to(q % 2, (1, 128)) == 1, far[base : base + 1, :], near[base : base + 1, :])
        second = jnp.where(
            jnp.broadcast_to(q % 2, (1, 128)) == 1, far[base + 1 : base + 2, :], near[base + 1 : base + 2, :]
        )
        picked = jnp.where(jnp.broadcast_to(q, (1, 128)) >= 2, second, first)
        return jnp.where(valid, picked, 0.0)

    return (
        table(0, quad),
        table(0, jnp.maximum(quad - 1, 0)),
        table(0, jnp.minimum(quad + 1, 3)),
        table(2, quad),
        table(4, quad),
    )


def apply(got, bj, core, near, sub, zsub, ysub, kz, kyl, kyh, kxl, kxh, diag):
    odd = parity()
    quad = lax.axis_index("quad")
    own, t_yl, t_yh, t_zl, t_zh = tables(got)
    planes = [bj[z] + look_up(own, sub[z] + 1) for z in range(4)]
    below = choose(odd, core[...], near[...]) + look_up(t_zl, zsub[0])
    above = choose(odd, near[...], core[...]) + look_up(t_zh, zsub[1])
    before = gather_rows(got[jnp.maximum(quad - 1, 0)], 8, 4)
    after = gather_rows(got[jnp.minimum(quad + 1, 3)], 8, 4)
    before = jnp.where(jnp.broadcast_to(quad, before.shape) > 0, before, 0.0) + look_up(t_yl, ysub[...])[0:4, :]
    after = jnp.where(jnp.broadcast_to(quad, after.shape) < 3, after, 0.0) + look_up(t_yh, ysub[...])[4:8, :]
    lower = [below] + planes[:3]
    upper = planes[1:] + [above]
    images = []
    for z in range(4):
        v = planes[z]
        images.append(
            diag[z] * v
            - kz[z] * lower[z]
            - kz[z + 1] * upper[z]
            - kyl[z] * y_before(v, before[z : z + 1, :])
            - kyh[z] * y_after(v, after[z : z + 1, :])
            - kxl[z] * x_before(v)
            - kxh[z] * x_after(v)
        )
    return planes, images


def total_of(lefts, rights):
    acc = lefts[0] * rights[0]
    for a, b in zip(lefts[1:], rights[1:]):
        acc = acc + a * b
    return jnp.sum(jnp.sum(acc, axis=0, keepdims=True), axis=1, keepdims=True)


def first(
    got, bj, core, near, sub, zsub, ysub, kz, kyl, kyh, kxl, kxh, diag, rs, inv, gam, cols,
    z_out, q_out, bj_out, to_core, to_near, ups, downs, pay, rows,
):
    planes, images = apply(got, bj, core, near, sub, zsub, ysub, kz, kyl, kyh, kxl, kxh, diag)
    for z in range(4):
        z_out[z] = planes[z]
        q_out[z] = images[z]
    rz = total_of([rs[z] for z in range(4)], planes)
    pq = total_of(planes, images)
    out = solve_lines([kz[z] for z in range(4)], [inv[z] for z in range(4)], [gam[z] for z in range(3)], images)
    for z in range(4):
        bj_out[z] = out[z]
    send_faces(out, to_core, to_near, ups, downs)
    cin = jnp.broadcast_to(restrict(sub, q_out, rows), (8, 64))
    lane = lane_of((1, 128))
    parts = []
    for q in range(4):
        part = lax.dot_general(
            cin, cols[q, 0:64, :64], (((1,), (1,)), ((), ())), precision=HIGH, preferred_element_type=F32
        )[0:1, :]
        part = jnp.concatenate([part, part], axis=1)
        parts.append(jnp.where(lane < 64, part, jnp.where(lane == 64, rz, jnp.where(lane == 65, pq, 0.0))))
    tile = jnp.concatenate(parts + parts, axis=0)
    for j in range(32):
        pay[j * 8 : (j + 1) * 8, :] = tile


def second(
    got, bj, core, near, sub, zsub, ysub, kz, kyl, kyh, kxl, kxh, diag, rs, z0, q0, dots,
    z_out, g_out, r_out, pay,
):
    planes, images = apply(got, bj, core, near, sub, zsub, ysub, kz, kyl, kyh, kxl, kxh, diag)
    alpha = dots[0:1, 64:65] / dots[0:1, 65:66]
    zs, gs, rr = [], [], []
    for z in range(4):
        rr.append(rs[z] - alpha * q0[z])
        zs.append(z0[z] - alpha * planes[z])
        gs.append(q0[z] - alpha * images[z])
        z_out[z] = zs[z]
        g_out[z] = gs[z]
        r_out[z] = rr[z]
    new = total_of(rr, zs)
    own = total_of(zs, gs)
    cross = total_of([z0[z] for z in range(4)], gs)
    lane = lane_of((8, 128))
    tile = jnp.where(lane == 0, new, jnp.where(lane == 1, own, jnp.where(lane == 2, cross, 0.0)))
    for j in range(32):
        pay[j * 8 : (j + 1) * 8, :] = tile


def last(got, dots, z0, q0, z1, g1, r1, x_out, r_out):
    total = jnp.sum(got[...], axis=0, keepdims=True)
    new, own, cross = total[:, 0:1], total[:, 1:2], total[:, 2:3]
    rz, pq = dots[0:1, 64:65], dots[0:1, 65:66]
    alpha = rz / pq
    beta = new / rz
    step = new / (own + 2.0 * beta * cross + beta * beta * pq)
    for z in range(4):
        x_out[z] = alpha * z0[z] + step * (z1[z] + beta * z0[z])
        r_out[z] = r1[z] - step * (g1[z] + beta * q0[z])


def body(right_side, phase_label, density_gain, subdomain, block_factor, coupling):
    slabs = lax.axis_size("slab")
    fac, cou = block_factor[0], coupling[0]
    grid, plane, edge = sds(4, 16, 1024), sds(16, 1024), sds(4, 1024)
    cores = [[i for i in range(slabs) if i % 2 == c] for c in range(2)]
    with_core = [(i, i ^ 1) for i in range(slabs)]
    with_near = [(i, i + 1 if i % 2 else i - 1) for i in range(1, slabs - 1)]

    def exchange(value, axis, groups=None):
        return lax.all_to_all(value, axis, 0, 0, tiled=True, axis_index_groups=groups)

    def swap(to_core, to_near):
        return lax.ppermute(to_core, "slab", with_core), lax.ppermute(to_near, "slab", with_near)

    mob, core, near, pay = call(
        begin, (grid, sds(384, 128), sds(384, 128), sds(4, 128, 128)), [pltpu.VMEM((64, 128), F32)]
    )(right_side, phase_label, density_gain, subdomain, fac)
    core, near = swap(core, near)
    got = exchange(pay, "quad")
    kz, kyl, kyh, kxl, kxh, diag, inv, gam, bj, to_core, to_near, ups, downs, zsub, ysub, pay = call(
        setup,
        (sds(5, 16, 1024), grid, grid, grid, grid, grid, grid, sds(3, 16, 1024), grid, plane, plane, edge, edge)
        + (jax.ShapeDtypeStruct((2, 16, 1024), jnp.int32), jax.ShapeDtypeStruct((8, 1024), jnp.int32), sds(32, 40, 128)),
    )(right_side, mob, core, near, fac, cou, got)
    bj_core, bj_near = swap(to_core, to_near)
    own = exchange(pay, "slab", cores)
    other = lax.ppermute(own, "slab", with_core)
    work = [
        pltpu.VMEM((64, 64, 128), F32),
        pltpu.VMEM((64, 128), F32),
        pltpu.VMEM((64, 64, 128), F32),
        pltpu.VMEM((64, 128), F32),
        pltpu.VMEM((66, 64, 128), F32),
        pltpu.VMEM((64, 128), F32),
    ]
    part = call(chain_first, sds(4, 40, 128), work)(own, other, fac, core, near, ups, downs)
    coarse = exchange(part, "quad")
    stencil = (subdomain, zsub, ysub, kz, kyl, kyh, kxl, kxh, diag, right_side)
    z0, q0, bj1, to_core, to_near, ups, downs, pay = call(
        first, (grid, grid, grid, plane, plane, edge, edge, sds(256, 128)), [pltpu.VMEM((64, 128), F32)]
    )(coarse, bj, bj_core, bj_near, *stencil, inv, gam, got)
    bj_core, bj_near = swap(to_core, to_near)
    everyone = exchange(pay.reshape(256, 1, 128), BOTH).reshape(256, 128)
    part, dots = call(chain_second, (sds(4, 40, 128), sds(8, 128)), work)(
        own, other, everyone, fac, core, near, ups, downs
    )
    coarse = exchange(part, "quad")
    z1, g1, r1, pay = call(second, (grid, grid, grid, sds(256, 128)))(
        coarse, bj1, bj_core, bj_near, *stencil, z0, q0, dots
    )
    everyone = exchange(pay.reshape(256, 1, 128), BOTH).reshape(256, 128)
    return tuple(call(last, (grid, grid))(everyone, dots, z0, q0, z1, g1, r1))


def solution(mesh):
    spec = P("slab", "quad", None)
    return jax.shard_map(body, mesh=mesh, in_specs=(spec,) * 6, out_specs=(spec, spec), check_vma=False)
```

```python
import jax
import jax.numpy as jnp
from jax import lax
from jax.experimental import pallas as pl
from jax.experimental.pallas import tpu as pltpu
from jax.sharding import PartitionSpec as P

F32 = jnp.float32
HIGH = lax.Precision.HIGHEST
BOTH = ("slab", "quad")


def sds(*shape):
    return jax.ShapeDtypeStruct(shape, F32)


def call(kernel, outs, scratch=(), far=(), spread_out=()):
    single = not isinstance(outs, tuple)
    shapes = (outs,) if single else outs
    whole = [-1 - i for i in spread_out if i < 0]
    copied = [i for i in spread_out if i >= 0]
    vmem, hbm = pl.BlockSpec(memory_space=pltpu.VMEM), pl.BlockSpec(memory_space=pltpu.HBM)

    def run(*args):
        count = len(args)
        extra = [pltpu.VMEM(args[i].shape, args[i].dtype) for i in far]
        extra += [pltpu.VMEM(shapes[i].shape, F32) for i in whole]
        extra += [pltpu.VMEM(shapes[i].shape[1:], F32) for i in copied]
        copies = len(far) + len(whole) + sum(shapes[i].shape[0] for i in copied)
        if copies:
            extra.append(pltpu.SemaphoreType.DMA((copies,)))

        def wrapped(*refs):
            ins, made = list(refs[:count]), list(refs[count : count + len(shapes)])
            rest = list(refs[count + len(shapes) : count + len(shapes) + len(scratch)])
            more = list(refs[count + len(shapes) + len(scratch) :])
            sems = more.pop() if copies else None
            coming = {}
            for n, i in enumerate(far):
                coming[i] = pltpu.make_async_copy(ins[i], more[n], sems.at[n])
                coming[i].start()
                ins[i] = more[n]
            targets = {}
            for n, i in enumerate(whole + copied):
                targets[i] = made[i]
                made[i] = more[len(far) + n]
            waited = set()

            def ready(*which):
                for i in which:
                    if i in coming and i not in waited:
                        waited.add(i)
                        coming[i].wait()

            kernel(ready, *ins, *made, *rest)
            ready(*far)
            at = len(far)
            going = []
            for i in whole:
                going.append(pltpu.make_async_copy(made[i], targets[i], sems.at[at]))
                at += 1
            for i in copied:
                for m in range(shapes[i].shape[0]):
                    going.append(pltpu.make_async_copy(made[i], targets[i].at[m], sems.at[at]))
                    at += 1
            for copy in going:
                copy.start()
            for copy in going:
                copy.wait()

        out = pl.pallas_call(
            wrapped,
            in_specs=[hbm if i in far else vmem for i in range(count)],
            out_specs=tuple(hbm if i in whole + copied else vmem for i in range(len(shapes))),
            out_shape=tuple(pltpu.HBM(s.shape, s.dtype) if i in whole + copied else s for i, s in enumerate(shapes)),
            scratch_shapes=list(scratch) + extra,
            compiler_params=pltpu.CompilerParams(vmem_limit_bytes=16 << 20),
            name=kernel.__name__,
        )(*[pltpu.with_memory_space_constraint(a, pltpu.HBM) if i in far else a for i, a in enumerate(args)])
        return out[0] if single else out

    return run


def harmonic(here, there):
    return jnp.where(there > 0, 2.0 * here * there / (here + there), here)


def x_before(plane):
    lane = lax.broadcasted_iota(jnp.int32, plane.shape, 1)
    return jnp.where(lane == 0, 0.0, pltpu.roll(plane, 1, 1))


def x_after(plane):
    width = plane.shape[1]
    lane = lax.broadcasted_iota(jnp.int32, plane.shape, 1)
    return jnp.where(lane == width - 1, 0.0, pltpu.roll(plane, width - 1, 1))


def y_before(plane, halo):
    row = lax.broadcasted_iota(jnp.int32, plane.shape, 0)
    return jnp.where(row == 0, halo, pltpu.roll(plane, 1, 0))


def y_after(plane, halo):
    height = plane.shape[0]
    row = lax.broadcasted_iota(jnp.int32, plane.shape, 0)
    return jnp.where(row == height - 1, halo, pltpu.roll(plane, height - 1, 0))


def lane_of(shape):
    return lax.broadcasted_iota(jnp.int32, shape, len(shape) - 1)


def restrict(sub_ref, field_ref, rows_ref):
    def group(g, unused):
        def tile(t, totals):
            rows = pl.ds(pl.multiple_of((t % 2) * 8, 8), 8)
            sub = sub_ref[t // 2, rows, :]
            field = field_ref[t // 2, rows, :]
            out = []
            for label in range(8):
                picked = jnp.where(sub == g * 8 + label, field, 0.0)
                total = totals[label]
                for j in range(8):
                    total = total + picked[:, j * 128 : (j + 1) * 128]
                out.append(total)
            return tuple(out)

        totals = lax.fori_loop(0, 8, tile, tuple(jnp.zeros((8, 128), F32) for _ in range(8)))
        stacked = jnp.concatenate([jnp.sum(t, axis=0, keepdims=True) for t in totals], axis=0)
        rows_ref[pl.ds(pl.multiple_of(g * 8, 8), 8), :] = stacked
        return unused

    lax.fori_loop(0, 8, group, 0)
    return jnp.sum(rows_ref[...].T, axis=0, keepdims=True)


def look_up(table, index):
    wide = jnp.broadcast_to(table, (8, 128))
    rows = []
    for r in range(index.shape[0] // 8):
        parts = []
        for c in range(index.shape[1] // 128):
            part = index[r * 8 : (r + 1) * 8, c * 128 : (c + 1) * 128]
            parts.append(jnp.take_along_axis(wide, part, axis=1, mode="promise_in_bounds"))
        rows.append(jnp.concatenate(parts, axis=1))
    return jnp.concatenate(rows, axis=0)


def solve_lines(kz, inv, rhs):
    rho = [rhs[0] * inv[0]]
    for j in range(1, 4):
        rho.append((rhs[j] + kz[j] * rho[j - 1]) * inv[j])
    out = [None] * 4
    out[3] = rho[3]
    for j in (2, 1, 0):
        out[j] = rho[j] + kz[j + 1] * inv[j] * out[j + 1]
    return out


def parity():
    return lax.axis_index("slab") % 2


def choose(flag, a, b):
    return jnp.where(jnp.broadcast_to(flag, a.shape) == 1, a, b)


def spread(out, at, plane):
    h = plane.shape[0]
    for c in range(8):
        out[at + c * h : at + (c + 1) * h, :] = plane[:, c * 128 : (c + 1) * 128]


def gather_rows(block, at, h):
    return jnp.concatenate([block[at + c * h : at + (c + 1) * h, :] for c in range(8)], axis=1)


def face_for(dest, upward, downward):
    return choose((lax.axis_index("quad") + 1 == dest).astype(jnp.int32), upward, downward)


def begin(ready, rs, ph, gain, sub, fac, mob, core, near, pay, rows):
    odd = parity()
    ready(0, 3)
    cin = restrict(sub, rs, rows)
    ready(1, 2, 4)
    ms, ss = [], []
    for z in range(4):
        m = 1.0 / (gain[z] * (0.001 + 0.999 * ph[z].astype(F32)))
        mob[z] = m
        ms.append(m)
        ss.append((sub[z] + 1).astype(F32))
    spread(core, 0, choose(odd, ms[0], ms[3]))
    spread(core, 128, choose(odd, ss[0], ss[3]))
    spread(near, 0, choose(odd, ms[3], ms[0]))
    spread(near, 128, choose(odd, ss[3], ss[0]))
    for part in (core, near):
        part[256:320, :] = fac[:, :128]
        part[320:384, :] = fac[:, 128:]
    upward = jnp.concatenate([m[15:16, :] for m in ms] + [s[15:16, :] for s in ss], axis=0)
    downward = jnp.concatenate([m[0:1, :] for m in ms] + [s[0:1, :] for s in ss], axis=0)
    both = jnp.concatenate([cin, cin], axis=1)
    lane = lane_of((64, 128))
    row = lax.broadcasted_iota(jnp.int32, (64, 128), 0)
    tail = jnp.where(row == 0, both, 0.0)
    for q in range(4):
        block = fac[:, (q // 2) * 128 : (q // 2 + 1) * 128]
        if q % 2:
            block = pltpu.roll(block, 64, 1)
        pay[q, 0:64, :] = jnp.where(lane < 64, block, tail)
        spread(pay.at[q], 64, face_for(q, upward, downward))


def send_faces(out, to_core, to_near, ups, downs):
    odd = parity()
    to_core[...] = choose(odd, out[0], out[3])
    to_near[...] = choose(odd, out[3], out[0])
    for z in range(4):
        ups[z : z + 1, :] = out[z][15:16, :]
        downs[z : z + 1, :] = out[z][0:1, :]


def setup(
    ready, rs, mob, core, near, fac, cou, got, kz, ky, kyt, kx, kxe, inv, bj, to_core, to_near, ups, downs, zsub, ysub, cols, beside, pay
):
    odd = parity()
    quad = lax.axis_index("quad")
    planes = [mob[z] for z in range(4)]
    c_mob, n_mob = gather_rows(core, 0, 16), gather_rows(near, 0, 16)
    c_sub, n_sub = gather_rows(core, 128, 16), gather_rows(near, 128, 16)
    below = [choose(odd, c_mob, n_mob)] + planes[:3]
    above = planes[1:] + [choose(odd, n_mob, c_mob)]
    zsub[0] = choose(odd, c_sub, n_sub).astype(jnp.int32)
    zsub[1] = choose(odd, n_sub, c_sub).astype(jnp.int32)
    before = gather_rows(got[jnp.maximum(quad - 1, 0)], 64, 8)
    after = gather_rows(got[jnp.minimum(quad + 1, 3)], 64, 8)
    ylo = jnp.where(jnp.broadcast_to(quad, before.shape) > 0, before, 0.0)
    yhi = jnp.where(jnp.broadcast_to(quad, after.shape) < 3, after, 0.0)
    ysub[...] = jnp.concatenate([ylo[4:8, :], yhi[4:8, :]], axis=0).astype(jnp.int32)
    faces = [harmonic(planes[z], below[z]) for z in range(4)]
    faces.append(harmonic(planes[3], above[3]))
    for z in range(5):
        kz[z] = faces[z]
    diags = []
    for z in range(4):
        m = planes[z]
        a = harmonic(m, y_before(m, ylo[z : z + 1, :]))
        b = harmonic(m, y_after(m, yhi[z : z + 1, :]))
        c = harmonic(m, x_before(m))
        d = harmonic(m, x_after(m))
        ky[z] = a
        kyt[z : z + 1, :] = b[15:16, :]
        kx[z] = c
        kxe[z] = jnp.where(lane_of((16, 128)) == 127, d[:, 896:], 0.0)
        diags.append(faces[z] + faces[z + 1] + a + b + c + d)
    invs = [1.0 / diags[0]]
    gams = [-faces[1] * invs[0]]
    for j in range(1, 4):
        invs.append(1.0 / (diags[j] + faces[j] * gams[j - 1]))
        gams.append(-faces[j + 1] * invs[j])
    for j in range(4):
        inv[j] = invs[j]
    ready(0)
    out = solve_lines(faces, invs, [rs[z] for z in range(4)])
    for z in range(4):
        bj[z] = out[z]
    send_faces(out, to_core, to_near, ups, downs)
    for q in range(4):
        cols[q] = got[q, 0:64, :]
    c_fac = jnp.concatenate([core[256:320, :], core[320:384, :]], axis=1)
    n_fac = jnp.concatenate([near[256:320, :], near[320:384, :]], axis=1)
    beside[0] = choose(odd, c_fac, n_fac)
    beside[1] = choose(odd, n_fac, c_fac)
    ready(4, 5)
    cins = [pltpu.roll(got[q][0:8, :], 64, 1)[0:1, :64] for q in range(4)]
    cin = jnp.concatenate(cins, axis=1)
    rhs = lax.dot_general(
        jnp.broadcast_to(cin, (8, 256)), fac[...], (((1,), (1,)), ((), ())), precision=HIGH, preferred_element_type=F32
    )
    flag = jnp.broadcast_to(odd, (64, 64)) == 1
    mat = jnp.where(flag, cou[...], cou[...].T)
    packed = jnp.concatenate([mat[:32, :], mat[32:, :]], axis=1)
    tail = jnp.concatenate([rhs, rhs], axis=1)
    pay[0:32, :] = packed
    pay[32:40, :] = tail


def chain(ready, own, other, rhs_ref, fac, beside, ups, downs, out, mats, us, uc, ws, wc):
    odd = lax.axis_index("slab") % 2
    lane = lane_of((32, 128))
    low = lane < 64
    ready(0, 1)
    for m in range(32):
        for j, src in ((0, own), (1, other)):
            packed = src[m, 0:32, :]
            at = 2 * m + (odd if j == 0 else 1 - odd)
            mats[at, 0:32, :] = jnp.where(low, packed, 0.0)
            mats[at, 32:64, :] = jnp.where(low, pltpu.roll(packed, 64, 1), 0.0)
    cols = rhs_ref[...].T
    for k in range(1, 64, 2):
        uc[k] = jnp.broadcast_to(cols[:64, k : k + 1], (64, 128))
    row = rhs_ref[0:1, :]
    us[0:1, :] = row
    col = None
    for k in range(1, 64):
        if k % 2:
            col = jnp.broadcast_to(jnp.sum(mats[k] * row, axis=1, keepdims=True), (64, 128)) + uc[k]
            uc[k] = col
        else:
            row = jnp.sum(mats[k] * col, axis=0, keepdims=True) + rhs_ref[k : k + 1, :]
            us[k : k + 1, :] = row
    ws[0:8, :] = jnp.zeros((8, 128), F32)
    wc[0] = jnp.zeros((64, 128), F32)
    wc[65] = jnp.zeros((64, 128), F32)
    wc[64] = col
    for k in range(63, 0, -1):
        if k % 2:
            row = jnp.sum(mats[k] * col, axis=0, keepdims=True) + us[k - 1 : k, :]
            ws[k : k + 1, :] = row
        else:
            col = jnp.broadcast_to(jnp.sum(mats[k] * row, axis=1, keepdims=True), (64, 128)) + uc[k - 1]
            wc[k] = col
    slab = lax.axis_index("slab")
    ready(2, 3)
    shares = ((0, fac[...]), (-1, beside[0]), (1, beside[1]))
    for j, (shift, table) in enumerate(shares):
        at = slab + shift + 1
        from_row = ws[pl.ds(jnp.minimum(at, 63), 1), :]
        from_col = wc[at].T[0:1, :]
        is_row = jnp.broadcast_to(at % 2, (1, 64)) == 1
        w = jnp.where(is_row, from_row[:, :64], from_col)
        part = jnp.dot(jnp.broadcast_to(w, (8, 64)), table, precision=HIGH, preferred_element_type=F32)
        for q in range(4):
            out[q, 2 * j : 2 * j + 1, :] = part[0:1, :128]
            out[q, 2 * j + 1 : 2 * j + 2, :] = part[0:1, 128:]
    for q in range(4):
        out[q, 6:8, :] = jnp.zeros((2, 128), F32)
        spread(out.at[q], 8, face_for(q, ups[...], downs[...]))


def chain_first(ready, own, other, fac, beside, ups, downs, out, mats, us, uc, ws, wc, rhs):
    odd = lax.axis_index("slab") % 2
    lane = lane_of((1, 128))
    for m in range(32):
        for j, src in ((0, own), (1, other)):
            at = 2 * m + (odd if j == 0 else 1 - odd)
            rhs[pl.ds(at, 1), :] = jnp.where(lane < 64, src[m, 32:33, :], 0.0)
    chain(ready, own, other, rhs, fac, beside, ups, downs, out, mats, us, uc, ws, wc)


def chain_second(ready, own, other, got, fac, beside, ups, downs, out, dots, mats, us, uc, ws, wc, rhs):
    total = got[pl.ds(0, 64, 4), :]
    for q in range(1, 4):
        total = total + got[pl.ds(q, 64, 4), :]
    rhs[...] = jnp.where(lane_of((64, 128)) < 64, total, 0.0)
    dots[...] = jnp.broadcast_to(jnp.sum(total, axis=0, keepdims=True), (8, 128))
    chain(ready, own, other, rhs, fac, beside, ups, downs, out, mats, us, uc, ws, wc)


def tables(got):
    quad = lax.axis_index("quad")
    total = got[0, 0:8, :] + got[1, 0:8, :] + got[2, 0:8, :] + got[3, 0:8, :]
    near = pltpu.roll(total, 1, 1)
    far = pltpu.roll(total, 65, 1)
    lane = lane_of((1, 128))
    valid = (lane >= 1) & (lane <= 64)

    def table(base, q):
        first = jnp.where(jnp.broadcast_to(q % 2, (1, 128)) == 1, far[base : base + 1, :], near[base : base + 1, :])
        second = jnp.where(
            jnp.broadcast_to(q % 2, (1, 128)) == 1, far[base + 1 : base + 2, :], near[base + 1 : base + 2, :]
        )
        picked = jnp.where(jnp.broadcast_to(q, (1, 128)) >= 2, second, first)
        return jnp.where(valid, picked, 0.0)

    return (
        table(0, quad),
        table(0, jnp.maximum(quad - 1, 0)),
        table(0, jnp.minimum(quad + 1, 3)),
        table(2, quad),
        table(4, quad),
    )


def apply(got, bj, core, near, sub, zsub, ysub, kz, ky, kyt, kx, kxe):
    odd = parity()
    quad = lax.axis_index("quad")
    own, t_yl, t_yh, t_zl, t_zh = tables(got)
    planes = [bj[z] + look_up(own, sub[z] + 1) for z in range(4)]
    below = choose(odd, core[...], near[...]) + look_up(t_zl, zsub[0])
    above = choose(odd, near[...], core[...]) + look_up(t_zh, zsub[1])
    before = gather_rows(got[jnp.maximum(quad - 1, 0)], 8, 4)
    after = gather_rows(got[jnp.minimum(quad + 1, 3)], 8, 4)
    before = jnp.where(jnp.broadcast_to(quad, before.shape) > 0, before, 0.0) + look_up(t_yl, ysub[...])[0:4, :]
    after = jnp.where(jnp.broadcast_to(quad, after.shape) < 3, after, 0.0) + look_up(t_yh, ysub[...])[4:8, :]
    line = [below] + planes + [above]
    rise = [kz[j] * (line[j + 1] - line[j]) for j in range(5)]
    images = []
    for z in range(4):
        v = planes[z]
        y_low = ky[z] * (v - y_before(v, before[z : z + 1, :]))
        y_high = y_after(y_low, kyt[z : z + 1, :] * (after[z : z + 1, :] - v[15:16, :]))
        x_low = kx[z] * (v - x_before(v))
        x_high = x_after(x_low)
        x_high = jnp.concatenate([x_high[:, :896], x_high[:, 896:] - kxe[z] * v[:, 896:]], axis=1)
        images.append((rise[z] - rise[z + 1]) + (y_low - y_high) + (x_low - x_high))
    return planes, images


def total_of(lefts, rights):
    acc = lefts[0] * rights[0]
    for a, b in zip(lefts[1:], rights[1:]):
        acc = acc + a * b
    return jnp.sum(jnp.sum(acc, axis=0, keepdims=True), axis=1, keepdims=True)


def first(
    ready, got, bj, core, near, sub, zsub, ysub, kz, ky, kyt, kx, kxe, rs, inv, cols,
    z_out, q_out, bj_out, to_core, to_near, ups, downs, pay, rows,
):
    ready(4, 12)
    planes, images = apply(got, bj, core, near, sub, zsub, ysub, kz, ky, kyt, kx, kxe)
    for z in range(4):
        z_out[z] = planes[z]
        q_out[z] = images[z]
    rz = total_of([rs[z] for z in range(4)], planes)
    pq = total_of(planes, images)
    out = solve_lines([kz[z] for z in range(5)], [inv[z] for z in range(4)], images)
    for z in range(4):
        bj_out[z] = out[z]
    send_faces(out, to_core, to_near, ups, downs)
    cin = jnp.broadcast_to(restrict(sub, q_out, rows), (8, 64))
    lane = lane_of((1, 128))
    parts = []
    for q in range(4):
        part = lax.dot_general(
            cin, cols[q, 0:64, :64], (((1,), (1,)), ((), ())), precision=HIGH, preferred_element_type=F32
        )[0:1, :]
        part = jnp.concatenate([part, part], axis=1)
        parts.append(jnp.where(lane < 64, part, jnp.where(lane == 64, rz, jnp.where(lane == 65, pq, 0.0))))
    pay[...] = jnp.concatenate(parts + parts, axis=0)


def second(
    ready, got, bj, core, near, sub, zsub, ysub, kz, ky, kyt, kx, kxe, rs, z0, q0, dots,
    z_out, g_out, r_out, pay,
):
    ready(4, 12)
    planes, images = apply(got, bj, core, near, sub, zsub, ysub, kz, ky, kyt, kx, kxe)
    alpha = dots[0:1, 64:65] / dots[0:1, 65:66]
    zs, gs, rr = [], [], []
    for z in range(4):
        rr.append(rs[z] - alpha * q0[z])
        zs.append(z0[z] - alpha * planes[z])
        gs.append(q0[z] - alpha * images[z])
        z_out[z] = zs[z]
        g_out[z] = gs[z]
        r_out[z] = rr[z]
    new = total_of(rr, zs)
    own = total_of(zs, gs)
    cross = total_of([z0[z] for z in range(4)], gs)
    lane = lane_of((8, 128))
    pay[...] = jnp.where(lane == 0, new, jnp.where(lane == 1, own, jnp.where(lane == 2, cross, 0.0)))


def last(ready, got, dots, z0, q0, z1, g1, r1, x_out, r_out):
    total = jnp.sum(got[...], axis=0, keepdims=True)
    new, own, cross = total[:, 0:1], total[:, 1:2], total[:, 2:3]
    rz, pq = dots[0:1, 64:65], dots[0:1, 65:66]
    alpha = rz / pq
    beta = new / rz
    step = new / (own + 2.0 * beta * cross + beta * beta * pq)
    for z in range(4):
        x_out[z] = alpha * z0[z] + step * (z1[z] + beta * z0[z])
        r_out[z] = r1[z] - step * (g1[z] + beta * q0[z])


def body(right_side, phase_label, density_gain, subdomain, block_factor, coupling):
    slabs = lax.axis_size("slab")
    fac, cou = block_factor[0], coupling[0]
    grid, plane, edge = sds(4, 16, 1024), sds(16, 1024), sds(4, 1024)
    cores = [[i for i in range(slabs) if i % 2 == c] for c in range(2)]
    with_core = [(i, i ^ 1) for i in range(slabs)]
    with_near = [(i, i + 1 if i % 2 else i - 1) for i in range(1, slabs - 1)]

    def exchange(value, axis, groups=None):
        return lax.all_to_all(value, axis, 0, 0, tiled=True, axis_index_groups=groups)

    def swap(to_core, to_near):
        return lax.ppermute(to_core, "slab", with_core), lax.ppermute(to_near, "slab", with_near)

    mob, core, near, pay = call(
        begin,
        (grid, sds(384, 128), sds(384, 128), sds(4, 128, 128)),
        [pltpu.VMEM((64, 128), F32)],
        (0, 1, 2, 3, 4),
        (-4,),
    )(right_side, phase_label, density_gain, subdomain, fac)
    core, near = swap(core, near)
    got = exchange(pay, "quad")
    kz, ky, kyt, kx, kxe, inv, bj, to_core, to_near, ups, downs, zsub, ysub, cols, beside, pay = call(
        setup,
        (sds(5, 16, 1024), grid, edge, grid, sds(4, 16, 128), grid, grid, plane, plane, edge, edge)
        + (jax.ShapeDtypeStruct((2, 16, 1024), jnp.int32), jax.ShapeDtypeStruct((8, 1024), jnp.int32))
        + (sds(4, 64, 128), sds(2, 64, 256), sds(32, 40, 128)),
        (),
        (0, 4, 5),
        (15,),
    )(right_side, mob, core, near, fac, cou, got)
    bj_core, bj_near = swap(to_core, to_near)
    own = exchange(pay, "slab", cores)
    other = lax.ppermute(own, "slab", with_core)
    work = [
        pltpu.VMEM((64, 64, 128), F32),
        pltpu.VMEM((64, 128), F32),
        pltpu.VMEM((64, 64, 128), F32),
        pltpu.VMEM((64, 128), F32),
        pltpu.VMEM((66, 64, 128), F32),
        pltpu.VMEM((64, 128), F32),
    ]
    part = call(chain_first, sds(4, 40, 128), work, (2,), (-1,))(own, other, fac, beside, ups, downs)
    coarse = exchange(part, "quad")
    stencil = (subdomain, zsub, ysub, kz, ky, kyt, kx, kxe, right_side)
    z0, q0, bj1, to_core, to_near, ups, downs, pay = call(
        first,
        (grid, grid, grid, plane, plane, edge, edge, sds(32, 8, 128)),
        [pltpu.VMEM((64, 128), F32)],
        (4, 12),
        (7,),
    )(coarse, bj, bj_core, bj_near, *stencil, inv, cols)
    bj_core, bj_near = swap(to_core, to_near)
    everyone = exchange(pay.reshape(256, 1, 128), BOTH).reshape(256, 128)
    part, dots = call(chain_second, (sds(4, 40, 128), sds(8, 128)), work, (0, 1, 3), (-1,))(
        own, other, everyone, fac, beside, ups, downs
    )
    coarse = exchange(part, "quad")
    z1, g1, r1, pay = call(second, (grid, grid, grid, sds(32, 8, 128)), (), (4, 12), (3,))(
        coarse, bj1, bj_core, bj_near, *stencil, z0, q0, dots
    )
    everyone = exchange(pay.reshape(256, 1, 128), BOTH).reshape(256, 128)
    return tuple(call(last, (grid, grid))(everyone, dots, z0, q0, z1, g1, r1))


def solution(mesh):
    spec = P("slab", "quad", None)
    return jax.shard_map(body, mesh=mesh, in_specs=(spec,) * 6, out_specs=(spec, spec), check_vma=False)
```

```python
import jax
import jax.numpy as jnp
from jax import lax
from jax.experimental import pallas as pl
from jax.experimental.pallas import tpu as pltpu
from jax.sharding import PartitionSpec as P

F32 = jnp.float32
HIGH = lax.Precision.HIGHEST
BOTH = ("slab", "quad")
PIECES = 4


def sds(*shape):
    return jax.ShapeDtypeStruct(shape, F32)


def call(kernel, outs, scratch=(), far=(), spread_out=()):
    single = not isinstance(outs, tuple)
    shapes = (outs,) if single else outs
    whole = [-1 - i for i in spread_out if i < 0]
    copied = [i for i in spread_out if i >= 0]
    vmem, hbm = pl.BlockSpec(memory_space=pltpu.VMEM), pl.BlockSpec(memory_space=pltpu.HBM)

    def run(*args):
        count = len(args)
        extra = [pltpu.VMEM(args[i].shape, args[i].dtype) for i in far]
        extra += [pltpu.VMEM(shapes[i].shape, F32) for i in whole]
        extra += [pltpu.VMEM(shapes[i].shape[1:], F32) for i in copied]
        pieces_of = {i: PIECES if len(args[i].shape) == 3 and args[i].shape[0] % 8 == 0 else 1 for i in far}
        copies = sum(pieces_of.values()) + len(whole) + sum(shapes[i].shape[0] for i in copied)
        if copies:
            extra.append(pltpu.SemaphoreType.DMA((copies,)))

        def wrapped(*refs):
            ins, made = list(refs[:count]), list(refs[count : count + len(shapes)])
            rest = list(refs[count + len(shapes) : count + len(shapes) + len(scratch)])
            more = list(refs[count + len(shapes) + len(scratch) :])
            sems = more.pop() if copies else None
            coming, at = {}, 0
            for n, i in enumerate(far):
                size = ins[i].shape[0] // pieces_of[i]
                coming[i] = []
                for p in range(pieces_of[i]):
                    src, dst = ins[i], more[n]
                    if pieces_of[i] > 1:
                        src, dst = src.at[pl.ds(p * size, size)], dst.at[pl.ds(p * size, size)]
                    coming[i].append(pltpu.make_async_copy(src, dst, sems.at[at]))
                    coming[i][p].start()
                    at += 1
                ins[i] = more[n]
            targets = {}
            for n, i in enumerate(whole + copied):
                targets[i] = made[i]
                made[i] = more[len(far) + n]
            waited = set()

            def ready(*which, pieces=range(PIECES)):
                for i in which:
                    for p in pieces:
                        if i in coming and p < pieces_of[i] and (i, p) not in waited:
                            waited.add((i, p))
                            coming[i][p].wait()

            kernel(ready, *ins, *made, *rest)
            ready(*far)
            at = sum(pieces_of.values())
            going = []
            for i in whole:
                going.append(pltpu.make_async_copy(made[i], targets[i], sems.at[at]))
                at += 1
            for i in copied:
                for m in range(shapes[i].shape[0]):
                    going.append(pltpu.make_async_copy(made[i], targets[i].at[m], sems.at[at]))
                    at += 1
            for copy in going:
                copy.start()
            for copy in going:
                copy.wait()

        out = pl.pallas_call(
            wrapped,
            in_specs=[hbm if i in far else vmem for i in range(count)],
            out_specs=tuple(hbm if i in whole + copied else vmem for i in range(len(shapes))),
            out_shape=tuple(pltpu.HBM(s.shape, s.dtype) if i in whole + copied else s for i, s in enumerate(shapes)),
            scratch_shapes=list(scratch) + extra,
            compiler_params=pltpu.CompilerParams(vmem_limit_bytes=16 << 20),
            name=kernel.__name__,
        )(*[pltpu.with_memory_space_constraint(a, pltpu.HBM) if i in far else a for i, a in enumerate(args)])
        return out[0] if single else out

    return run


def harmonic(here, there):
    return jnp.where(there > 0, 2.0 * here * there / (here + there), here)


def x_before(plane):
    lane = lax.broadcasted_iota(jnp.int32, plane.shape, 1)
    return jnp.where(lane == 0, 0.0, pltpu.roll(plane, 1, 1))


def x_after(plane):
    width = plane.shape[1]
    lane = lax.broadcasted_iota(jnp.int32, plane.shape, 1)
    return jnp.where(lane == width - 1, 0.0, pltpu.roll(plane, width - 1, 1))


def y_before(plane, halo):
    row = lax.broadcasted_iota(jnp.int32, plane.shape, 0)
    return jnp.where(row == 0, halo, pltpu.roll(plane, 1, 0))


def y_after(plane, halo):
    height = plane.shape[0]
    row = lax.broadcasted_iota(jnp.int32, plane.shape, 0)
    return jnp.where(row == height - 1, halo, pltpu.roll(plane, height - 1, 0))


def lane_of(shape):
    return lax.broadcasted_iota(jnp.int32, shape, len(shape) - 1)


def restrict(sub_ref, field_ref, rows_ref):
    def group(g, unused):
        def tile(t, totals):
            rows = pl.ds(pl.multiple_of((t % 2) * 8, 8), 8)
            sub = sub_ref[t // 2, rows, :]
            field = field_ref[t // 2, rows, :]
            out = []
            for label in range(8):
                picked = jnp.where(sub == g * 8 + label, field, 0.0)
                total = totals[label]
                for j in range(8):
                    total = total + picked[:, j * 128 : (j + 1) * 128]
                out.append(total)
            return tuple(out)

        totals = lax.fori_loop(0, 8, tile, tuple(jnp.zeros((8, 128), F32) for _ in range(8)))
        stacked = jnp.concatenate([jnp.sum(t, axis=0, keepdims=True) for t in totals], axis=0)
        rows_ref[pl.ds(pl.multiple_of(g * 8, 8), 8), :] = stacked
        return unused

    lax.fori_loop(0, 8, group, 0)
    return jnp.sum(rows_ref[...].T, axis=0, keepdims=True)


def look_up(table, index):
    wide = jnp.broadcast_to(table, (8, 128))
    rows = []
    for r in range(index.shape[0] // 8):
        parts = []
        for c in range(index.shape[1] // 128):
            part = index[r * 8 : (r + 1) * 8, c * 128 : (c + 1) * 128]
            parts.append(jnp.take_along_axis(wide, part, axis=1, mode="promise_in_bounds"))
        rows.append(jnp.concatenate(parts, axis=1))
    return jnp.concatenate(rows, axis=0)


def solve_lines(kz, inv, rhs):
    rho = [rhs[0] * inv[0]]
    for j in range(1, 4):
        rho.append((rhs[j] + kz[j] * rho[j - 1]) * inv[j])
    out = [None] * 4
    out[3] = rho[3]
    for j in (2, 1, 0):
        out[j] = rho[j] + kz[j + 1] * inv[j] * out[j + 1]
    return out


def parity():
    return lax.axis_index("slab") % 2


def choose(flag, a, b):
    return jnp.where(jnp.broadcast_to(flag, a.shape) == 1, a, b)


def spread(out, at, plane):
    h = plane.shape[0]
    for c in range(8):
        out[at + c * h : at + (c + 1) * h, :] = plane[:, c * 128 : (c + 1) * 128]


def gather_rows(block, at, h):
    return jnp.concatenate([block[at + c * h : at + (c + 1) * h, :] for c in range(8)], axis=1)


def face_for(dest, upward, downward):
    return choose((lax.axis_index("quad") + 1 == dest).astype(jnp.int32), upward, downward)


def begin(ready, rs, ph, gain, sub, fac, mob, core, near, pay, rows):
    odd = parity()
    ready(0, 3)
    cin = restrict(sub, rs, rows)
    ready(1, 2, 4)
    ms, ss = [], []
    for z in range(4):
        m = 1.0 / (gain[z] * (0.001 + 0.999 * ph[z].astype(F32)))
        mob[z] = m
        ms.append(m)
        ss.append((sub[z] + 1).astype(F32))
    spread(core, 0, choose(odd, ms[0], ms[3]))
    spread(core, 128, choose(odd, ss[0], ss[3]))
    spread(near, 0, choose(odd, ms[3], ms[0]))
    spread(near, 128, choose(odd, ss[3], ss[0]))
    for part in (core, near):
        part[256:320, :] = fac[:, :128]
        part[320:384, :] = fac[:, 128:]
    upward = jnp.concatenate([m[15:16, :] for m in ms] + [s[15:16, :] for s in ss], axis=0)
    downward = jnp.concatenate([m[0:1, :] for m in ms] + [s[0:1, :] for s in ss], axis=0)
    both = jnp.concatenate([cin, cin], axis=1)
    lane = lane_of((64, 128))
    row = lax.broadcasted_iota(jnp.int32, (64, 128), 0)
    tail = jnp.where(row == 0, both, 0.0)
    for q in range(4):
        block = fac[:, (q // 2) * 128 : (q // 2 + 1) * 128]
        if q % 2:
            block = pltpu.roll(block, 64, 1)
        pay[q, 0:64, :] = jnp.where(lane < 64, block, tail)
        spread(pay.at[q], 64, face_for(q, upward, downward))


def send_faces(out, to_core, to_near, ups, downs):
    odd = parity()
    to_core[...] = choose(odd, out[0], out[3])
    to_near[...] = choose(odd, out[3], out[0])
    for z in range(4):
        ups[z : z + 1, :] = out[z][15:16, :]
        downs[z : z + 1, :] = out[z][0:1, :]


def share(ready, got, fac, cou, cols, pay):
    for q in range(4):
        cols[q] = got[q, 0:64, :]
    cins = [pltpu.roll(got[q, 0:8, :], 64, 1)[0:1, :64] for q in range(4)]
    cin = jnp.concatenate(cins, axis=1)
    ready(1)
    rhs = lax.dot_general(
        jnp.broadcast_to(cin, (8, 256)), fac[...], (((1,), (1,)), ((), ())), precision=HIGH, preferred_element_type=F32
    )
    ready(2)
    mat = choose(parity(), cou[...], cou[...].T)
    pay[0:32, :] = jnp.concatenate([mat[:32, :], mat[32:, :]], axis=1)
    pay[32:40, :] = jnp.concatenate([rhs, rhs], axis=1)


def setup(
    ready, rs, mob, core, near, got, kz, ky, kyt, kx, kxe, inv, bj, to_core, to_near, ups, downs, zsub, ysub, beside
):
    odd = parity()
    quad = lax.axis_index("quad")
    planes = [mob[z] for z in range(4)]
    c_mob, n_mob = gather_rows(core, 0, 16), gather_rows(near, 0, 16)
    c_sub, n_sub = gather_rows(core, 128, 16), gather_rows(near, 128, 16)
    below = [choose(odd, c_mob, n_mob)] + planes[:3]
    above = planes[1:] + [choose(odd, n_mob, c_mob)]
    zsub[0] = choose(odd, c_sub, n_sub).astype(jnp.int32)
    zsub[1] = choose(odd, n_sub, c_sub).astype(jnp.int32)
    c_fac = jnp.concatenate([core[256:320, :], core[320:384, :]], axis=1)
    n_fac = jnp.concatenate([near[256:320, :], near[320:384, :]], axis=1)
    beside[0] = choose(odd, c_fac, n_fac)
    beside[1] = choose(odd, n_fac, c_fac)
    before = gather_rows(got[jnp.maximum(quad - 1, 0)], 64, 8)
    after = gather_rows(got[jnp.minimum(quad + 1, 3)], 64, 8)
    ylo = jnp.where(jnp.broadcast_to(quad, before.shape) > 0, before, 0.0)
    yhi = jnp.where(jnp.broadcast_to(quad, after.shape) < 3, after, 0.0)
    ysub[...] = jnp.concatenate([ylo[4:8, :], yhi[4:8, :]], axis=0).astype(jnp.int32)
    faces = [harmonic(planes[z], below[z]) for z in range(4)]
    faces.append(harmonic(planes[3], above[3]))
    for z in range(5):
        kz[z] = faces[z]
    diags = []
    for z in range(4):
        m = planes[z]
        a = harmonic(m, y_before(m, ylo[z : z + 1, :]))
        b = harmonic(m, y_after(m, yhi[z : z + 1, :]))
        c = harmonic(m, x_before(m))
        d = harmonic(m, x_after(m))
        ky[z] = a
        kyt[z : z + 1, :] = b[15:16, :]
        kx[z] = c
        kxe[z] = jnp.where(lane_of((16, 128)) == 127, d[:, 896:], 0.0)
        diags.append(faces[z] + faces[z + 1] + a + b + c + d)
    invs = [1.0 / diags[0]]
    for j in range(1, 4):
        invs.append(1.0 / (diags[j] - faces[j] * faces[j] * invs[j - 1]))
    for j in range(4):
        inv[j] = invs[j]
    ready(0)
    out = solve_lines(faces, invs, [rs[z] for z in range(4)])
    for z in range(4):
        bj[z] = out[z]
    send_faces(out, to_core, to_near, ups, downs)


def smooth(ready, field, kz, inv, bj, to_core, to_near, ups, downs):
    out = solve_lines([kz[z] for z in range(5)], [inv[z] for z in range(4)], [field[z] for z in range(4)])
    for z in range(4):
        bj[z] = out[z]
    send_faces(out, to_core, to_near, ups, downs)


def chain(ready, own, other, rhs_ref, fac, beside, ups, downs, out, mats, us, uc, ws, wc):
    odd = lax.axis_index("slab") % 2
    low = lane_of((32, 128)) < 64
    cols = rhs_ref[...].T
    for k in range(1, 64, 2):
        uc[k] = jnp.broadcast_to(cols[:64, k : k + 1], (64, 128))
    row = rhs_ref[0:1, :]
    us[0:1, :] = row
    col = None
    for k in range(1, 64):
        m = k // 2
        if m % 8 == 0:
            ready(0, 1, pieces=(m // 8,))
        packed = choose(odd, own[m, 0:32, :], other[m, 0:32, :])
        if k % 2 == 0:
            packed = choose(odd, other[m, 0:32, :], own[m, 0:32, :])
        mat = jnp.concatenate([jnp.where(low, packed, 0.0), jnp.where(low, pltpu.roll(packed, 64, 1), 0.0)], axis=0)
        mats[k] = mat
        if k % 2:
            col = jnp.broadcast_to(jnp.sum(mat * row, axis=1, keepdims=True), (64, 128)) + uc[k]
            uc[k] = col
        else:
            row = jnp.sum(mat * col, axis=0, keepdims=True) + rhs_ref[k : k + 1, :]
            us[k : k + 1, :] = row
    ws[0:8, :] = jnp.zeros((8, 128), F32)
    wc[0] = jnp.zeros((64, 128), F32)
    wc[65] = jnp.zeros((64, 128), F32)
    wc[64] = col
    for k in range(63, 0, -1):
        if k % 2:
            row = jnp.sum(mats[k] * col, axis=0, keepdims=True) + us[k - 1 : k, :]
            ws[k : k + 1, :] = row
        else:
            col = jnp.broadcast_to(jnp.sum(mats[k] * row, axis=1, keepdims=True), (64, 128)) + uc[k - 1]
            wc[k] = col
    slab = lax.axis_index("slab")
    ready(2, 3, 4, 5, 6)
    shares = ((0, fac[...]), (-1, beside[0]), (1, beside[1]))
    for j, (shift, table) in enumerate(shares):
        at = slab + shift + 1
        from_row = ws[pl.ds(jnp.minimum(at, 63), 1), :]
        from_col = wc[at].T[0:1, :]
        is_row = jnp.broadcast_to(at % 2, (1, 64)) == 1
        w = jnp.where(is_row, from_row[:, :64], from_col)
        part = jnp.dot(jnp.broadcast_to(w, (8, 64)), table, precision=HIGH, preferred_element_type=F32)
        for q in range(4):
            out[q, 2 * j : 2 * j + 1, :] = part[0:1, :128]
            out[q, 2 * j + 1 : 2 * j + 2, :] = part[0:1, 128:]
    for q in range(4):
        out[q, 6:8, :] = jnp.zeros((2, 128), F32)
        spread(out.at[q], 8, face_for(q, ups[...], downs[...]))


def chain_first(ready, own, other, fac, beside, ups, downs, out, mats, us, uc, ws, wc, rhs):
    odd = lax.axis_index("slab") % 2
    lane = lane_of((1, 128))
    for m in range(32):
        for j, src in ((0, own), (1, other)):
            at = 2 * m + (odd if j == 0 else 1 - odd)
            rhs[pl.ds(at, 1), :] = jnp.where(lane < 64, src[m, 32:33, :], 0.0)
    chain(ready, own, other, rhs, fac, beside, ups, downs, out, mats, us, uc, ws, wc)


def chain_second(ready, own, other, got, fac, beside, ups, downs, out, dots, mats, us, uc, ws, wc, rhs):
    total = got[pl.ds(0, 64, 4), :]
    for q in range(1, 4):
        total = total + got[pl.ds(q, 64, 4), :]
    rhs[...] = jnp.where(lane_of((64, 128)) < 64, total, 0.0)
    dots[...] = jnp.broadcast_to(jnp.sum(total, axis=0, keepdims=True), (8, 128))
    chain(ready, own, other, rhs, fac, beside, ups, downs, out, mats, us, uc, ws, wc)


def tables(got):
    quad = lax.axis_index("quad")
    total = got[0, 0:8, :] + got[1, 0:8, :] + got[2, 0:8, :] + got[3, 0:8, :]
    near = pltpu.roll(total, 1, 1)
    far = pltpu.roll(total, 65, 1)
    lane = lane_of((1, 128))
    valid = (lane >= 1) & (lane <= 64)

    def table(base, q):
        first = jnp.where(jnp.broadcast_to(q % 2, (1, 128)) == 1, far[base : base + 1, :], near[base : base + 1, :])
        second = jnp.where(
            jnp.broadcast_to(q % 2, (1, 128)) == 1, far[base + 1 : base + 2, :], near[base + 1 : base + 2, :]
        )
        picked = jnp.where(jnp.broadcast_to(q, (1, 128)) >= 2, second, first)
        return jnp.where(valid, picked, 0.0)

    return (
        table(0, quad),
        table(0, jnp.maximum(quad - 1, 0)),
        table(0, jnp.minimum(quad + 1, 3)),
        table(2, quad),
        table(4, quad),
    )


def apply(got, bj, core, near, sub, zsub, ysub, kz, ky, kyt, kx, kxe):
    odd = parity()
    quad = lax.axis_index("quad")
    own, t_yl, t_yh, t_zl, t_zh = tables(got)
    planes = [bj[z] + look_up(own, sub[z] + 1) for z in range(4)]
    below = choose(odd, core[...], near[...]) + look_up(t_zl, zsub[0])
    above = choose(odd, near[...], core[...]) + look_up(t_zh, zsub[1])
    before = gather_rows(got[jnp.maximum(quad - 1, 0)], 8, 4)
    after = gather_rows(got[jnp.minimum(quad + 1, 3)], 8, 4)
    before = jnp.where(jnp.broadcast_to(quad, before.shape) > 0, before, 0.0) + look_up(t_yl, ysub[...])[0:4, :]
    after = jnp.where(jnp.broadcast_to(quad, after.shape) < 3, after, 0.0) + look_up(t_yh, ysub[...])[4:8, :]
    line = [below] + planes + [above]
    rise = [kz[j] * (line[j + 1] - line[j]) for j in range(5)]
    images = []
    for z in range(4):
        v = planes[z]
        y_low = ky[z] * (v - y_before(v, before[z : z + 1, :]))
        y_high = y_after(y_low, kyt[z : z + 1, :] * (after[z : z + 1, :] - v[15:16, :]))
        x_low = kx[z] * (v - x_before(v))
        x_high = x_after(x_low)
        x_high = jnp.concatenate([x_high[:, :896], x_high[:, 896:] - kxe[z] * v[:, 896:]], axis=1)
        images.append((rise[z] - rise[z + 1]) + (y_low - y_high) + (x_low - x_high))
    return planes, images


def total_of(lefts, rights):
    acc = lefts[0] * rights[0]
    for a, b in zip(lefts[1:], rights[1:]):
        acc = acc + a * b
    return jnp.sum(jnp.sum(acc, axis=0, keepdims=True), axis=1, keepdims=True)


def first(
    ready, got, bj, core, near, sub, zsub, ysub, kz, ky, kyt, kx, kxe, rs, cols,
    z_out, q_out, pay, rows,
):
    ready(4)
    planes, images = apply(got, bj, core, near, sub, zsub, ysub, kz, ky, kyt, kx, kxe)
    for z in range(4):
        z_out[z] = planes[z]
        q_out[z] = images[z]
    cin = jnp.broadcast_to(restrict(sub, q_out, rows), (8, 64))
    ready(12)
    rz = total_of([rs[z] for z in range(4)], planes)
    pq = total_of(planes, images)
    lane = lane_of((1, 128))
    parts = []
    for q in range(4):
        part = lax.dot_general(
            cin, cols[q, 0:64, :64], (((1,), (1,)), ((), ())), precision=HIGH, preferred_element_type=F32
        )[0:1, :]
        part = jnp.concatenate([part, part], axis=1)
        parts.append(jnp.where(lane < 64, part, jnp.where(lane == 64, rz, jnp.where(lane == 65, pq, 0.0))))
    pay[...] = jnp.concatenate(parts + parts, axis=0)


def second(
    ready, got, bj, core, near, sub, zsub, ysub, kz, ky, kyt, kx, kxe, rs, z0, q0, dots,
    z_out, g_out, r_out, pay,
):
    ready(4)
    planes, images = apply(got, bj, core, near, sub, zsub, ysub, kz, ky, kyt, kx, kxe)
    alpha = dots[0:1, 64:65] / dots[0:1, 65:66]
    ready(12)
    zs, gs, rr = [], [], []
    for z in range(4):
        rr.append(rs[z] - alpha * q0[z])
        zs.append(z0[z] - alpha * planes[z])
        gs.append(q0[z] - alpha * images[z])
        z_out[z] = zs[z]
        g_out[z] = gs[z]
        r_out[z] = rr[z]
    new = total_of(rr, zs)
    own = total_of(zs, gs)
    cross = total_of([z0[z] for z in range(4)], gs)
    lane = lane_of((8, 128))
    pay[...] = jnp.where(lane == 0, new, jnp.where(lane == 1, own, jnp.where(lane == 2, cross, 0.0)))


def last(ready, got, dots, z0, q0, z1, g1, r1, x_out, r_out):
    total = jnp.sum(got[...], axis=0, keepdims=True)
    new, own, cross = total[:, 0:1], total[:, 1:2], total[:, 2:3]
    rz, pq = dots[0:1, 64:65], dots[0:1, 65:66]
    alpha = rz / pq
    beta = new / rz
    step = new / (own + 2.0 * beta * cross + beta * beta * pq)
    for z in range(4):
        x_out[z] = alpha * z0[z] + step * (z1[z] + beta * z0[z])
        r_out[z] = r1[z] - step * (g1[z] + beta * q0[z])


def body(right_side, phase_label, density_gain, subdomain, block_factor, coupling):
    slabs = lax.axis_size("slab")
    fac, cou = block_factor[0], coupling[0]
    grid, plane, edge = sds(4, 16, 1024), sds(16, 1024), sds(4, 1024)
    cores = [[i for i in range(slabs) if i % 2 == c] for c in range(2)]
    with_core = [(i, i ^ 1) for i in range(slabs)]
    with_near = [(i, i + 1 if i % 2 else i - 1) for i in range(1, slabs - 1)]

    def exchange(value, axis, groups=None):
        return lax.all_to_all(value, axis, 0, 0, tiled=True, axis_index_groups=groups)

    def swap(to_core, to_near):
        return lax.ppermute(to_core, "slab", with_core), lax.ppermute(to_near, "slab", with_near)

    mob, core, near, pay = call(
        begin,
        (grid, sds(384, 128), sds(384, 128), sds(4, 128, 128)),
        [pltpu.VMEM((64, 128), F32)],
        (0, 1, 2, 3, 4),
        (-4,),
    )(right_side, phase_label, density_gain, subdomain, fac)
    core, near = swap(core, near)
    got = exchange(pay, "quad")
    cols, pay = call(share, (sds(4, 64, 128), sds(32, 40, 128)), (), (1, 2), (1,))(got, fac, cou)
    pay, core, near = lax.optimization_barrier((pay, core, near))
    own = exchange(pay, "slab", cores)
    kz, ky, kyt, kx, kxe, inv, bj, to_core, to_near, ups, downs, zsub, ysub, beside = call(
        setup,
        (sds(5, 16, 1024), grid, edge, grid, sds(4, 16, 128), grid, grid, plane, plane, edge, edge)
        + (jax.ShapeDtypeStruct((2, 16, 1024), jnp.int32), jax.ShapeDtypeStruct((8, 1024), jnp.int32), sds(2, 64, 256)),
        (),
        (0,),
        (-10, -11),
    )(right_side, mob, core, near, got)
    own, bj_core, bj_near = lax.optimization_barrier((own, *swap(to_core, to_near)))
    other = lax.ppermute(own, "slab", with_core)
    work = [
        pltpu.VMEM((64, 64, 128), F32),
        pltpu.VMEM((64, 128), F32),
        pltpu.VMEM((64, 64, 128), F32),
        pltpu.VMEM((64, 128), F32),
        pltpu.VMEM((66, 64, 128), F32),
        pltpu.VMEM((64, 128), F32),
    ]
    part = call(chain_first, sds(4, 40, 128), work, (2, 4, 5), (-1,))(own, other, fac, beside, ups, downs)
    coarse = exchange(part, "quad")
    stencil = (subdomain, zsub, ysub, kz, ky, kyt, kx, kxe, right_side)
    z0, q0, pay = call(
        first, (grid, grid, sds(32, 8, 128)), [pltpu.VMEM((64, 128), F32)], (4, 12), (2,)
    )(coarse, bj, bj_core, bj_near, *stencil, cols)
    everyone = exchange(pay.reshape(256, 1, 128), BOTH).reshape(256, 128)
    bj1, to_core, to_near, ups, downs = call(smooth, (grid, plane, plane, edge, edge), (), (), (-4, -5))(q0, kz, inv)
    bj_core, bj_near = swap(to_core, to_near)
    part, dots = call(chain_second, (sds(4, 40, 128), sds(8, 128)), work, (0, 1, 3, 5, 6), (-1,))(
        own, other, everyone, fac, beside, ups, downs
    )
    coarse = exchange(part, "quad")
    z1, g1, r1, pay = call(second, (grid, grid, grid, sds(32, 8, 128)), (), (4, 12), (3,))(
        coarse, bj1, bj_core, bj_near, *stencil, z0, q0, dots
    )
    everyone = exchange(pay.reshape(256, 1, 128), BOTH).reshape(256, 128)
    return tuple(call(last, (grid, grid))(everyone, dots, z0, q0, z1, g1, r1))


def solution(mesh):
    spec = P("slab", "quad", None)
    return jax.shard_map(body, mesh=mesh, in_specs=(spec,) * 6, out_specs=(spec, spec), check_vma=False)
```

```python
import jax
import jax.numpy as jnp
from jax import lax
from jax.experimental import pallas as pl
from jax.experimental.pallas import tpu as pltpu
from jax.sharding import PartitionSpec as P

F32 = jnp.float32
HIGH = lax.Precision.HIGHEST
BOTH = ("slab", "quad")
PIECES = 4
GROUP = 16
SCALE = 2.0**-30


def sds(*shape):
    return jax.ShapeDtypeStruct(shape, F32)


def call(kernel, outs, scratch=(), far=(), spread_out=()):
    single = not isinstance(outs, tuple)
    shapes = (outs,) if single else outs
    whole = [-1 - i for i in spread_out if i < 0]
    copied = [i for i in spread_out if i >= 0]
    vmem, hbm = pl.BlockSpec(memory_space=pltpu.VMEM), pl.BlockSpec(memory_space=pltpu.HBM)

    def run(*args):
        count = len(args)
        extra = [pltpu.VMEM(args[i].shape, args[i].dtype) for i in far]
        extra += [pltpu.VMEM(shapes[i].shape, F32) for i in whole]
        extra += [pltpu.VMEM(shapes[i].shape[1:], F32) for i in copied]
        pieces_of = {i: PIECES if len(args[i].shape) == 3 and args[i].shape[0] % 8 == 0 else 1 for i in far}
        copies = sum(pieces_of.values()) + len(whole) + sum(shapes[i].shape[0] for i in copied)
        if copies:
            extra.append(pltpu.SemaphoreType.DMA((copies,)))

        def wrapped(*refs):
            ins, made = list(refs[:count]), list(refs[count : count + len(shapes)])
            rest = list(refs[count + len(shapes) : count + len(shapes) + len(scratch)])
            more = list(refs[count + len(shapes) + len(scratch) :])
            sems = more.pop() if copies else None
            coming, at = {}, 0
            for n, i in enumerate(far):
                size = ins[i].shape[0] // pieces_of[i]
                coming[i] = []
                for p in range(pieces_of[i]):
                    src, dst = ins[i], more[n]
                    if pieces_of[i] > 1:
                        src, dst = src.at[pl.ds(p * size, size)], dst.at[pl.ds(p * size, size)]
                    coming[i].append(pltpu.make_async_copy(src, dst, sems.at[at]))
                    coming[i][p].start()
                    at += 1
                ins[i] = more[n]
            targets = {}
            for n, i in enumerate(whole + copied):
                targets[i] = made[i]
                made[i] = more[len(far) + n]
            waited = set()

            def ready(*which, pieces=range(PIECES)):
                for i in which:
                    for p in pieces:
                        if i in coming and p < pieces_of[i] and (i, p) not in waited:
                            waited.add((i, p))
                            coming[i][p].wait()

            kernel(ready, *ins, *made, *rest)
            ready(*far)
            at = sum(pieces_of.values())
            going = []
            for i in whole:
                going.append(pltpu.make_async_copy(made[i], targets[i], sems.at[at]))
                at += 1
            for i in copied:
                for m in range(shapes[i].shape[0]):
                    going.append(pltpu.make_async_copy(made[i], targets[i].at[m], sems.at[at]))
                    at += 1
            for copy in going:
                copy.start()
            for copy in going:
                copy.wait()

        out = pl.pallas_call(
            wrapped,
            in_specs=[hbm if i in far else vmem for i in range(count)],
            out_specs=tuple(hbm if i in whole + copied else vmem for i in range(len(shapes))),
            out_shape=tuple(pltpu.HBM(s.shape, s.dtype) if i in whole + copied else s for i, s in enumerate(shapes)),
            scratch_shapes=list(scratch) + extra,
            compiler_params=pltpu.CompilerParams(vmem_limit_bytes=16 << 20),
            name=kernel.__name__,
        )(*[pltpu.with_memory_space_constraint(a, pltpu.HBM) if i in far else a for i, a in enumerate(args)])
        return out[0] if single else out

    return run


def harmonic(here, there):
    return jnp.where(there > 0, 2.0 * here * there / (here + there), here)


def x_before(plane):
    lane = lax.broadcasted_iota(jnp.int32, plane.shape, 1)
    return jnp.where(lane == 0, 0.0, pltpu.roll(plane, 1, 1))


def x_after(plane):
    width = plane.shape[1]
    lane = lax.broadcasted_iota(jnp.int32, plane.shape, 1)
    return jnp.where(lane == width - 1, 0.0, pltpu.roll(plane, width - 1, 1))


def y_before(plane, halo):
    row = lax.broadcasted_iota(jnp.int32, plane.shape, 0)
    return jnp.where(row == 0, halo, pltpu.roll(plane, 1, 0))


def y_after(plane, halo):
    height = plane.shape[0]
    row = lax.broadcasted_iota(jnp.int32, plane.shape, 0)
    return jnp.where(row == height - 1, halo, pltpu.roll(plane, height - 1, 0))


def lane_of(shape):
    return lax.broadcasted_iota(jnp.int32, shape, len(shape) - 1)


def restrict(sub_ref, field_ref, rows_ref, least=0):
    def group(g, unused):
        def tile(t, totals):
            rows = pl.ds(pl.multiple_of((t % 2) * 8, 8), 8)
            sub = sub_ref[t // 2, rows, :]
            field = field_ref[t // 2, rows, :]
            out = []
            for label in range(8):
                picked = jnp.where(sub == g * 8 + (label + least), field, 0.0)
                total = totals[label]
                for j in range(8):
                    total = total + picked[:, j * 128 : (j + 1) * 128]
                out.append(total)
            return tuple(out)

        totals = lax.fori_loop(0, 8, tile, tuple(jnp.zeros((8, 128), F32) for _ in range(8)))
        stacked = jnp.concatenate([jnp.sum(t, axis=0, keepdims=True) for t in totals], axis=0)
        rows_ref[pl.ds(pl.multiple_of(g * 8, 8), 8), :] = stacked
        return unused

    lax.fori_loop(0, 8, group, 0)
    return jnp.sum(rows_ref[...].T, axis=0, keepdims=True)


def look_up(table, index):
    wide = jnp.broadcast_to(table, (8, 128))
    rows = []
    for r in range(index.shape[0] // 8):
        parts = []
        for c in range(index.shape[1] // 128):
            part = index[r * 8 : (r + 1) * 8, c * 128 : (c + 1) * 128]
            parts.append(jnp.take_along_axis(wide, part, axis=1, mode="promise_in_bounds"))
        rows.append(jnp.concatenate(parts, axis=1))
    return jnp.concatenate(rows, axis=0)


def solve_lines(kz, inv, rhs):
    rho = [rhs[0] * inv[0]]
    for j in range(1, 4):
        rho.append((rhs[j] + kz[j] * rho[j - 1]) * inv[j])
    out = [None] * 4
    out[3] = rho[3]
    for j in (2, 1, 0):
        out[j] = rho[j] + kz[j + 1] * inv[j] * out[j + 1]
    return out


def parity():
    return lax.axis_index("slab") % 2


def choose(flag, a, b):
    return jnp.where(jnp.broadcast_to(flag, a.shape) == 1, a, b)


def spread(out, at, plane):
    h = plane.shape[0]
    for c in range(8):
        out[at + c * h : at + (c + 1) * h, :] = plane[:, c * 128 : (c + 1) * 128]


def gather_rows(block, at, h):
    return jnp.concatenate([block[at + c * h : at + (c + 1) * h, :] for c in range(8)], axis=1)


def face_for(dest, upward, downward):
    return choose((lax.axis_index("quad") + 1 == dest).astype(jnp.int32), upward, downward)


def begin(ready, rs, ph, gain, sub, fac, cou, mob, core, near, rs_out, sub_out, fac_out, cou_out, pay, rows):
    odd = parity()
    ready(0, 3)
    cin = restrict(sub, rs, rows)
    rs_out[...] = rs[...]
    sub_out[...] = sub[...] + 1
    ready(1, 2, 4, 5)
    fac_out[...] = fac[...]
    cou_out[...] = pack(choose(odd, cou[...], cou[...].T))
    ms, ss = [], []
    for z in range(4):
        m = 1.0 / (gain[z] * (0.001 + 0.999 * ph[z].astype(F32)))
        mob[z] = m
        ms.append(m)
        ss.append((sub[z] + 1).astype(F32))
    spread(core, 0, choose(odd, ms[0], ms[3]))
    spread(core, 128, choose(odd, ss[0], ss[3]))
    spread(near, 0, choose(odd, ms[3], ms[0]))
    spread(near, 128, choose(odd, ss[3], ss[0]))
    for part in (core, near):
        part[256:320, :] = fac[:, :128]
        part[320:384, :] = fac[:, 128:]
    upward = jnp.concatenate([m[15:16, :] for m in ms] + [s[15:16, :] for s in ss], axis=0)
    downward = jnp.concatenate([m[0:1, :] for m in ms] + [s[0:1, :] for s in ss], axis=0)
    both = jnp.concatenate([cin, cin], axis=1)
    lane = lane_of((64, 128))
    row = lax.broadcasted_iota(jnp.int32, (64, 128), 0)
    tail = jnp.where(row == 0, both, 0.0)
    for q in range(4):
        block = fac[:, (q // 2) * 128 : (q // 2 + 1) * 128]
        if q % 2:
            block = pltpu.roll(block, 64, 1)
        pay[q, 0:64, :] = jnp.where(lane < 64, block, tail)
        spread(pay.at[q], 64, face_for(q, upward, downward))


def send_faces(out, to_core, to_near, ups, downs):
    odd = parity()
    to_core[...] = choose(odd, out[0], out[3])
    to_near[...] = choose(odd, out[3], out[0])
    for z in range(4):
        ups[z : z + 1, :] = out[z][15:16, :]
        downs[z : z + 1, :] = out[z][0:1, :]


def share(ready, got, fac, cou, cols, pay):
    low = lane_of((64, 128)) < 64
    for h in range(2):
        cols[h] = jnp.where(low, got[2 * h, 0:64, :], pltpu.roll(got[2 * h + 1, 0:64, :], 64, 1))
    cins = [pltpu.roll(got[q, 0:8, :], 64, 1)[0:1, :64] for q in range(4)]
    cin = jnp.concatenate(cins, axis=1)
    rhs = lax.dot_general(
        jnp.broadcast_to(cin, (8, 256)), fac[...], (((1,), (1,)), ((), ())), precision=HIGH, preferred_element_type=F32
    )
    pay[0:32, :] = cou[...]
    pay[32:40, :] = jnp.concatenate([rhs, rhs], axis=1)


def setup(
    ready, rs, mob, core, near, got, kz, ky, kyt, kx, kxe, inv, to_core, to_near, ups, downs, zsub, ysub, beside
):
    odd = parity()
    quad = lax.axis_index("quad")
    planes = [mob[z] for z in range(4)]
    c_mob, n_mob = gather_rows(core, 0, 16), gather_rows(near, 0, 16)
    c_sub, n_sub = gather_rows(core, 128, 16), gather_rows(near, 128, 16)
    below = [choose(odd, c_mob, n_mob)] + planes[:3]
    above = planes[1:] + [choose(odd, n_mob, c_mob)]
    zsub[0] = choose(odd, c_sub, n_sub).astype(jnp.int32)
    zsub[1] = choose(odd, n_sub, c_sub).astype(jnp.int32)
    c_fac = jnp.concatenate([core[256:320, :], core[320:384, :]], axis=1)
    n_fac = jnp.concatenate([near[256:320, :], near[320:384, :]], axis=1)
    beside[0] = choose(odd, c_fac, n_fac)
    beside[1] = choose(odd, n_fac, c_fac)
    before = gather_rows(got[jnp.maximum(quad - 1, 0)], 64, 8)
    after = gather_rows(got[jnp.minimum(quad + 1, 3)], 64, 8)
    ylo = jnp.where(jnp.broadcast_to(quad, before.shape) > 0, before, 0.0)
    yhi = jnp.where(jnp.broadcast_to(quad, after.shape) < 3, after, 0.0)
    ysub[...] = jnp.concatenate([ylo[4:8, :], yhi[4:8, :]], axis=0).astype(jnp.int32)
    faces = [harmonic(planes[z], below[z]) for z in range(4)]
    faces.append(harmonic(planes[3], above[3]))
    for z in range(5):
        kz[z] = faces[z]
    diags = []
    for z in range(4):
        m = planes[z]
        a = harmonic(m, y_before(m, ylo[z : z + 1, :]))
        b = harmonic(m, y_after(m, yhi[z : z + 1, :]))
        c = harmonic(m, x_before(m))
        d = harmonic(m, x_after(m))
        ky[z] = a
        kyt[z : z + 1, :] = b[15:16, :]
        kx[z] = c
        kxe[z] = jnp.where(lane_of((16, 128)) == 127, d[:, 896:], 0.0)
        diags.append(faces[z] + faces[z + 1] + a + b + c + d)
    invs = [1.0 / diags[0]]
    for j in range(1, 4):
        invs.append(1.0 / (diags[j] - faces[j] * faces[j] * invs[j - 1]))
    for j in range(4):
        inv[j] = invs[j]
    ready(0)
    out = solve_lines(faces, invs, [rs[z] for z in range(4)])
    send_faces(out, to_core, to_near, ups, downs)


def smooth(ready, field, kz, inv, to_core, to_near, ups, downs):
    out = solve_lines([kz[z] for z in range(5)], [inv[z] for z in range(4)], [field[z] for z in range(4)])
    send_faces(out, to_core, to_near, ups, downs)


def unpack(packed):
    low = lane_of((32, 128)) < 64
    return jnp.concatenate([jnp.where(low, packed, 0.0), jnp.where(low, pltpu.roll(packed, 64, 1), 0.0)], axis=0)


def pack(mat):
    return jnp.concatenate([mat[:32, :64], mat[32:, :64]], axis=1)


def across(mat, row):
    return jnp.broadcast_to(jnp.sum(mat * row, axis=1, keepdims=True), (64, 128))


def down(mat, col):
    return jnp.sum(mat * col, axis=0, keepdims=True)


def as_col(rows_t, k):
    return jnp.broadcast_to(rows_t[:64, k : k + 1], (64, 128))


def condense(mats, rhs):
    rows_t = rhs.T
    held = {}
    col = as_col(rows_t, 1)
    held[1] = col
    row = None
    for k in range(2, GROUP):
        if k % 2:
            col = across(mats[k], row) + as_col(rows_t, k)
            held[k] = col
        else:
            row = down(mats[k], col) + rhs[k : k + 1, :]
            held[k] = row
    end = col
    for k in range(GROUP - 1, 0, -1):
        if k % 2:
            row = down(mats[k], col)
            if k > 1:
                row = row + held[k - 1]
        else:
            col = across(mats[k], row) + held[k - 1]
    return jnp.concatenate([end.T[0:1, :], jnp.zeros((1, 64), F32)], axis=1), row


def of_slab(own, other, k, rows):
    at_even, at_odd = (other, own) if k % 2 else (own, other)
    return choose(parity(), at_odd[k // 2, rows, :], at_even[k // 2, rows, :])


def local_mats(own, other, mats):
    for k in range(GROUP):
        mats[k] = unpack(of_slab(own, other, k, slice(0, 32)))


def condense_first(ready, own, other, out, rhs_out, mats, tall):
    rows = [of_slab(own, other, k, slice(32, 33)) for k in range(GROUP)]
    rhs = jnp.where(lane_of((GROUP, 128)) < 64, jnp.concatenate(rows, axis=0), 0.0)
    rhs_out[...] = rhs
    local_mats(own, other, mats)
    eye = lax.broadcasted_iota(jnp.int32, (64, 64), 0) == lax.broadcasted_iota(jnp.int32, (64, 64), 1)
    one = jnp.where(eye, 1.0, 0.0)
    runs = [[mats[b][:, :64] if b else one] for b in range(0, GROUP, 4)]
    for k in range(1, 4):
        for b, run in enumerate(runs):
            mat = mats[4 * b + k][:, :64]
            dims = (((1,), (1 if k % 2 else 0,)), ((), ()))
            run.append(lax.dot_general(run[-1], mat, dims, precision=HIGH, preferred_element_type=F32))
    psi = one * SCALE
    for b, run in enumerate(runs):
        wide = jnp.concatenate(run, axis=1)
        wide = wide * SCALE if b == 0 else jnp.dot(psi, wide, precision=HIGH, preferred_element_type=F32)
        tall[:, b * 256 : (b + 1) * 256] = wide
        psi = wide[:, 192:]
    gram = lax.dot_general(
        tall[...], tall[...], (((1,), (1,)), ((), ())), precision=HIGH, preferred_element_type=F32
    )
    end, start = condense(mats, rhs)
    out[0:32, :] = pack(psi.T * (1.0 / SCALE))
    out[32:64, :] = of_slab(own, other, 0, slice(0, 32))
    out[64:96, :] = pack(gram)
    out[96:104, :] = jnp.concatenate([end, start, rhs[0:1, :], jnp.zeros((5, 128), F32)], axis=0)


def condense_second(ready, got, own, other, out, rhs_out, mats):
    local_mats(own, other, mats)
    total = got[pl.ds(0, GROUP, 4), :]
    for q in range(1, 4):
        total = total + got[pl.ds(q, GROUP, 4), :]
    rhs = jnp.where(lane_of((GROUP, 128)) < 64, total, 0.0)
    rhs_out[...] = rhs
    end, start = condense(mats, rhs)
    dots = jnp.sum(total, axis=0, keepdims=True)
    out[...] = jnp.concatenate([end, start, rhs[0:1, :], dots, jnp.zeros((4, 128), F32)], axis=0)


def chain(ready, bounds, vecs, mats, rhs, fac, beside, ups, downs, out, ys, vs, wb, ws, wc):
    slab = lax.axis_index("slab")
    group, place = slab // GROUP, slab % GROUP
    groups = 4
    psi = [unpack(bounds[g, 0:32, :]) for g in range(groups)]
    lead = [unpack(bounds[g, 32:64, :]) for g in range(groups)]
    ends_t = jnp.concatenate([v[0:1, :] for v in vecs] + [jnp.zeros((4, 128), F32)], axis=0).T
    ends = [as_col(ends_t, g) for g in range(groups)]
    starts = []
    lasts = []
    for g in range(groups):
        begins = jnp.where(lane_of((1, 128)) < 64, vecs[g][2:3, :], 0.0)
        if g:
            begins = begins + down(lead[g], lasts[g - 1])
        starts.append(begins)
        ys[g : g + 1, :] = begins
        lasts.append(across(psi[g], begins) + ends[g])
    grown = []
    for g in range(groups):
        packed = bounds[g, 64:96, :]
        gram = jnp.concatenate([packed[:, :64], packed[:, 64:]], axis=0)
        part = jnp.dot(
            jnp.broadcast_to(starts[g][:, :64], (8, 64)), gram, precision=HIGH, preferred_element_type=F32
        )[0:1, :]
        part = part * (1.0 / SCALE) * (1.0 / SCALE)
        grown.append(jnp.concatenate([part, jnp.zeros((1, 64), F32)], axis=1) + vecs[g][1:2, :])
    vs[...] = jnp.zeros((8, 128), F32)
    wb[0] = jnp.zeros((64, 128), F32)
    wb[groups] = lasts[groups - 1]
    head = grown[groups - 1]
    vs[groups - 1 : groups, :] = head
    for g in range(groups - 2, -1, -1):
        back = across(lead[g + 1], head)
        wb[g + 1] = lasts[g] + back
        head = grown[g] + down(psi[g], back)
        vs[g : g + 1, :] = head
    rows_t = rhs[...].T
    row = ys[pl.ds(group, 1), :]
    held = {0: row}
    col = None
    for k in range(1, GROUP):
        if k % 2:
            col = across(mats[k], row) + as_col(rows_t, k)
            held[k] = col
        else:
            row = down(mats[k], col) + rhs[k : k + 1, :]
            held[k] = row
    wc[0] = wb[group]
    col = wb[group + 1]
    wc[GROUP] = col
    ws[GROUP + 1 : GROUP + 2, :] = vs[pl.ds(group + 1, 1), :]
    for k in range(GROUP - 1, 0, -1):
        if k % 2:
            row = down(mats[k], col) + held[k - 1]
            ws[k : k + 1, :] = row
        else:
            col = across(mats[k], row) + held[k - 1]
            wc[k] = col
    ready(*range(len(vecs) + 10))
    shares = ((0, fac[...]), (-1, beside[0]), (1, beside[1]))
    for j, (shift, table) in enumerate(shares):
        at = place + shift + 1
        from_row = ws[pl.ds(at, 1), :]
        from_col = wc[at].T[0:1, :]
        is_row = jnp.broadcast_to(at % 2, (1, 64)) == 1
        w = jnp.where(is_row, from_row[:, :64], from_col[:, :64])
        part = jnp.dot(jnp.broadcast_to(w, (8, 64)), table, precision=HIGH, preferred_element_type=F32)
        for q in range(4):
            out[q, 2 * j : 2 * j + 1, :] = part[0:1, :128]
            out[q, 2 * j + 1 : 2 * j + 2, :] = part[0:1, 128:]
    for q in range(4):
        out[q, 6:8, :] = jnp.zeros((2, 128), F32)
        spread(out.at[q], 8, face_for(q, ups[...], downs[...]))


def chain_first(ready, bounds, own, other, rhs, fac, beside, ups, downs, out, mats, *work):
    local_mats(own, other, mats)
    vecs = [bounds[g, 96:104, :] for g in range(4)]
    chain(ready, bounds, vecs, mats, rhs, fac, beside, ups, downs, out, *work)


def chain_second(ready, bounds, got, own, other, rhs, fac, beside, ups, downs, out, dots, mats, *work):
    local_mats(own, other, mats)
    vecs = [got[g] for g in range(4)]
    total = vecs[0][3:4, :] + vecs[1][3:4, :] + vecs[2][3:4, :] + vecs[3][3:4, :]
    dots[...] = jnp.broadcast_to(total, (8, 128))
    chain(ready, bounds, vecs, mats, rhs, fac, beside, ups, downs, out, *work)


def tables(got):
    quad = lax.axis_index("quad")
    total = got[0, 0:8, :] + got[1, 0:8, :] + got[2, 0:8, :] + got[3, 0:8, :]
    near = pltpu.roll(total, 1, 1)
    far = pltpu.roll(total, 65, 1)
    lane = lane_of((1, 128))
    valid = (lane >= 1) & (lane <= 64)

    def table(base, q):
        first = jnp.where(jnp.broadcast_to(q % 2, (1, 128)) == 1, far[base : base + 1, :], near[base : base + 1, :])
        second = jnp.where(
            jnp.broadcast_to(q % 2, (1, 128)) == 1, far[base + 1 : base + 2, :], near[base + 1 : base + 2, :]
        )
        picked = jnp.where(jnp.broadcast_to(q, (1, 128)) >= 2, second, first)
        return jnp.where(valid, picked, 0.0)

    return (
        table(0, quad),
        table(0, jnp.maximum(quad - 1, 0)),
        table(0, jnp.minimum(quad + 1, 3)),
        table(2, quad),
        table(4, quad),
    )


def apply(got, field, core, near, sub, zsub, ysub, kz, ky, kyt, kx, kxe, inv):
    odd = parity()
    quad = lax.axis_index("quad")
    own, t_yl, t_yh, t_zl, t_zh = tables(got)
    bj = solve_lines([kz[z] for z in range(5)], [inv[z] for z in range(4)], [field[z] for z in range(4)])
    planes = [bj[z] + look_up(own, sub[z]) for z in range(4)]
    below = choose(odd, core[...], near[...]) + look_up(t_zl, zsub[0])
    above = choose(odd, near[...], core[...]) + look_up(t_zh, zsub[1])
    before = gather_rows(got[jnp.maximum(quad - 1, 0)], 8, 4)
    after = gather_rows(got[jnp.minimum(quad + 1, 3)], 8, 4)
    before = jnp.where(jnp.broadcast_to(quad, before.shape) > 0, before, 0.0) + look_up(t_yl, ysub[...])[0:4, :]
    after = jnp.where(jnp.broadcast_to(quad, after.shape) < 3, after, 0.0) + look_up(t_yh, ysub[...])[4:8, :]
    line = [below] + planes + [above]
    rise = [kz[j] * (line[j + 1] - line[j]) for j in range(5)]
    images = []
    for z in range(4):
        v = planes[z]
        y_low = ky[z] * (v - y_before(v, before[z : z + 1, :]))
        y_high = y_after(y_low, kyt[z : z + 1, :] * (after[z : z + 1, :] - v[15:16, :]))
        x_low = kx[z] * (v - x_before(v))
        x_high = x_after(x_low)
        x_high = jnp.concatenate([x_high[:, :896], x_high[:, 896:] - kxe[z] * v[:, 896:]], axis=1)
        images.append((rise[z] - rise[z + 1]) + (y_low - y_high) + (x_low - x_high))
    return planes, images


def total_of(lefts, rights):
    acc = lefts[0] * rights[0]
    for a, b in zip(lefts[1:], rights[1:]):
        acc = acc + a * b
    return jnp.sum(jnp.sum(acc, axis=0, keepdims=True), axis=1, keepdims=True)


def first(
    ready, got, core, near, sub, zsub, ysub, kz, ky, kyt, kx, kxe, inv, rs, cols,
    z_out, q_out, pay, rows,
):
    ready(4)
    planes, images = apply(got, rs, core, near, sub, zsub, ysub, kz, ky, kyt, kx, kxe, inv)
    for z in range(4):
        z_out[z] = planes[z]
        q_out[z] = images[z]
    cin = jnp.broadcast_to(restrict(sub, q_out, rows, 1), (8, 64))
    ready(12)
    rz = total_of([rs[z] for z in range(4)], planes)
    pq = total_of(planes, images)
    lane = lane_of((1, 128))
    parts = []
    for q in range(4):
        part = lax.dot_general(
            cin, cols[q // 2][:, q % 2 * 64 : q % 2 * 64 + 64], (((1,), (1,)), ((), ())), precision=HIGH, preferred_element_type=F32
        )[0:1, :]
        part = jnp.concatenate([part, part], axis=1)
        parts.append(jnp.where(lane < 64, part, jnp.where(lane == 64, rz, jnp.where(lane == 65, pq, 0.0))))
    pay[...] = jnp.concatenate(parts + parts, axis=0)


def second(
    ready, got, core, near, sub, zsub, ysub, kz, ky, kyt, kx, kxe, inv, rs, z0, q0, dots,
    z_out, g_out, r_out, pay,
):
    ready(4)
    planes, images = apply(got, q0, core, near, sub, zsub, ysub, kz, ky, kyt, kx, kxe, inv)
    alpha = dots[0:1, 64:65] / dots[0:1, 65:66]
    ready(12)
    zs, gs, rr = [], [], []
    for z in range(4):
        rr.append(rs[z] - alpha * q0[z])
        zs.append(z0[z] - alpha * planes[z])
        gs.append(q0[z] - alpha * images[z])
        z_out[z] = zs[z]
        g_out[z] = gs[z]
        r_out[z] = rr[z]
    new = total_of(rr, zs)
    own = total_of(zs, gs)
    cross = total_of([z0[z] for z in range(4)], gs)
    lane = lane_of((8, 128))
    pay[...] = jnp.where(lane == 0, new, jnp.where(lane == 1, own, jnp.where(lane == 2, cross, 0.0)))


def last(ready, got, dots, z0, q0, z1, g1, r1, x_out, r_out):
    total = jnp.sum(got[...], axis=0, keepdims=True)
    new, own, cross = total[:, 0:1], total[:, 1:2], total[:, 2:3]
    rz, pq = dots[0:1, 64:65], dots[0:1, 65:66]
    alpha = rz / pq
    beta = new / rz
    step = new / (own + 2.0 * beta * cross + beta * beta * pq)
    for z in range(4):
        x_out[z] = alpha * z0[z] + step * (z1[z] + beta * z0[z])
        r_out[z] = r1[z] - step * (g1[z] + beta * q0[z])


def body(right_side, phase_label, density_gain, subdomain, block_factor, coupling):
    slabs = lax.axis_size("slab")
    fac, cou = block_factor[0], coupling[0]
    grid, plane, edge = sds(4, 16, 1024), sds(16, 1024), sds(4, 1024)
    quads = lax.axis_size("quad")
    within = [list(range(g + c, g + GROUP, 2)) for g in range(0, slabs, GROUP) for c in range(2)]
    planes = [list(range(g, g + GROUP * quads)) for g in range(0, slabs * quads, GROUP * quads)]
    between = [list(range(i, slabs, GROUP)) for i in range(GROUP)]
    with_core = [(i, i ^ 1) for i in range(slabs)]
    with_near = [(i, i + 1 if i % 2 else i - 1) for i in range(1, slabs - 1)]

    def exchange(value, axis, groups=None):
        return lax.all_to_all(value, axis, 0, 0, tiled=True, axis_index_groups=groups)

    def swap(to_core, to_near):
        return lax.ppermute(to_core, "slab", with_core), lax.ppermute(to_near, "slab", with_near)

    mob, core, near, rs, sub, fac, cou, pay = call(
        begin,
        (grid, sds(384, 128), sds(384, 128), grid, jax.ShapeDtypeStruct((4, 16, 1024), jnp.int32))
        + (sds(64, 256), sds(32, 128), sds(4, 128, 128)),
        [pltpu.VMEM((64, 128), F32)],
        (3, 0, 1, 2, 4, 5),
        (-8,),
    )(right_side, phase_label, density_gain, subdomain, fac, cou)
    core, near = swap(core, near)
    got = exchange(pay, "quad")
    cols, pay = call(share, (sds(2, 64, 128), sds(GROUP // 2, 40, 128)), (), (), (1,))(got, fac, cou)
    pay, core, near = lax.optimization_barrier((pay, core, near))
    own = exchange(pay, "slab", within)
    kz, ky, kyt, kx, kxe, inv, to_core, to_near, ups, downs, zsub, ysub, beside = call(
        setup,
        (sds(5, 16, 1024), grid, edge, grid, sds(4, 16, 128), grid, plane, plane, edge, edge)
        + (jax.ShapeDtypeStruct((2, 16, 1024), jnp.int32), jax.ShapeDtypeStruct((8, 1024), jnp.int32), sds(2, 64, 256)),
        (),
        (),
        (-9, -10),
    )(rs, mob, core, near, got)
    own, to_core, to_near = lax.optimization_barrier((own, to_core, to_near))
    other = lax.ppermute(own, "slab", with_core)
    mats = pltpu.VMEM((GROUP, 64, 128), F32)
    pay, rhs = call(
        condense_first,
        (sds(4, 104, 128), sds(GROUP, 128)),
        [mats, pltpu.VMEM((64, GROUP * 64), F32)],
        (),
        (0,),
    )(own, other)
    pay, to_core, to_near = lax.optimization_barrier((pay, to_core, to_near))
    bj_core, bj_near = swap(to_core, to_near)
    bounds = exchange(pay, "slab", between)
    bounds, bj_core, bj_near = lax.optimization_barrier((bounds, bj_core, bj_near))
    work = [
        mats,
        pltpu.VMEM((8, 128), F32),
        pltpu.VMEM((8, 128), F32),
        pltpu.VMEM((5, 64, 128), F32),
        pltpu.VMEM((GROUP + 8, 128), F32),
        pltpu.VMEM((GROUP + 2, 64, 128), F32),
    ]
    part = call(chain_first, sds(4, 40, 128), work, (6, 7), (-1,))(
        bounds, own, other, rhs, fac, beside, ups, downs
    )
    coarse = exchange(part, "quad")
    stencil = (sub, zsub, ysub, kz, ky, kyt, kx, kxe, inv, rs)
    z0, q0, pay = call(
        first, (grid, grid, sds(8, 8, 128)), [pltpu.VMEM((64, 128), F32)], (), (2,)
    )(coarse, bj_core, bj_near, *stencil, cols)
    plane_rows = exchange(pay.reshape(64, 1, 128), BOTH, planes).reshape(64, 128)
    to_core, to_near, ups, downs = call(smooth, (plane, plane, edge, edge), (), (), (-3, -4))(q0, kz, inv)
    bj_core, bj_near = swap(to_core, to_near)
    pay, rhs = call(condense_second, (sds(4, 8, 128), sds(GROUP, 128)), [mats], (), (0,))(plane_rows, own, other)
    vecs = exchange(pay, "slab", between)
    part, dots = call(chain_second, (sds(4, 40, 128), sds(8, 128)), work, (7, 8), (-1,))(
        bounds, vecs, own, other, rhs, fac, beside, ups, downs
    )
    coarse = exchange(part, "quad")
    z1, g1, r1, pay = call(second, (grid, grid, grid, sds(32, 8, 128)), (), (), (3,))(
        coarse, bj_core, bj_near, *stencil, z0, q0, dots
    )
    everyone = exchange(pay.reshape(256, 1, 128), BOTH).reshape(256, 128)
    return tuple(call(last, (grid, grid))(everyone, dots, z0, q0, z1, g1, r1))


def solution(mesh):
    spec = P("slab", "quad", None)
    return jax.shard_map(body, mesh=mesh, in_specs=(spec,) * 6, out_specs=(spec, spec), check_vma=False)
```

```python
import jax
import jax.numpy as jnp
from jax import lax
from jax.experimental import pallas as pl
from jax.experimental.pallas import tpu as pltpu
from jax.sharding import PartitionSpec as P

F32 = jnp.float32
HIGH = lax.Precision.HIGHEST
BOTH = ("slab", "quad")
PIECES = 4
GROUP = 16
SCALE = 2.0**-30


def sds(*shape):
    return jax.ShapeDtypeStruct(shape, F32)


def call(kernel, outs, scratch=(), far=(), spread_out=()):
    single = not isinstance(outs, tuple)
    shapes = (outs,) if single else outs
    whole = [-1 - i for i in spread_out if i < 0]
    copied = [i for i in spread_out if i >= 0]
    vmem, hbm = pl.BlockSpec(memory_space=pltpu.VMEM), pl.BlockSpec(memory_space=pltpu.HBM)

    def run(*args):
        count = len(args)
        extra = [pltpu.VMEM(args[i].shape, args[i].dtype) for i in far]
        extra += [pltpu.VMEM(shapes[i].shape, F32) for i in whole]
        extra += [pltpu.VMEM(shapes[i].shape[1:], F32) for i in copied]
        pieces_of = {i: PIECES if len(args[i].shape) == 3 and args[i].shape[0] % 8 == 0 else 1 for i in far}
        copies = sum(pieces_of.values()) + len(whole) + sum(shapes[i].shape[0] for i in copied)
        if copies:
            extra.append(pltpu.SemaphoreType.DMA((copies,)))

        def wrapped(*refs):
            ins, made = list(refs[:count]), list(refs[count : count + len(shapes)])
            rest = list(refs[count + len(shapes) : count + len(shapes) + len(scratch)])
            more = list(refs[count + len(shapes) + len(scratch) :])
            sems = more.pop() if copies else None
            coming, at = {}, 0
            for n, i in enumerate(far):
                size = ins[i].shape[0] // pieces_of[i]
                coming[i] = []
                for p in range(pieces_of[i]):
                    src, dst = ins[i], more[n]
                    if pieces_of[i] > 1:
                        src, dst = src.at[pl.ds(p * size, size)], dst.at[pl.ds(p * size, size)]
                    coming[i].append(pltpu.make_async_copy(src, dst, sems.at[at]))
                    coming[i][p].start()
                    at += 1
                ins[i] = more[n]
            targets = {}
            for n, i in enumerate(whole + copied):
                targets[i] = made[i]
                made[i] = more[len(far) + n]
            waited = set()

            def ready(*which, pieces=range(PIECES)):
                for i in which:
                    for p in pieces:
                        if i in coming and p < pieces_of[i] and (i, p) not in waited:
                            waited.add((i, p))
                            coming[i][p].wait()

            kernel(ready, *ins, *made, *rest)
            ready(*far)
            at = sum(pieces_of.values())
            going = []
            for i in whole:
                going.append(pltpu.make_async_copy(made[i], targets[i], sems.at[at]))
                at += 1
            for i in copied:
                for m in range(shapes[i].shape[0]):
                    going.append(pltpu.make_async_copy(made[i], targets[i].at[m], sems.at[at]))
                    at += 1
            for copy in going:
                copy.start()
            for copy in going:
                copy.wait()

        out = pl.pallas_call(
            wrapped,
            in_specs=[hbm if i in far else vmem for i in range(count)],
            out_specs=tuple(hbm if i in whole + copied else vmem for i in range(len(shapes))),
            out_shape=tuple(pltpu.HBM(s.shape, s.dtype) if i in whole + copied else s for i, s in enumerate(shapes)),
            scratch_shapes=list(scratch) + extra,
            compiler_params=pltpu.CompilerParams(vmem_limit_bytes=16 << 20),
            name=kernel.__name__,
        )(*[pltpu.with_memory_space_constraint(a, pltpu.HBM) if i in far else a for i, a in enumerate(args)])
        return out[0] if single else out

    return run


def harmonic(here, there):
    return jnp.where(there > 0, 2.0 * here * there / (here + there), here)


def x_before(plane):
    lane = lax.broadcasted_iota(jnp.int32, plane.shape, 1)
    return jnp.where(lane == 0, 0.0, pltpu.roll(plane, 1, 1))


def x_after(plane):
    width = plane.shape[1]
    lane = lax.broadcasted_iota(jnp.int32, plane.shape, 1)
    return jnp.where(lane == width - 1, 0.0, pltpu.roll(plane, width - 1, 1))


def y_before(plane, halo):
    row = lax.broadcasted_iota(jnp.int32, plane.shape, 0)
    return jnp.where(row == 0, halo, pltpu.roll(plane, 1, 0))


def y_after(plane, halo):
    height = plane.shape[0]
    row = lax.broadcasted_iota(jnp.int32, plane.shape, 0)
    return jnp.where(row == height - 1, halo, pltpu.roll(plane, height - 1, 0))


def lane_of(shape):
    return lax.broadcasted_iota(jnp.int32, shape, len(shape) - 1)


def restrict(sub_ref, field_ref, rows_ref, least=0):
    for base in range(0, 64, 16):

        def tile(t, totals):
            at = t // 2
            rows = pl.ds(pl.multiple_of((at % 2) * 8, 8), 8)
            lanes = pl.ds(pl.multiple_of((t % 2) * 512, 512), 512)
            sub = sub_ref[at // 2, rows, lanes]
            field = field_ref[at // 2, rows, lanes]
            out = []
            for label in range(16):
                picked = jnp.where(sub == base + label + least, field, 0.0)
                parts = [picked[:, j * 128 : (j + 1) * 128] for j in range(4)]
                out.append(totals[label] + ((parts[0] + parts[1]) + (parts[2] + parts[3])))
            return tuple(out)

        totals = lax.fori_loop(0, 16, tile, tuple(jnp.zeros((8, 128), F32) for _ in range(16)), unroll=4)
        for half in range(0, 16, 8):
            sums = [jnp.sum(t, axis=0, keepdims=True) for t in totals[half : half + 8]]
            rows_ref[base + half : base + half + 8, :] = jnp.concatenate(sums, axis=0)
    return jnp.sum(rows_ref[...].T, axis=0, keepdims=True)


def look_up(table, index):
    wide = jnp.broadcast_to(table, (8, 128))
    rows = []
    for r in range(index.shape[0] // 8):
        parts = []
        for c in range(index.shape[1] // 128):
            part = index[r * 8 : (r + 1) * 8, c * 128 : (c + 1) * 128]
            parts.append(jnp.take_along_axis(wide, part, axis=1, mode="promise_in_bounds"))
        rows.append(jnp.concatenate(parts, axis=1))
    return jnp.concatenate(rows, axis=0)


def solve_lines(kz, inv, rhs):
    rho = [rhs[0] * inv[0]]
    for j in range(1, 4):
        rho.append((rhs[j] + kz[j] * rho[j - 1]) * inv[j])
    out = [None] * 4
    out[3] = rho[3]
    for j in (2, 1, 0):
        out[j] = rho[j] + kz[j + 1] * inv[j] * out[j + 1]
    return out


def parity():
    return lax.axis_index("slab") % 2


def choose(flag, a, b):
    return jnp.where(jnp.broadcast_to(flag, a.shape) == 1, a, b)


def spread(out, at, plane):
    h = plane.shape[0]
    for c in range(8):
        out[at + c * h : at + (c + 1) * h, :] = plane[:, c * 128 : (c + 1) * 128]


def gather_rows(block, at, h):
    return jnp.concatenate([block[at + c * h : at + (c + 1) * h, :] for c in range(8)], axis=1)


def face_for(dest, upward, downward):
    return choose((lax.axis_index("quad") + 1 == dest).astype(jnp.int32), upward, downward)


def begin(ready, rs, ph, gain, sub, fac, cou, mob, core, near, rs_out, sub_out, fac_out, cou_out, pay, rows):
    odd = parity()
    ready(0, 3)
    cin = restrict(sub, rs, rows)
    rs_out[...] = rs[...]
    sub_out[...] = sub[...] + 1
    ready(1, 2, 4, 5)
    fac_out[...] = fac[...]
    cou_out[...] = pack(choose(odd, cou[...], cou[...].T))
    ms, ss = [], []
    for z in range(4):
        m = 1.0 / (gain[z] * (0.001 + 0.999 * ph[z].astype(F32)))
        mob[z] = m
        ms.append(m)
        ss.append((sub[z] + 1).astype(F32))
    spread(core, 0, choose(odd, ms[0], ms[3]))
    spread(core, 128, choose(odd, ss[0], ss[3]))
    spread(near, 0, choose(odd, ms[3], ms[0]))
    spread(near, 128, choose(odd, ss[3], ss[0]))
    for part in (core, near):
        part[256:320, :] = fac[:, :128]
        part[320:384, :] = fac[:, 128:]
    upward = jnp.concatenate([m[15:16, :] for m in ms] + [s[15:16, :] for s in ss], axis=0)
    downward = jnp.concatenate([m[0:1, :] for m in ms] + [s[0:1, :] for s in ss], axis=0)
    both = jnp.broadcast_to(jnp.concatenate([cin, cin], axis=1), (8, 128))
    for q in range(4):
        pay[q, 0:32, :] = pack(fac[:, q * 64 : (q + 1) * 64])
        pay[q, 32:40, :] = both
        spread(pay.at[q], 40, face_for(q, upward, downward))


def send_faces(out, to_core, to_near, ups, downs):
    odd = parity()
    to_core[...] = choose(odd, out[0], out[3])
    to_near[...] = choose(odd, out[3], out[0])
    for z in range(4):
        ups[z : z + 1, :] = out[z][15:16, :]
        downs[z : z + 1, :] = out[z][0:1, :]


def share(ready, got, fac, cou, cols, pay):
    for q in range(4):
        cols[q] = got[q, 0:32, :]
    cins = [got[q, 32:33, :64] for q in range(4)]
    cin = jnp.concatenate(cins, axis=1)
    rhs = lax.dot_general(
        jnp.broadcast_to(cin, (8, 256)), fac[...], (((1,), (1,)), ((), ())), precision=HIGH, preferred_element_type=F32
    )
    pay[0:32, :] = cou[...]
    pay[32:40, :] = jnp.concatenate([rhs, rhs], axis=1)


def setup(
    ready, rs, mob, core, near, got, kz, ky, kyt, kx, kxe, inv, to_core, to_near, ups, downs, zsub, ysub, beside
):
    odd = parity()
    quad = lax.axis_index("quad")
    planes = [mob[z] for z in range(4)]
    c_mob, n_mob = gather_rows(core, 0, 16), gather_rows(near, 0, 16)
    c_sub, n_sub = gather_rows(core, 128, 16), gather_rows(near, 128, 16)
    below = [choose(odd, c_mob, n_mob)] + planes[:3]
    above = planes[1:] + [choose(odd, n_mob, c_mob)]
    zsub[0] = choose(odd, c_sub, n_sub).astype(jnp.int32)
    zsub[1] = choose(odd, n_sub, c_sub).astype(jnp.int32)
    c_fac = jnp.concatenate([core[256:320, :], core[320:384, :]], axis=1)
    n_fac = jnp.concatenate([near[256:320, :], near[320:384, :]], axis=1)
    beside[0] = choose(odd, c_fac, n_fac)
    beside[1] = choose(odd, n_fac, c_fac)
    before = gather_rows(got[jnp.maximum(quad - 1, 0)], 40, 8)
    after = gather_rows(got[jnp.minimum(quad + 1, 3)], 40, 8)
    ylo = jnp.where(jnp.broadcast_to(quad, before.shape) > 0, before, 0.0)
    yhi = jnp.where(jnp.broadcast_to(quad, after.shape) < 3, after, 0.0)
    ysub[...] = jnp.concatenate([ylo[4:8, :], yhi[4:8, :]], axis=0).astype(jnp.int32)
    faces = [harmonic(planes[z], below[z]) for z in range(4)]
    faces.append(harmonic(planes[3], above[3]))
    for z in range(5):
        kz[z] = faces[z]
    diags = []
    for z in range(4):
        m = planes[z]
        a = harmonic(m, y_before(m, ylo[z : z + 1, :]))
        b = harmonic(m, y_after(m, yhi[z : z + 1, :]))
        c = harmonic(m, x_before(m))
        d = harmonic(m, x_after(m))
        ky[z] = a
        kyt[z : z + 1, :] = b[15:16, :]
        kx[z] = c
        kxe[z] = jnp.where(lane_of((16, 128)) == 127, d[:, 896:], 0.0)
        diags.append(faces[z] + faces[z + 1] + a + b + c + d)
    invs = [1.0 / diags[0]]
    for j in range(1, 4):
        invs.append(1.0 / (diags[j] - faces[j] * faces[j] * invs[j - 1]))
    for j in range(4):
        inv[j] = invs[j]
    ready(0)
    out = solve_lines(faces, invs, [rs[z] for z in range(4)])
    send_faces(out, to_core, to_near, ups, downs)


def smooth(ready, field, kz, inv, to_core, to_near, ups, downs):
    out = solve_lines([kz[z] for z in range(5)], [inv[z] for z in range(4)], [field[z] for z in range(4)])
    send_faces(out, to_core, to_near, ups, downs)


def unpack(packed):
    low = lane_of((32, 128)) < 64
    return jnp.concatenate([jnp.where(low, packed, 0.0), jnp.where(low, pltpu.roll(packed, 64, 1), 0.0)], axis=0)


def pack(mat):
    return jnp.concatenate([mat[:32, :64], mat[32:, :64]], axis=1)


def across(mat, row):
    return jnp.broadcast_to(jnp.sum(mat * row, axis=1, keepdims=True), (64, 128))


def down(mat, col):
    return jnp.sum(mat * col, axis=0, keepdims=True)


def as_col(rows_t, k):
    return jnp.broadcast_to(rows_t[:64, k : k + 1], (64, 128))


def condense(mats, rhs):
    rows_t = rhs.T
    held = {}
    col = as_col(rows_t, 1)
    held[1] = col
    row = None
    for k in range(2, GROUP):
        if k % 2:
            col = across(mats[k], row) + as_col(rows_t, k)
            held[k] = col
        else:
            row = down(mats[k], col) + rhs[k : k + 1, :]
            held[k] = row
    end = col
    for k in range(GROUP - 1, 0, -1):
        if k % 2:
            row = down(mats[k], col)
            if k > 1:
                row = row + held[k - 1]
        else:
            col = across(mats[k], row) + held[k - 1]
    return jnp.concatenate([end.T[0:1, :], jnp.zeros((1, 64), F32)], axis=1), row


def of_slab(own, other, k, rows):
    at_even, at_odd = (other, own) if k % 2 else (own, other)
    return choose(parity(), at_odd[k // 2, rows, :], at_even[k // 2, rows, :])


def local_mats(own, other, mats):
    for k in range(GROUP):
        mats[k] = unpack(of_slab(own, other, k, slice(0, 32)))


def condense_first(ready, own, other, out, rhs_out, mats, tall):
    rows = [of_slab(own, other, k, slice(32, 33)) for k in range(GROUP)]
    rhs = jnp.where(lane_of((GROUP, 128)) < 64, jnp.concatenate(rows, axis=0), 0.0)
    rhs_out[...] = rhs
    local_mats(own, other, mats)
    eye = lax.broadcasted_iota(jnp.int32, (64, 64), 0) == lax.broadcasted_iota(jnp.int32, (64, 64), 1)
    one = jnp.where(eye, 1.0, 0.0)
    runs = [[mats[b][:, :64] if b else one] for b in range(0, GROUP, 4)]
    for k in range(1, 4):
        for b, run in enumerate(runs):
            mat = mats[4 * b + k][:, :64]
            dims = (((1,), (1 if k % 2 else 0,)), ((), ()))
            run.append(lax.dot_general(run[-1], mat, dims, precision=HIGH, preferred_element_type=F32))
    psi = one * SCALE
    for b, run in enumerate(runs):
        wide = jnp.concatenate(run, axis=1)
        wide = wide * SCALE if b == 0 else jnp.dot(psi, wide, precision=HIGH, preferred_element_type=F32)
        tall[:, b * 256 : (b + 1) * 256] = wide
        psi = wide[:, 192:]
    gram = lax.dot_general(
        tall[...], tall[...], (((1,), (1,)), ((), ())), precision=HIGH, preferred_element_type=F32
    )
    end, start = condense(mats, rhs)
    out[0:32, :] = pack(psi.T * (1.0 / SCALE))
    out[32:64, :] = of_slab(own, other, 0, slice(0, 32))
    out[64:96, :] = pack(gram)
    out[96:104, :] = jnp.concatenate([end, start, rhs[0:1, :], jnp.zeros((5, 128), F32)], axis=0)


def condense_second(ready, got, own, other, out, rhs_out, mats):
    local_mats(own, other, mats)
    total = got[pl.ds(0, GROUP, 4), :]
    for q in range(1, 4):
        total = total + got[pl.ds(q, GROUP, 4), :]
    rhs = jnp.where(lane_of((GROUP, 128)) < 64, total, 0.0)
    rhs_out[...] = rhs
    end, start = condense(mats, rhs)
    dots = jnp.sum(total, axis=0, keepdims=True)
    out[...] = jnp.concatenate([end, start, rhs[0:1, :], dots, jnp.zeros((4, 128), F32)], axis=0)


def chain(ready, bounds, vecs, mats, rhs, fac, beside, ups, downs, out, ys, vs, wb, ws, wc):
    slab = lax.axis_index("slab")
    group, place = slab // GROUP, slab % GROUP
    groups = 4
    psi = [unpack(bounds[g, 0:32, :]) for g in range(groups)]
    lead = [unpack(bounds[g, 32:64, :]) for g in range(groups)]
    ends_t = jnp.concatenate([v[0:1, :] for v in vecs] + [jnp.zeros((4, 128), F32)], axis=0).T
    ends = [as_col(ends_t, g) for g in range(groups)]
    starts = []
    lasts = []
    for g in range(groups):
        begins = jnp.where(lane_of((1, 128)) < 64, vecs[g][2:3, :], 0.0)
        if g:
            begins = begins + down(lead[g], lasts[g - 1])
        starts.append(begins)
        ys[g : g + 1, :] = begins
        lasts.append(across(psi[g], begins) + ends[g])
    grown = []
    for g in range(groups):
        packed = bounds[g, 64:96, :]
        gram = jnp.concatenate([packed[:, :64], packed[:, 64:]], axis=0)
        part = jnp.dot(
            jnp.broadcast_to(starts[g][:, :64], (8, 64)), gram, precision=HIGH, preferred_element_type=F32
        )[0:1, :]
        part = part * (1.0 / SCALE) * (1.0 / SCALE)
        grown.append(jnp.concatenate([part, jnp.zeros((1, 64), F32)], axis=1) + vecs[g][1:2, :])
    vs[...] = jnp.zeros((8, 128), F32)
    wb[0] = jnp.zeros((64, 128), F32)
    wb[groups] = lasts[groups - 1]
    head = grown[groups - 1]
    vs[groups - 1 : groups, :] = head
    for g in range(groups - 2, -1, -1):
        back = across(lead[g + 1], head)
        wb[g + 1] = lasts[g] + back
        head = grown[g] + down(psi[g], back)
        vs[g : g + 1, :] = head
    rows_t = rhs[...].T
    row = ys[pl.ds(group, 1), :]
    held = {0: row}
    col = None
    for k in range(1, GROUP):
        if k % 2:
            col = across(mats[k], row) + as_col(rows_t, k)
            held[k] = col
        else:
            row = down(mats[k], col) + rhs[k : k + 1, :]
            held[k] = row
    wc[0] = wb[group]
    col = wb[group + 1]
    wc[GROUP] = col
    ws[GROUP + 1 : GROUP + 2, :] = vs[pl.ds(group + 1, 1), :]
    for k in range(GROUP - 1, 0, -1):
        if k % 2:
            row = down(mats[k], col) + held[k - 1]
            ws[k : k + 1, :] = row
        else:
            col = across(mats[k], row) + held[k - 1]
            wc[k] = col
    ready(*range(len(vecs) + 10))
    shares = ((0, fac[...]), (-1, beside[0]), (1, beside[1]))
    for j, (shift, table) in enumerate(shares):
        at = place + shift + 1
        from_row = ws[pl.ds(at, 1), :]
        from_col = wc[at].T[0:1, :]
        is_row = jnp.broadcast_to(at % 2, (1, 64)) == 1
        w = jnp.where(is_row, from_row[:, :64], from_col[:, :64])
        part = jnp.dot(jnp.broadcast_to(w, (8, 64)), table, precision=HIGH, preferred_element_type=F32)
        for q in range(4):
            out[q, 2 * j : 2 * j + 1, :] = part[0:1, :128]
            out[q, 2 * j + 1 : 2 * j + 2, :] = part[0:1, 128:]
    for q in range(4):
        out[q, 6:8, :] = jnp.zeros((2, 128), F32)
        spread(out.at[q], 8, face_for(q, ups[...], downs[...]))


def chain_first(ready, bounds, own, other, rhs, fac, beside, ups, downs, out, mats, *work):
    local_mats(own, other, mats)
    vecs = [bounds[g, 96:104, :] for g in range(4)]
    chain(ready, bounds, vecs, mats, rhs, fac, beside, ups, downs, out, *work)


def chain_second(ready, bounds, got, own, other, rhs, fac, beside, ups, downs, out, dots, mats, *work):
    local_mats(own, other, mats)
    vecs = [got[g] for g in range(4)]
    total = vecs[0][3:4, :] + vecs[1][3:4, :] + vecs[2][3:4, :] + vecs[3][3:4, :]
    dots[...] = jnp.broadcast_to(total, (8, 128))
    chain(ready, bounds, vecs, mats, rhs, fac, beside, ups, downs, out, *work)


def tables(got):
    quad = lax.axis_index("quad")
    total = got[0, 0:8, :] + got[1, 0:8, :] + got[2, 0:8, :] + got[3, 0:8, :]
    near = pltpu.roll(total, 1, 1)
    far = pltpu.roll(total, 65, 1)
    lane = lane_of((1, 128))
    valid = (lane >= 1) & (lane <= 64)

    def table(base, q):
        first = jnp.where(jnp.broadcast_to(q % 2, (1, 128)) == 1, far[base : base + 1, :], near[base : base + 1, :])
        second = jnp.where(
            jnp.broadcast_to(q % 2, (1, 128)) == 1, far[base + 1 : base + 2, :], near[base + 1 : base + 2, :]
        )
        picked = jnp.where(jnp.broadcast_to(q, (1, 128)) >= 2, second, first)
        return jnp.where(valid, picked, 0.0)

    return (
        table(0, quad),
        table(0, jnp.maximum(quad - 1, 0)),
        table(0, jnp.minimum(quad + 1, 3)),
        table(2, quad),
        table(4, quad),
    )


def apply(got, field, core, near, sub, zsub, ysub, kz, ky, kyt, kx, kxe, inv):
    odd = parity()
    quad = lax.axis_index("quad")
    own, t_yl, t_yh, t_zl, t_zh = tables(got)
    bj = solve_lines([kz[z] for z in range(5)], [inv[z] for z in range(4)], [field[z] for z in range(4)])
    planes = [bj[z] + look_up(own, sub[z]) for z in range(4)]
    below = choose(odd, core[...], near[...]) + look_up(t_zl, zsub[0])
    above = choose(odd, near[...], core[...]) + look_up(t_zh, zsub[1])
    before = gather_rows(got[jnp.maximum(quad - 1, 0)], 8, 4)
    after = gather_rows(got[jnp.minimum(quad + 1, 3)], 8, 4)
    before = jnp.where(jnp.broadcast_to(quad, before.shape) > 0, before, 0.0) + look_up(t_yl, ysub[...])[0:4, :]
    after = jnp.where(jnp.broadcast_to(quad, after.shape) < 3, after, 0.0) + look_up(t_yh, ysub[...])[4:8, :]
    line = [below] + planes + [above]
    rise = [kz[j] * (line[j + 1] - line[j]) for j in range(5)]
    images = []
    for z in range(4):
        v = planes[z]
        y_low = ky[z] * (v - y_before(v, before[z : z + 1, :]))
        y_high = y_after(y_low, kyt[z : z + 1, :] * (after[z : z + 1, :] - v[15:16, :]))
        x_low = kx[z] * (v - x_before(v))
        x_high = x_after(x_low)
        x_high = jnp.concatenate([x_high[:, :896], x_high[:, 896:] - kxe[z] * v[:, 896:]], axis=1)
        images.append((rise[z] - rise[z + 1]) + (y_low - y_high) + (x_low - x_high))
    return planes, images


def total_of(lefts, rights):
    acc = lefts[0] * rights[0]
    for a, b in zip(lefts[1:], rights[1:]):
        acc = acc + a * b
    return jnp.sum(jnp.sum(acc, axis=0, keepdims=True), axis=1, keepdims=True)


def first(
    ready, got, core, near, sub, zsub, ysub, kz, ky, kyt, kx, kxe, inv, rs, cols,
    z_out, q_out, pay, rows,
):
    ready(4)
    planes, images = apply(got, rs, core, near, sub, zsub, ysub, kz, ky, kyt, kx, kxe, inv)
    for z in range(4):
        z_out[z] = planes[z]
        q_out[z] = images[z]
    cin = jnp.broadcast_to(restrict(sub, q_out, rows, 1), (8, 64))
    ready(12)
    rz = total_of([rs[z] for z in range(4)], planes)
    pq = total_of(planes, images)
    lane = lane_of((1, 128))
    parts = []
    for q in range(4):
        part = lax.dot_general(
            cin, jnp.concatenate([cols[q, :, :64], cols[q, :, 64:]], axis=0), (((1,), (1,)), ((), ())), precision=HIGH, preferred_element_type=F32
        )[0:1, :]
        part = jnp.concatenate([part, part], axis=1)
        parts.append(jnp.where(lane < 64, part, jnp.where(lane == 64, rz, jnp.where(lane == 65, pq, 0.0))))
    pay[...] = jnp.concatenate(parts + parts, axis=0)


def second(
    ready, got, core, near, sub, zsub, ysub, kz, ky, kyt, kx, kxe, inv, rs, z0, q0, dots,
    z_out, g_out, r_out, pay,
):
    ready(4)
    planes, images = apply(got, q0, core, near, sub, zsub, ysub, kz, ky, kyt, kx, kxe, inv)
    alpha = dots[0:1, 64:65] / dots[0:1, 65:66]
    ready(12)
    zs, gs, rr = [], [], []
    for z in range(4):
        rr.append(rs[z] - alpha * q0[z])
        zs.append(z0[z] - alpha * planes[z])
        gs.append(q0[z] - alpha * images[z])
        z_out[z] = zs[z]
        g_out[z] = gs[z]
        r_out[z] = rr[z]
    new = total_of(rr, zs)
    own = total_of(zs, gs)
    cross = total_of([z0[z] for z in range(4)], gs)
    lane = lane_of((8, 128))
    pay[...] = jnp.where(lane == 0, new, jnp.where(lane == 1, own, jnp.where(lane == 2, cross, 0.0)))


def last(ready, got, dots, z0, q0, z1, g1, r1, x_out, r_out):
    total = jnp.sum(got[...], axis=0, keepdims=True)
    new, own, cross = total[:, 0:1], total[:, 1:2], total[:, 2:3]
    rz, pq = dots[0:1, 64:65], dots[0:1, 65:66]
    alpha = rz / pq
    beta = new / rz
    step = new / (own + 2.0 * beta * cross + beta * beta * pq)
    for z in range(4):
        x_out[z] = alpha * z0[z] + step * (z1[z] + beta * z0[z])
        r_out[z] = r1[z] - step * (g1[z] + beta * q0[z])


def body(right_side, phase_label, density_gain, subdomain, block_factor, coupling):
    slabs = lax.axis_size("slab")
    fac, cou = block_factor[0], coupling[0]
    grid, plane, edge = sds(4, 16, 1024), sds(16, 1024), sds(4, 1024)
    quads = lax.axis_size("quad")
    within = [list(range(g + c, g + GROUP, 2)) for g in range(0, slabs, GROUP) for c in range(2)]
    planes = [list(range(g, g + GROUP * quads)) for g in range(0, slabs * quads, GROUP * quads)]
    between = [list(range(i, slabs, GROUP)) for i in range(GROUP)]
    with_core = [(i, i ^ 1) for i in range(slabs)]
    with_near = [(i, i + 1 if i % 2 else i - 1) for i in range(1, slabs - 1)]

    def exchange(value, axis, groups=None):
        return lax.all_to_all(value, axis, 0, 0, tiled=True, axis_index_groups=groups)

    def swap(to_core, to_near):
        return lax.ppermute(to_core, "slab", with_core), lax.ppermute(to_near, "slab", with_near)

    mob, core, near, rs, sub, fac, cou, pay = call(
        begin,
        (grid, sds(384, 128), sds(384, 128), grid, jax.ShapeDtypeStruct((4, 16, 1024), jnp.int32))
        + (sds(64, 256), sds(32, 128), sds(4, 104, 128)),
        [pltpu.VMEM((64, 128), F32)],
        (3, 0, 1, 2, 4, 5),
        (-8,),
    )(right_side, phase_label, density_gain, subdomain, fac, cou)
    core, near = swap(core, near)
    got = exchange(pay, "quad")
    cols, pay = call(share, (sds(4, 32, 128), sds(GROUP // 2, 40, 128)), (), (), (1,))(got, fac, cou)
    pay, core, near = lax.optimization_barrier((pay, core, near))
    own = exchange(pay, "slab", within)
    kz, ky, kyt, kx, kxe, inv, to_core, to_near, ups, downs, zsub, ysub, beside = call(
        setup,
        (sds(5, 16, 1024), grid, edge, grid, sds(4, 16, 128), grid, plane, plane, edge, edge)
        + (jax.ShapeDtypeStruct((2, 16, 1024), jnp.int32), jax.ShapeDtypeStruct((8, 1024), jnp.int32), sds(2, 64, 256)),
        (),
        (),
        (-9, -10),
    )(rs, mob, core, near, got)
    own, to_core, to_near = lax.optimization_barrier((own, to_core, to_near))
    other = lax.ppermute(own, "slab", with_core)
    mats = pltpu.VMEM((GROUP, 64, 128), F32)
    pay, rhs = call(
        condense_first,
        (sds(4, 104, 128), sds(GROUP, 128)),
        [mats, pltpu.VMEM((64, GROUP * 64), F32)],
        (),
        (0,),
    )(own, other)
    pay, to_core, to_near = lax.optimization_barrier((pay, to_core, to_near))
    bj_core, bj_near = swap(to_core, to_near)
    bounds = exchange(pay, "slab", between)
    bounds, bj_core, bj_near = lax.optimization_barrier((bounds, bj_core, bj_near))
    work = [
        mats,
        pltpu.VMEM((8, 128), F32),
        pltpu.VMEM((8, 128), F32),
        pltpu.VMEM((5, 64, 128), F32),
        pltpu.VMEM((GROUP + 8, 128), F32),
        pltpu.VMEM((GROUP + 2, 64, 128), F32),
    ]
    part = call(chain_first, sds(4, 40, 128), work, (6, 7), (-1,))(
        bounds, own, other, rhs, fac, beside, ups, downs
    )
    coarse = exchange(part, "quad")
    stencil = (sub, zsub, ysub, kz, ky, kyt, kx, kxe, inv, rs)
    z0, q0, pay = call(
        first, (grid, grid, sds(8, 8, 128)), [pltpu.VMEM((64, 128), F32)], (), (2,)
    )(coarse, bj_core, bj_near, *stencil, cols)
    plane_rows = exchange(pay.reshape(64, 1, 128), BOTH, planes).reshape(64, 128)
    to_core, to_near, ups, downs = call(smooth, (plane, plane, edge, edge), (), (), (-3, -4))(q0, kz, inv)
    bj_core, bj_near = swap(to_core, to_near)
    pay, rhs = call(condense_second, (sds(4, 8, 128), sds(GROUP, 128)), [mats], (), (0,))(plane_rows, own, other)
    vecs = exchange(pay, "slab", between)
    part, dots = call(chain_second, (sds(4, 40, 128), sds(8, 128)), work, (7, 8), (-1,))(
        bounds, vecs, own, other, rhs, fac, beside, ups, downs
    )
    coarse = exchange(part, "quad")
    z1, g1, r1, pay = call(second, (grid, grid, grid, sds(32, 8, 128)), (), (), (3,))(
        coarse, bj_core, bj_near, *stencil, z0, q0, dots
    )
    everyone = exchange(pay.reshape(256, 1, 128), BOTH).reshape(256, 128)
    return tuple(call(last, (grid, grid))(everyone, dots, z0, q0, z1, g1, r1))


def solution(mesh):
    spec = P("slab", "quad", None)
    return jax.shard_map(body, mesh=mesh, in_specs=(spec,) * 6, out_specs=(spec, spec), check_vma=False)
```

```python
import jax
import jax.numpy as jnp
from jax import lax
from jax.experimental import pallas as pl
from jax.experimental.pallas import tpu as pltpu
from jax.sharding import PartitionSpec as P

F32 = jnp.float32
HIGH = lax.Precision.HIGHEST
BOTH = ("slab", "quad")
PIECES = 4
GROUP = 16
SCALE = 2.0**-30


def sds(*shape):
    return jax.ShapeDtypeStruct(shape, F32)


def call(kernel, outs, scratch=(), far=(), spread_out=()):
    single = not isinstance(outs, tuple)
    shapes = (outs,) if single else outs
    whole = [-1 - i for i in spread_out if i < 0]
    copied = [i for i in spread_out if i >= 0]
    vmem, hbm = pl.BlockSpec(memory_space=pltpu.VMEM), pl.BlockSpec(memory_space=pltpu.HBM)

    def run(*args):
        count = len(args)
        extra = [pltpu.VMEM(args[i].shape, args[i].dtype) for i in far]
        extra += [pltpu.VMEM(shapes[i].shape, F32) for i in whole]
        extra += [pltpu.VMEM(shapes[i].shape[1:], F32) for i in copied]
        pieces_of = {i: PIECES if len(args[i].shape) == 3 and args[i].shape[0] % 8 == 0 else 1 for i in far}
        copies = sum(pieces_of.values()) + len(whole) + sum(shapes[i].shape[0] for i in copied)
        if copies:
            extra.append(pltpu.SemaphoreType.DMA((copies,)))

        def wrapped(*refs):
            ins, made = list(refs[:count]), list(refs[count : count + len(shapes)])
            rest = list(refs[count + len(shapes) : count + len(shapes) + len(scratch)])
            more = list(refs[count + len(shapes) + len(scratch) :])
            sems = more.pop() if copies else None
            coming, at = {}, 0
            for n, i in enumerate(far):
                size = ins[i].shape[0] // pieces_of[i]
                coming[i] = []
                for p in range(pieces_of[i]):
                    src, dst = ins[i], more[n]
                    if pieces_of[i] > 1:
                        src, dst = src.at[pl.ds(p * size, size)], dst.at[pl.ds(p * size, size)]
                    coming[i].append(pltpu.make_async_copy(src, dst, sems.at[at]))
                    coming[i][p].start()
                    at += 1
                ins[i] = more[n]
            targets = {}
            for n, i in enumerate(whole + copied):
                targets[i] = made[i]
                made[i] = more[len(far) + n]
            waited = set()

            def ready(*which, pieces=range(PIECES)):
                for i in which:
                    for p in pieces:
                        if i in coming and p < pieces_of[i] and (i, p) not in waited:
                            waited.add((i, p))
                            coming[i][p].wait()

            kernel(ready, *ins, *made, *rest)
            ready(*far)
            at = sum(pieces_of.values())
            going = []
            for i in whole:
                going.append(pltpu.make_async_copy(made[i], targets[i], sems.at[at]))
                at += 1
            for i in copied:
                for m in range(shapes[i].shape[0]):
                    going.append(pltpu.make_async_copy(made[i], targets[i].at[m], sems.at[at]))
                    at += 1
            for copy in going:
                copy.start()
            for copy in going:
                copy.wait()

        out = pl.pallas_call(
            wrapped,
            in_specs=[hbm if i in far else vmem for i in range(count)],
            out_specs=tuple(hbm if i in whole + copied else vmem for i in range(len(shapes))),
            out_shape=tuple(pltpu.HBM(s.shape, s.dtype) if i in whole + copied else s for i, s in enumerate(shapes)),
            scratch_shapes=list(scratch) + extra,
            compiler_params=pltpu.CompilerParams(vmem_limit_bytes=16 << 20),
            name=kernel.__name__,
        )(*[pltpu.with_memory_space_constraint(a, pltpu.HBM) if i in far else a for i, a in enumerate(args)])
        return out[0] if single else out

    return run


def harmonic(here, there):
    return jnp.where(there > 0, 2.0 * here * there / (here + there), here)


def x_before(plane):
    lane = lax.broadcasted_iota(jnp.int32, plane.shape, 1)
    return jnp.where(lane == 0, 0.0, pltpu.roll(plane, 1, 1))


def x_after(plane):
    width = plane.shape[1]
    lane = lax.broadcasted_iota(jnp.int32, plane.shape, 1)
    return jnp.where(lane == width - 1, 0.0, pltpu.roll(plane, width - 1, 1))


def y_before(plane, halo):
    row = lax.broadcasted_iota(jnp.int32, plane.shape, 0)
    return jnp.where(row == 0, halo, pltpu.roll(plane, 1, 0))


def y_after(plane, halo):
    height = plane.shape[0]
    row = lax.broadcasted_iota(jnp.int32, plane.shape, 0)
    return jnp.where(row == height - 1, halo, pltpu.roll(plane, height - 1, 0))


def lane_of(shape):
    return lax.broadcasted_iota(jnp.int32, shape, len(shape) - 1)


def restrict(sub_ref, field_ref, rows_ref, least=0):
    for base in range(0, 64, 16):

        def tile(t, totals):
            at = t // 2
            rows = pl.ds(pl.multiple_of((at % 2) * 8, 8), 8)
            lanes = pl.ds(pl.multiple_of((t % 2) * 512, 512), 512)
            sub = sub_ref[at // 2, rows, lanes]
            field = field_ref[at // 2, rows, lanes]
            out = []
            for label in range(16):
                picked = jnp.where(sub == base + label + least, field, 0.0)
                parts = [picked[:, j * 128 : (j + 1) * 128] for j in range(4)]
                out.append(totals[label] + ((parts[0] + parts[1]) + (parts[2] + parts[3])))
            return tuple(out)

        totals = lax.fori_loop(0, 16, tile, tuple(jnp.zeros((8, 128), F32) for _ in range(16)), unroll=4)
        for half in range(0, 16, 8):
            sums = [jnp.sum(t, axis=0, keepdims=True) for t in totals[half : half + 8]]
            rows_ref[base + half : base + half + 8, :] = jnp.concatenate(sums, axis=0)
    return jnp.sum(rows_ref[...].T, axis=0, keepdims=True)


def look_up(table, index):
    wide = jnp.broadcast_to(table, (8, 128))
    rows = []
    for r in range(index.shape[0] // 8):
        parts = []
        for c in range(index.shape[1] // 128):
            part = index[r * 8 : (r + 1) * 8, c * 128 : (c + 1) * 128]
            parts.append(jnp.take_along_axis(wide, part, axis=1, mode="promise_in_bounds"))
        rows.append(jnp.concatenate(parts, axis=1))
    return jnp.concatenate(rows, axis=0)


def solve_lines(kz, inv, rhs):
    rho = [rhs[0] * inv[0]]
    for j in range(1, 4):
        rho.append((rhs[j] + kz[j] * rho[j - 1]) * inv[j])
    out = [None] * 4
    out[3] = rho[3]
    for j in (2, 1, 0):
        out[j] = rho[j] + kz[j + 1] * inv[j] * out[j + 1]
    return out


def parity():
    return lax.axis_index("slab") % 2


def choose(flag, a, b):
    return jnp.where(jnp.broadcast_to(flag, a.shape) == 1, a, b)


def spread(out, at, plane):
    h = plane.shape[0]
    for c in range(8):
        out[at + c * h : at + (c + 1) * h, :] = plane[:, c * 128 : (c + 1) * 128]


def gather_rows(block, at, h):
    return jnp.concatenate([block[at + c * h : at + (c + 1) * h, :] for c in range(8)], axis=1)


def face_for(dest, upward, downward):
    return choose((lax.axis_index("quad") + 1 == dest).astype(jnp.int32), upward, downward)


def begin(ready, rs, ph, gain, sub, fac, cou, mob, core, near, rs_out, sub_out, fac_out, cou_out, pay, rows):
    odd = parity()
    ready(0, 3)
    cin = restrict(sub, rs, rows)
    rs_out[...] = rs[...]
    sub_out[...] = sub[...] + 1
    ready(1, 2, 4, 5)
    fac_out[...] = fac[...]
    cou_out[...] = pack(choose(odd, cou[...], cou[...].T))
    ms, ss = [], []
    for z in range(4):
        m = 1.0 / (gain[z] * (0.001 + 0.999 * ph[z].astype(F32)))
        mob[z] = m
        ms.append(m)
        ss.append((sub[z] + 1).astype(F32))
    spread(core, 0, choose(odd, ms[0], ms[3]))
    spread(core, 128, choose(odd, ss[0], ss[3]))
    spread(near, 0, choose(odd, ms[3], ms[0]))
    spread(near, 128, choose(odd, ss[3], ss[0]))
    for part in (core, near):
        part[256:320, :] = fac[:, :128]
        part[320:384, :] = fac[:, 128:]
    upward = jnp.concatenate([m[15:16, :] for m in ms] + [s[15:16, :] for s in ss], axis=0)
    downward = jnp.concatenate([m[0:1, :] for m in ms] + [s[0:1, :] for s in ss], axis=0)
    both = jnp.concatenate([cin, cin], axis=1)
    lane = lane_of((64, 128))
    row = lax.broadcasted_iota(jnp.int32, (64, 128), 0)
    tail = jnp.where(row == 0, both, 0.0)
    for q in range(4):
        block = fac[:, (q // 2) * 128 : (q // 2 + 1) * 128]
        if q % 2:
            block = pltpu.roll(block, 64, 1)
        pay[q, 0:64, :] = jnp.where(lane < 64, block, tail)
        spread(pay.at[q], 64, face_for(q, upward, downward))


def send_faces(out, to_core, to_near, ups, downs):
    odd = parity()
    to_core[...] = choose(odd, out[0], out[3])
    to_near[...] = choose(odd, out[3], out[0])
    for z in range(4):
        ups[z : z + 1, :] = out[z][15:16, :]
        downs[z : z + 1, :] = out[z][0:1, :]


def share(ready, got, fac, cou, cols, pay):
    low = lane_of((64, 128)) < 64
    for h in range(2):
        cols[h] = jnp.where(low, got[2 * h, 0:64, :], pltpu.roll(got[2 * h + 1, 0:64, :], 64, 1))
    cins = [pltpu.roll(got[q, 0:8, :], 64, 1)[0:1, :64] for q in range(4)]
    cin = jnp.concatenate(cins, axis=1)
    rhs = lax.dot_general(
        jnp.broadcast_to(cin, (8, 256)), fac[...], (((1,), (1,)), ((), ())), precision=HIGH, preferred_element_type=F32
    )
    pay[0:32, :] = cou[...]
    pay[32:40, :] = jnp.concatenate([rhs, rhs], axis=1)


def setup(
    ready, rs, mob, core, near, got, kz, ky, kyt, kx, kxe, inv, to_core, to_near, ups, downs, zsub, ysub, beside
):
    odd = parity()
    quad = lax.axis_index("quad")
    planes = [mob[z] for z in range(4)]
    c_mob, n_mob = gather_rows(core, 0, 16), gather_rows(near, 0, 16)
    c_sub, n_sub = gather_rows(core, 128, 16), gather_rows(near, 128, 16)
    below = [choose(odd, c_mob, n_mob)] + planes[:3]
    above = planes[1:] + [choose(odd, n_mob, c_mob)]
    zsub[0] = choose(odd, c_sub, n_sub).astype(jnp.int32)
    zsub[1] = choose(odd, n_sub, c_sub).astype(jnp.int32)
    c_fac = jnp.concatenate([core[256:320, :], core[320:384, :]], axis=1)
    n_fac = jnp.concatenate([near[256:320, :], near[320:384, :]], axis=1)
    beside[0] = choose(odd, c_fac, n_fac)
    beside[1] = choose(odd, n_fac, c_fac)
    before = gather_rows(got[jnp.maximum(quad - 1, 0)], 64, 8)
    after = gather_rows(got[jnp.minimum(quad + 1, 3)], 64, 8)
    ylo = jnp.where(jnp.broadcast_to(quad, before.shape) > 0, before, 0.0)
    yhi = jnp.where(jnp.broadcast_to(quad, after.shape) < 3, after, 0.0)
    ysub[...] = jnp.concatenate([ylo[4:8, :], yhi[4:8, :]], axis=0).astype(jnp.int32)
    faces = [harmonic(planes[z], below[z]) for z in range(4)]
    faces.append(harmonic(planes[3], above[3]))
    for z in range(5):
        kz[z] = faces[z]
    diags = []
    for z in range(4):
        m = planes[z]
        a = harmonic(m, y_before(m, ylo[z : z + 1, :]))
        b = harmonic(m, y_after(m, yhi[z : z + 1, :]))
        c = harmonic(m, x_before(m))
        d = harmonic(m, x_after(m))
        ky[z] = a
        kyt[z : z + 1, :] = b[15:16, :]
        kx[z] = c
        kxe[z] = jnp.where(lane_of((16, 128)) == 127, d[:, 896:], 0.0)
        diags.append(faces[z] + faces[z + 1] + a + b + c + d)
    invs = [1.0 / diags[0]]
    for j in range(1, 4):
        invs.append(1.0 / (diags[j] - faces[j] * faces[j] * invs[j - 1]))
    for j in range(4):
        inv[j] = invs[j]
    ready(0)
    out = solve_lines(faces, invs, [rs[z] for z in range(4)])
    send_faces(out, to_core, to_near, ups, downs)


def smooth(ready, field, kz, inv, to_core, to_near, ups, downs):
    out = solve_lines([kz[z] for z in range(5)], [inv[z] for z in range(4)], [field[z] for z in range(4)])
    send_faces(out, to_core, to_near, ups, downs)


def unpack(packed):
    low = lane_of((32, 128)) < 64
    return jnp.concatenate([jnp.where(low, packed, 0.0), jnp.where(low, pltpu.roll(packed, 64, 1), 0.0)], axis=0)


def pack(mat):
    return jnp.concatenate([mat[:32, :64], mat[32:, :64]], axis=1)


def across(mat, row):
    return jnp.broadcast_to(jnp.sum(mat * row, axis=1, keepdims=True), (64, 128))


def down(mat, col):
    return jnp.sum(mat * col, axis=0, keepdims=True)


def as_col(rows_t, k):
    return jnp.broadcast_to(rows_t[:64, k : k + 1], (64, 128))


def condense(mats, rhs):
    rows_t = rhs.T
    held = {}
    col = as_col(rows_t, 1)
    held[1] = col
    row = None
    for k in range(2, GROUP):
        if k % 2:
            col = across(mats[k], row) + as_col(rows_t, k)
            held[k] = col
        else:
            row = down(mats[k], col) + rhs[k : k + 1, :]
            held[k] = row
    end = col
    for k in range(GROUP - 1, 0, -1):
        if k % 2:
            row = down(mats[k], col)
            if k > 1:
                row = row + held[k - 1]
        else:
            col = across(mats[k], row) + held[k - 1]
    return jnp.concatenate([end.T[0:1, :], jnp.zeros((1, 64), F32)], axis=1), row


def of_slab(own, other, k, rows):
    at_even, at_odd = (other, own) if k % 2 else (own, other)
    return choose(parity(), at_odd[k // 2, rows, :], at_even[k // 2, rows, :])


def local_mats(own, other, mats):
    for k in range(GROUP):
        mats[k] = unpack(of_slab(own, other, k, slice(0, 32)))


def condense_first(ready, own, other, out, rhs_out, mats, tall):
    rows = [of_slab(own, other, k, slice(32, 33)) for k in range(GROUP)]
    rhs = jnp.where(lane_of((GROUP, 128)) < 64, jnp.concatenate(rows, axis=0), 0.0)
    rhs_out[...] = rhs
    local_mats(own, other, mats)
    eye = lax.broadcasted_iota(jnp.int32, (64, 64), 0) == lax.broadcasted_iota(jnp.int32, (64, 64), 1)
    one = jnp.where(eye, 1.0, 0.0)
    runs = [[mats[b][:, :64] if b else one] for b in range(0, GROUP, 4)]
    for k in range(1, 4):
        for b, run in enumerate(runs):
            mat = mats[4 * b + k][:, :64]
            dims = (((1,), (1 if k % 2 else 0,)), ((), ()))
            run.append(lax.dot_general(run[-1], mat, dims, precision=HIGH, preferred_element_type=F32))
    psi = one * SCALE
    for b, run in enumerate(runs):
        wide = jnp.concatenate(run, axis=1)
        wide = wide * SCALE if b == 0 else jnp.dot(psi, wide, precision=HIGH, preferred_element_type=F32)
        tall[:, b * 256 : (b + 1) * 256] = wide
        psi = wide[:, 192:]
    gram = lax.dot_general(
        tall[...], tall[...], (((1,), (1,)), ((), ())), precision=HIGH, preferred_element_type=F32
    )
    end, start = condense(mats, rhs)
    out[0:32, :] = pack(psi.T * (1.0 / SCALE))
    out[32:64, :] = of_slab(own, other, 0, slice(0, 32))
    out[64:96, :] = pack(gram)
    out[96:104, :] = jnp.concatenate([end, start, rhs[0:1, :], jnp.zeros((5, 128), F32)], axis=0)


def condense_second(ready, got, own, other, out, rhs_out, mats):
    local_mats(own, other, mats)
    total = got[pl.ds(0, GROUP, 4), :]
    for q in range(1, 4):
        total = total + got[pl.ds(q, GROUP, 4), :]
    rhs = jnp.where(lane_of((GROUP, 128)) < 64, total, 0.0)
    rhs_out[...] = rhs
    end, start = condense(mats, rhs)
    dots = jnp.sum(total, axis=0, keepdims=True)
    out[...] = jnp.concatenate([end, start, rhs[0:1, :], dots, jnp.zeros((4, 128), F32)], axis=0)


def chain(ready, bounds, vecs, mats, rhs, fac, beside, ups, downs, out, ys, vs, wb, ws, wc):
    slab = lax.axis_index("slab")
    group, place = slab // GROUP, slab % GROUP
    groups = 4
    psi = [unpack(bounds[g, 0:32, :]) for g in range(groups)]
    lead = [unpack(bounds[g, 32:64, :]) for g in range(groups)]
    ends_t = jnp.concatenate([v[0:1, :] for v in vecs] + [jnp.zeros((4, 128), F32)], axis=0).T
    ends = [as_col(ends_t, g) for g in range(groups)]
    starts = []
    lasts = []
    for g in range(groups):
        begins = jnp.where(lane_of((1, 128)) < 64, vecs[g][2:3, :], 0.0)
        if g:
            begins = begins + down(lead[g], lasts[g - 1])
        starts.append(begins)
        ys[g : g + 1, :] = begins
        lasts.append(across(psi[g], begins) + ends[g])
    grown = []
    for g in range(groups):
        packed = bounds[g, 64:96, :]
        gram = jnp.concatenate([packed[:, :64], packed[:, 64:]], axis=0)
        part = jnp.dot(
            jnp.broadcast_to(starts[g][:, :64], (8, 64)), gram, precision=HIGH, preferred_element_type=F32
        )[0:1, :]
        part = part * (1.0 / SCALE) * (1.0 / SCALE)
        grown.append(jnp.concatenate([part, jnp.zeros((1, 64), F32)], axis=1) + vecs[g][1:2, :])
    vs[...] = jnp.zeros((8, 128), F32)
    wb[0] = jnp.zeros((64, 128), F32)
    wb[groups] = lasts[groups - 1]
    head = grown[groups - 1]
    vs[groups - 1 : groups, :] = head
    for g in range(groups - 2, -1, -1):
        back = across(lead[g + 1], head)
        wb[g + 1] = lasts[g] + back
        head = grown[g] + down(psi[g], back)
        vs[g : g + 1, :] = head
    rows_t = rhs[...].T
    row = ys[pl.ds(group, 1), :]
    held = {0: row}
    col = None
    for k in range(1, GROUP):
        if k % 2:
            col = across(mats[k], row) + as_col(rows_t, k)
            held[k] = col
        else:
            row = down(mats[k], col) + rhs[k : k + 1, :]
            held[k] = row
    wc[0] = wb[group]
    col = wb[group + 1]
    wc[GROUP] = col
    ws[GROUP + 1 : GROUP + 2, :] = vs[pl.ds(group + 1, 1), :]
    for k in range(GROUP - 1, 0, -1):
        if k % 2:
            row = down(mats[k], col) + held[k - 1]
            ws[k : k + 1, :] = row
        else:
            col = across(mats[k], row) + held[k - 1]
            wc[k] = col
    ready(*range(len(vecs) + 10))
    shares = ((0, fac[...]), (-1, beside[0]), (1, beside[1]))
    for j, (shift, table) in enumerate(shares):
        at = place + shift + 1
        from_row = ws[pl.ds(at, 1), :]
        from_col = wc[at].T[0:1, :]
        is_row = jnp.broadcast_to(at % 2, (1, 64)) == 1
        w = jnp.where(is_row, from_row[:, :64], from_col[:, :64])
        part = jnp.dot(jnp.broadcast_to(w, (8, 64)), table, precision=HIGH, preferred_element_type=F32)
        for q in range(4):
            out[q, 2 * j : 2 * j + 1, :] = part[0:1, :128]
            out[q, 2 * j + 1 : 2 * j + 2, :] = part[0:1, 128:]
    for q in range(4):
        out[q, 6:8, :] = jnp.zeros((2, 128), F32)
        spread(out.at[q], 8, face_for(q, ups[...], downs[...]))


def chain_first(ready, bounds, own, other, rhs, fac, beside, ups, downs, out, mats, *work):
    local_mats(own, other, mats)
    vecs = [bounds[g, 96:104, :] for g in range(4)]
    chain(ready, bounds, vecs, mats, rhs, fac, beside, ups, downs, out, *work)


def chain_second(ready, bounds, got, own, other, rhs, fac, beside, ups, downs, out, dots, mats, *work):
    local_mats(own, other, mats)
    vecs = [got[g] for g in range(4)]
    total = vecs[0][3:4, :] + vecs[1][3:4, :] + vecs[2][3:4, :] + vecs[3][3:4, :]
    dots[...] = jnp.broadcast_to(total, (8, 128))
    chain(ready, bounds, vecs, mats, rhs, fac, beside, ups, downs, out, *work)


def tables(got):
    quad = lax.axis_index("quad")
    total = got[0, 0:8, :] + got[1, 0:8, :] + got[2, 0:8, :] + got[3, 0:8, :]
    near = pltpu.roll(total, 1, 1)
    far = pltpu.roll(total, 65, 1)
    lane = lane_of((1, 128))
    valid = (lane >= 1) & (lane <= 64)

    def table(base, q):
        first = jnp.where(jnp.broadcast_to(q % 2, (1, 128)) == 1, far[base : base + 1, :], near[base : base + 1, :])
        second = jnp.where(
            jnp.broadcast_to(q % 2, (1, 128)) == 1, far[base + 1 : base + 2, :], near[base + 1 : base + 2, :]
        )
        picked = jnp.where(jnp.broadcast_to(q, (1, 128)) >= 2, second, first)
        return jnp.where(valid, picked, 0.0)

    return (
        table(0, quad),
        table(0, jnp.maximum(quad - 1, 0)),
        table(0, jnp.minimum(quad + 1, 3)),
        table(2, quad),
        table(4, quad),
    )


def apply(got, field, core, near, sub, zsub, ysub, kz, ky, kyt, kx, kxe, inv):
    odd = parity()
    quad = lax.axis_index("quad")
    own, t_yl, t_yh, t_zl, t_zh = tables(got)
    bj = solve_lines([kz[z] for z in range(5)], [inv[z] for z in range(4)], [field[z] for z in range(4)])
    planes = [bj[z] + look_up(own, sub[z]) for z in range(4)]
    below = choose(odd, core[...], near[...]) + look_up(t_zl, zsub[0])
    above = choose(odd, near[...], core[...]) + look_up(t_zh, zsub[1])
    before = gather_rows(got[jnp.maximum(quad - 1, 0)], 8, 4)
    after = gather_rows(got[jnp.minimum(quad + 1, 3)], 8, 4)
    before = jnp.where(jnp.broadcast_to(quad, before.shape) > 0, before, 0.0) + look_up(t_yl, ysub[...])[0:4, :]
    after = jnp.where(jnp.broadcast_to(quad, after.shape) < 3, after, 0.0) + look_up(t_yh, ysub[...])[4:8, :]
    line = [below] + planes + [above]
    rise = [kz[j] * (line[j + 1] - line[j]) for j in range(5)]
    images = []
    for z in range(4):
        v = planes[z]
        y_low = ky[z] * (v - y_before(v, before[z : z + 1, :]))
        y_high = y_after(y_low, kyt[z : z + 1, :] * (after[z : z + 1, :] - v[15:16, :]))
        x_low = kx[z] * (v - x_before(v))
        x_high = x_after(x_low)
        x_high = jnp.concatenate([x_high[:, :896], x_high[:, 896:] - kxe[z] * v[:, 896:]], axis=1)
        images.append((rise[z] - rise[z + 1]) + (y_low - y_high) + (x_low - x_high))
    return planes, images


def total_of(lefts, rights):
    acc = lefts[0] * rights[0]
    for a, b in zip(lefts[1:], rights[1:]):
        acc = acc + a * b
    return jnp.sum(jnp.sum(acc, axis=0, keepdims=True), axis=1, keepdims=True)


def first(
    ready, got, core, near, sub, zsub, ysub, kz, ky, kyt, kx, kxe, inv, rs, cols,
    z_out, q_out, pay, rows,
):
    ready(4)
    planes, images = apply(got, rs, core, near, sub, zsub, ysub, kz, ky, kyt, kx, kxe, inv)
    for z in range(4):
        z_out[z] = planes[z]
        q_out[z] = images[z]
    cin = jnp.broadcast_to(restrict(sub, q_out, rows, 1), (8, 64))
    ready(12)
    rz = total_of([rs[z] for z in range(4)], planes)
    pq = total_of(planes, images)
    lane = lane_of((1, 128))
    parts = []
    for q in range(4):
        part = lax.dot_general(
            cin, cols[q // 2][:, q % 2 * 64 : q % 2 * 64 + 64], (((1,), (1,)), ((), ())), precision=HIGH, preferred_element_type=F32
        )[0:1, :]
        part = jnp.concatenate([part, part], axis=1)
        parts.append(jnp.where(lane < 64, part, jnp.where(lane == 64, rz, jnp.where(lane == 65, pq, 0.0))))
    pay[...] = jnp.concatenate(parts + parts, axis=0)


def second(
    ready, got, core, near, sub, zsub, ysub, kz, ky, kyt, kx, kxe, inv, rs, z0, q0, dots,
    z_out, g_out, r_out, pay,
):
    ready(4)
    planes, images = apply(got, q0, core, near, sub, zsub, ysub, kz, ky, kyt, kx, kxe, inv)
    alpha = dots[0:1, 64:65] / dots[0:1, 65:66]
    ready(12)
    zs, gs, rr = [], [], []
    for z in range(4):
        rr.append(rs[z] - alpha * q0[z])
        zs.append(z0[z] - alpha * planes[z])
        gs.append(q0[z] - alpha * images[z])
        z_out[z] = zs[z]
        g_out[z] = gs[z]
        r_out[z] = rr[z]
    new = total_of(rr, zs)
    own = total_of(zs, gs)
    cross = total_of([z0[z] for z in range(4)], gs)
    lane = lane_of((8, 128))
    pay[...] = jnp.where(lane == 0, new, jnp.where(lane == 1, own, jnp.where(lane == 2, cross, 0.0)))


def last(ready, got, dots, z0, q0, z1, g1, r1, x_out, r_out):
    total = jnp.sum(got[...], axis=0, keepdims=True)
    new, own, cross = total[:, 0:1], total[:, 1:2], total[:, 2:3]
    rz, pq = dots[0:1, 64:65], dots[0:1, 65:66]
    alpha = rz / pq
    beta = new / rz
    step = new / (own + 2.0 * beta * cross + beta * beta * pq)
    for z in range(4):
        x_out[z] = alpha * z0[z] + step * (z1[z] + beta * z0[z])
        r_out[z] = r1[z] - step * (g1[z] + beta * q0[z])


def body(right_side, phase_label, density_gain, subdomain, block_factor, coupling):
    slabs = lax.axis_size("slab")
    fac, cou = block_factor[0], coupling[0]
    grid, plane, edge = sds(4, 16, 1024), sds(16, 1024), sds(4, 1024)
    quads = lax.axis_size("quad")
    within = [list(range(g + c, g + GROUP, 2)) for g in range(0, slabs, GROUP) for c in range(2)]
    planes = [list(range(g, g + GROUP * quads)) for g in range(0, slabs * quads, GROUP * quads)]
    between = [list(range(i, slabs, GROUP)) for i in range(GROUP)]
    with_core = [(i, i ^ 1) for i in range(slabs)]
    with_near = [(i, i + 1 if i % 2 else i - 1) for i in range(1, slabs - 1)]

    def exchange(value, axis, groups=None):
        return lax.all_to_all(value, axis, 0, 0, tiled=True, axis_index_groups=groups)

    def swap(to_core, to_near):
        return lax.ppermute(to_core, "slab", with_core), lax.ppermute(to_near, "slab", with_near)

    mob, core, near, rs, sub, fac, cou, pay = call(
        begin,
        (grid, sds(384, 128), sds(384, 128), grid, jax.ShapeDtypeStruct((4, 16, 1024), jnp.int32))
        + (sds(64, 256), sds(32, 128), sds(4, 128, 128)),
        [pltpu.VMEM((64, 128), F32)],
        (3, 0, 1, 2, 4, 5),
        (-8,),
    )(right_side, phase_label, density_gain, subdomain, fac, cou)
    core, near = swap(core, near)
    got = exchange(pay, "quad")
    cols, pay = call(share, (sds(2, 64, 128), sds(GROUP // 2, 40, 128)), (), (), (1,))(got, fac, cou)
    pay, core, near = lax.optimization_barrier((pay, core, near))
    own = exchange(pay, "slab", within)
    kz, ky, kyt, kx, kxe, inv, to_core, to_near, ups, downs, zsub, ysub, beside = call(
        setup,
        (sds(5, 16, 1024), grid, edge, grid, sds(4, 16, 128), grid, plane, plane, edge, edge)
        + (jax.ShapeDtypeStruct((2, 16, 1024), jnp.int32), jax.ShapeDtypeStruct((8, 1024), jnp.int32), sds(2, 64, 256)),
        (),
        (),
        (-9, -10),
    )(rs, mob, core, near, got)
    own, to_core, to_near = lax.optimization_barrier((own, to_core, to_near))
    other = lax.ppermute(own, "slab", with_core)
    mats = pltpu.VMEM((GROUP, 64, 128), F32)
    pay, rhs = call(
        condense_first,
        (sds(4, 104, 128), sds(GROUP, 128)),
        [mats, pltpu.VMEM((64, GROUP * 64), F32)],
        (),
        (0,),
    )(own, other)
    pay, to_core, to_near = lax.optimization_barrier((pay, to_core, to_near))
    bj_core, bj_near = swap(to_core, to_near)
    bounds = exchange(pay, "slab", between)
    bounds, bj_core, bj_near = lax.optimization_barrier((bounds, bj_core, bj_near))
    work = [
        mats,
        pltpu.VMEM((8, 128), F32),
        pltpu.VMEM((8, 128), F32),
        pltpu.VMEM((5, 64, 128), F32),
        pltpu.VMEM((GROUP + 8, 128), F32),
        pltpu.VMEM((GROUP + 2, 64, 128), F32),
    ]
    part = call(chain_first, sds(4, 40, 128), work, (6, 7), (-1,))(
        bounds, own, other, rhs, fac, beside, ups, downs
    )
    coarse = exchange(part, "quad")
    stencil = (sub, zsub, ysub, kz, ky, kyt, kx, kxe, inv, rs)
    z0, q0, pay = call(
        first, (grid, grid, sds(8, 8, 128)), [pltpu.VMEM((64, 128), F32)], (), (2,)
    )(coarse, bj_core, bj_near, *stencil, cols)
    plane_rows = exchange(pay.reshape(64, 1, 128), BOTH, planes).reshape(64, 128)
    to_core, to_near, ups, downs = call(smooth, (plane, plane, edge, edge), (), (), (-3, -4))(q0, kz, inv)
    bj_core, bj_near = swap(to_core, to_near)
    pay, rhs = call(condense_second, (sds(4, 8, 128), sds(GROUP, 128)), [mats], (), (0,))(plane_rows, own, other)
    vecs = exchange(pay, "slab", between)
    part, dots = call(chain_second, (sds(4, 40, 128), sds(8, 128)), work, (7, 8), (-1,))(
        bounds, vecs, own, other, rhs, fac, beside, ups, downs
    )
    coarse = exchange(part, "quad")
    z1, g1, r1, pay = call(second, (grid, grid, grid, sds(32, 8, 128)), (), (), (3,))(
        coarse, bj_core, bj_near, *stencil, z0, q0, dots
    )
    everyone = exchange(pay.reshape(256, 1, 128), BOTH).reshape(256, 128)
    return tuple(call(last, (grid, grid))(everyone, dots, z0, q0, z1, g1, r1))


def solution(mesh):
    spec = P("slab", "quad", None)
    return jax.shard_map(body, mesh=mesh, in_specs=(spec,) * 6, out_specs=(spec, spec), check_vma=False)
```

```python
import jax
import jax.numpy as jnp
from jax import lax
from jax.experimental import pallas as pl
from jax.experimental.pallas import tpu as pltpu
from jax.sharding import PartitionSpec as P

F32 = jnp.float32
HIGH = lax.Precision.HIGHEST
BOTH = ("slab", "quad")
PIECES = 4
GROUP = 16
SCALE = 2.0**-30


def sds(*shape):
    return jax.ShapeDtypeStruct(shape, F32)


def call(kernel, outs, scratch=(), far=(), spread_out=()):
    single = not isinstance(outs, tuple)
    shapes = (outs,) if single else outs
    whole = [-1 - i for i in spread_out if i < 0]
    copied = [i for i in spread_out if i >= 0]
    vmem, hbm = pl.BlockSpec(memory_space=pltpu.VMEM), pl.BlockSpec(memory_space=pltpu.HBM)

    def run(*args):
        count = len(args)
        extra = [pltpu.VMEM(args[i].shape, args[i].dtype) for i in far]
        extra += [pltpu.VMEM(shapes[i].shape, F32) for i in whole]
        extra += [pltpu.VMEM(shapes[i].shape[1:], F32) for i in copied]
        pieces_of = {i: PIECES if len(args[i].shape) == 3 and args[i].shape[0] % 8 == 0 else 1 for i in far}
        copies = sum(pieces_of.values()) + len(whole) + sum(shapes[i].shape[0] for i in copied)
        if copies:
            extra.append(pltpu.SemaphoreType.DMA((copies,)))

        def wrapped(*refs):
            ins, made = list(refs[:count]), list(refs[count : count + len(shapes)])
            rest = list(refs[count + len(shapes) : count + len(shapes) + len(scratch)])
            more = list(refs[count + len(shapes) + len(scratch) :])
            sems = more.pop() if copies else None
            coming, at = {}, 0
            for n, i in enumerate(far):
                size = ins[i].shape[0] // pieces_of[i]
                coming[i] = []
                for p in range(pieces_of[i]):
                    src, dst = ins[i], more[n]
                    if pieces_of[i] > 1:
                        src, dst = src.at[pl.ds(p * size, size)], dst.at[pl.ds(p * size, size)]
                    coming[i].append(pltpu.make_async_copy(src, dst, sems.at[at]))
                    coming[i][p].start()
                    at += 1
                ins[i] = more[n]
            targets = {}
            for n, i in enumerate(whole + copied):
                targets[i] = made[i]
                made[i] = more[len(far) + n]
            waited = set()

            def ready(*which, pieces=range(PIECES)):
                for i in which:
                    for p in pieces:
                        if i in coming and p < pieces_of[i] and (i, p) not in waited:
                            waited.add((i, p))
                            coming[i][p].wait()

            kernel(ready, *ins, *made, *rest)
            ready(*far)
            at = sum(pieces_of.values())
            going = []
            for i in whole:
                going.append(pltpu.make_async_copy(made[i], targets[i], sems.at[at]))
                at += 1
            for i in copied:
                for m in range(shapes[i].shape[0]):
                    going.append(pltpu.make_async_copy(made[i], targets[i].at[m], sems.at[at]))
                    at += 1
            for copy in going:
                copy.start()
            for copy in going:
                copy.wait()

        out = pl.pallas_call(
            wrapped,
            in_specs=[hbm if i in far else vmem for i in range(count)],
            out_specs=tuple(hbm if i in whole + copied else vmem for i in range(len(shapes))),
            out_shape=tuple(pltpu.HBM(s.shape, s.dtype) if i in whole + copied else s for i, s in enumerate(shapes)),
            scratch_shapes=list(scratch) + extra,
            compiler_params=pltpu.CompilerParams(vmem_limit_bytes=16 << 20),
            name=kernel.__name__,
        )(*[pltpu.with_memory_space_constraint(a, pltpu.HBM) if i in far else a for i, a in enumerate(args)])
        return out[0] if single else out

    return run


def harmonic(here, there):
    return jnp.where(there > 0, 2.0 * here * there / (here + there), here)


def x_before(plane):
    lane = lax.broadcasted_iota(jnp.int32, plane.shape, 1)
    return jnp.where(lane == 0, 0.0, pltpu.roll(plane, 1, 1))


def x_after(plane):
    width = plane.shape[1]
    lane = lax.broadcasted_iota(jnp.int32, plane.shape, 1)
    return jnp.where(lane == width - 1, 0.0, pltpu.roll(plane, width - 1, 1))


def y_before(plane, halo):
    row = lax.broadcasted_iota(jnp.int32, plane.shape, 0)
    return jnp.where(row == 0, halo, pltpu.roll(plane, 1, 0))


def y_after(plane, halo):
    height = plane.shape[0]
    row = lax.broadcasted_iota(jnp.int32, plane.shape, 0)
    return jnp.where(row == height - 1, halo, pltpu.roll(plane, height - 1, 0))


def lane_of(shape):
    return lax.broadcasted_iota(jnp.int32, shape, len(shape) - 1)


def restrict(sub_ref, field_ref, rows_ref, least=0):
    for base in range(0, 64, 16):

        def tile(t, totals):
            at = t // 2
            rows = pl.ds(pl.multiple_of((at % 2) * 8, 8), 8)
            lanes = pl.ds(pl.multiple_of((t % 2) * 512, 512), 512)
            sub = sub_ref[at // 2, rows, lanes]
            field = field_ref[at // 2, rows, lanes]
            out = []
            for label in range(16):
                picked = jnp.where(sub == base + label + least, field, 0.0)
                parts = [picked[:, j * 128 : (j + 1) * 128] for j in range(4)]
                out.append(totals[label] + ((parts[0] + parts[1]) + (parts[2] + parts[3])))
            return tuple(out)

        totals = lax.fori_loop(0, 16, tile, tuple(jnp.zeros((8, 128), F32) for _ in range(16)), unroll=4)
        for half in range(0, 16, 8):
            sums = [jnp.sum(t, axis=0, keepdims=True) for t in totals[half : half + 8]]
            rows_ref[base + half : base + half + 8, :] = jnp.concatenate(sums, axis=0)
    return jnp.sum(rows_ref[...].T, axis=0, keepdims=True)


def look_up(table, index):
    wide = jnp.broadcast_to(table, (8, 128))
    rows = []
    for r in range(index.shape[0] // 8):
        parts = []
        for c in range(index.shape[1] // 128):
            part = index[r * 8 : (r + 1) * 8, c * 128 : (c + 1) * 128]
            parts.append(jnp.take_along_axis(wide, part, axis=1, mode="promise_in_bounds"))
        rows.append(jnp.concatenate(parts, axis=1))
    return jnp.concatenate(rows, axis=0)


def solve_lines(kz, inv, rhs):
    rho = [rhs[0] * inv[0]]
    for j in range(1, 4):
        rho.append((rhs[j] + kz[j] * rho[j - 1]) * inv[j])
    out = [None] * 4
    out[3] = rho[3]
    for j in (2, 1, 0):
        out[j] = rho[j] + kz[j + 1] * inv[j] * out[j + 1]
    return out


def parity():
    return lax.axis_index("slab") % 2


def choose(flag, a, b):
    return jnp.where(jnp.broadcast_to(flag, a.shape) == 1, a, b)


def spread(out, at, plane):
    h = plane.shape[0]
    for c in range(8):
        out[at + c * h : at + (c + 1) * h, :] = plane[:, c * 128 : (c + 1) * 128]


def gather_rows(block, at, h):
    return jnp.concatenate([block[at + c * h : at + (c + 1) * h, :] for c in range(8)], axis=1)


def face_for(dest, upward, downward):
    return choose((lax.axis_index("quad") + 1 == dest).astype(jnp.int32), upward, downward)


def begin(ready, rs, ph, gain, sub, fac, cou, mob, core, near, rs_out, sub_out, fac_out, cou_out, pay, rows):
    odd = parity()
    ready(0, 3)
    cin = restrict(sub, rs, rows)
    rs_out[...] = rs[...]
    sub_out[...] = sub[...] + 1
    ready(1, 2, 4, 5)
    fac_out[...] = fac[...]
    cou_out[...] = pack(choose(odd, cou[...], cou[...].T))
    ms, ss = [], []
    for z in range(4):
        m = 1.0 / (gain[z] * (0.001 + 0.999 * ph[z].astype(F32)))
        mob[z] = m
        ms.append(m)
        ss.append((sub[z] + 1).astype(F32))
    spread(core, 0, choose(odd, ms[0], ms[3]))
    spread(core, 128, choose(odd, ss[0], ss[3]))
    spread(near, 0, choose(odd, ms[3], ms[0]))
    spread(near, 128, choose(odd, ss[3], ss[0]))
    for part in (core, near):
        part[256:320, :] = fac[:, :128]
        part[320:384, :] = fac[:, 128:]
    upward = jnp.concatenate([m[15:16, :] for m in ms] + [s[15:16, :] for s in ss], axis=0)
    downward = jnp.concatenate([m[0:1, :] for m in ms] + [s[0:1, :] for s in ss], axis=0)
    both = jnp.concatenate([cin, cin], axis=1)
    lane = lane_of((64, 128))
    row = lax.broadcasted_iota(jnp.int32, (64, 128), 0)
    tail = jnp.where(row == 0, both, 0.0)
    for q in range(4):
        block = fac[:, (q // 2) * 128 : (q // 2 + 1) * 128]
        if q % 2:
            block = pltpu.roll(block, 64, 1)
        pay[q, 0:64, :] = jnp.where(lane < 64, block, tail)
        spread(pay.at[q], 64, face_for(q, upward, downward))


def send_faces(out, to_core, to_near, ups, downs):
    odd = parity()
    to_core[...] = choose(odd, out[0], out[3])
    to_near[...] = choose(odd, out[3], out[0])
    for z in range(4):
        ups[z : z + 1, :] = out[z][15:16, :]
        downs[z : z + 1, :] = out[z][0:1, :]


def share(ready, got, fac, cou, cols, pay):
    low = lane_of((64, 128)) < 64
    for h in range(2):
        cols[h] = jnp.where(low, got[2 * h, 0:64, :], pltpu.roll(got[2 * h + 1, 0:64, :], 64, 1))
    cins = [pltpu.roll(got[q, 0:8, :], 64, 1)[0:1, :64] for q in range(4)]
    cin = jnp.concatenate(cins, axis=1)
    rhs = lax.dot_general(
        jnp.broadcast_to(cin, (8, 256)), fac[...], (((1,), (1,)), ((), ())), precision=HIGH, preferred_element_type=F32
    )
    pay[0:32, :] = cou[...]
    pay[32:40, :] = jnp.concatenate([rhs, rhs], axis=1)


def setup(
    ready, rs, mob, core, near, got, kz, ky, kyt, kx, kxe, inv, to_core, to_near, ups, downs, zsub, ysub, beside
):
    odd = parity()
    quad = lax.axis_index("quad")
    planes = [mob[z] for z in range(4)]
    c_mob, n_mob = gather_rows(core, 0, 16), gather_rows(near, 0, 16)
    c_sub, n_sub = gather_rows(core, 128, 16), gather_rows(near, 128, 16)
    below = [choose(odd, c_mob, n_mob)] + planes[:3]
    above = planes[1:] + [choose(odd, n_mob, c_mob)]
    zsub[0] = choose(odd, c_sub, n_sub).astype(jnp.int32)
    zsub[1] = choose(odd, n_sub, c_sub).astype(jnp.int32)
    c_fac = jnp.concatenate([core[256:320, :], core[320:384, :]], axis=1)
    n_fac = jnp.concatenate([near[256:320, :], near[320:384, :]], axis=1)
    beside[0] = choose(odd, c_fac, n_fac)
    beside[1] = choose(odd, n_fac, c_fac)
    before = gather_rows(got[jnp.maximum(quad - 1, 0)], 64, 8)
    after = gather_rows(got[jnp.minimum(quad + 1, 3)], 64, 8)
    ylo = jnp.where(jnp.broadcast_to(quad, before.shape) > 0, before, 0.0)
    yhi = jnp.where(jnp.broadcast_to(quad, after.shape) < 3, after, 0.0)
    ysub[...] = jnp.concatenate([ylo[4:8, :], yhi[4:8, :]], axis=0).astype(jnp.int32)
    faces = [harmonic(planes[z], below[z]) for z in range(4)]
    faces.append(harmonic(planes[3], above[3]))
    for z in range(5):
        kz[z] = faces[z]
    diags = []
    for z in range(4):
        m = planes[z]
        a = harmonic(m, y_before(m, ylo[z : z + 1, :]))
        b = harmonic(m, y_after(m, yhi[z : z + 1, :]))
        c = harmonic(m, x_before(m))
        d = harmonic(m, x_after(m))
        ky[z] = a
        kyt[z : z + 1, :] = b[15:16, :]
        kx[z] = c
        kxe[z] = jnp.where(lane_of((16, 128)) == 127, d[:, 896:], 0.0)
        diags.append(faces[z] + faces[z + 1] + a + b + c + d)
    invs = [1.0 / diags[0]]
    for j in range(1, 4):
        invs.append(1.0 / (diags[j] - faces[j] * faces[j] * invs[j - 1]))
    for j in range(4):
        inv[j] = invs[j]
    ready(0)
    out = solve_lines(faces, invs, [rs[z] for z in range(4)])
    send_faces(out, to_core, to_near, ups, downs)


def unpack(packed):
    low = lane_of((32, 128)) < 64
    return jnp.concatenate([jnp.where(low, packed, 0.0), jnp.where(low, pltpu.roll(packed, 64, 1), 0.0)], axis=0)


def pack(mat):
    return jnp.concatenate([mat[:32, :64], mat[32:, :64]], axis=1)


def across(mat, row):
    return jnp.broadcast_to(jnp.sum(mat * row, axis=1, keepdims=True), (64, 128))


def down(mat, col):
    return jnp.sum(mat * col, axis=0, keepdims=True)


def as_col(rows_t, k):
    return jnp.broadcast_to(rows_t[:64, k : k + 1], (64, 128))


def condense(mats, rhs):
    rows_t = rhs.T
    held = {}
    col = as_col(rows_t, 1)
    held[1] = col
    row = None
    for k in range(2, GROUP):
        if k % 2:
            col = across(mats[k], row) + as_col(rows_t, k)
            held[k] = col
        else:
            row = down(mats[k], col) + rhs[k : k + 1, :]
            held[k] = row
    end = col
    for k in range(GROUP - 1, 0, -1):
        if k % 2:
            row = down(mats[k], col)
            if k > 1:
                row = row + held[k - 1]
        else:
            col = across(mats[k], row) + held[k - 1]
    return jnp.concatenate([end.T[0:1, :], jnp.zeros((1, 64), F32)], axis=1), row


def of_slab(own, other, k, rows):
    at_even, at_odd = (other, own) if k % 2 else (own, other)
    return choose(parity(), at_odd[k // 2, rows, :], at_even[k // 2, rows, :])


def local_mats(own, other):
    return [unpack(of_slab(own, other, k, slice(0, 32))) for k in range(GROUP)]


def condense_first(ready, own, other, out, rhs_out, tall):
    rows = [of_slab(own, other, k, slice(32, 33)) for k in range(GROUP)]
    rhs = jnp.where(lane_of((GROUP, 128)) < 64, jnp.concatenate(rows, axis=0), 0.0)
    rhs_out[...] = rhs
    mats = local_mats(own, other)
    eye = lax.broadcasted_iota(jnp.int32, (64, 64), 0) == lax.broadcasted_iota(jnp.int32, (64, 64), 1)
    one = jnp.where(eye, 1.0, 0.0)
    runs = [[mats[b][:, :64] if b else one] for b in range(0, GROUP, 4)]
    for k in range(1, 4):
        for b, run in enumerate(runs):
            mat = mats[4 * b + k][:, :64]
            dims = (((1,), (1 if k % 2 else 0,)), ((), ()))
            run.append(lax.dot_general(run[-1], mat, dims, precision=HIGH, preferred_element_type=F32))
    psi = one * SCALE
    for b, run in enumerate(runs):
        wide = jnp.concatenate(run, axis=1)
        wide = wide * SCALE if b == 0 else jnp.dot(psi, wide, precision=HIGH, preferred_element_type=F32)
        tall[:, b * 256 : (b + 1) * 256] = wide
        psi = wide[:, 192:]
    gram = lax.dot_general(
        tall[...], tall[...], (((1,), (1,)), ((), ())), precision=HIGH, preferred_element_type=F32
    )
    end, start = condense(mats, rhs)
    out[0:32, :] = pack(psi.T * (1.0 / SCALE))
    out[32:64, :] = of_slab(own, other, 0, slice(0, 32))
    out[64:96, :] = pack(gram)
    out[96:104, :] = jnp.concatenate([end, start, rhs[0:1, :], jnp.zeros((5, 128), F32)], axis=0)


def condense_second(ready, got, own, other, out, rhs_out):
    mats = local_mats(own, other)
    total = got[pl.ds(0, GROUP, 4), :]
    for q in range(1, 4):
        total = total + got[pl.ds(q, GROUP, 4), :]
    rhs = jnp.where(lane_of((GROUP, 128)) < 64, total, 0.0)
    rhs_out[...] = rhs
    end, start = condense(mats, rhs)
    dots = jnp.sum(total, axis=0, keepdims=True)
    out[...] = jnp.concatenate([end, start, rhs[0:1, :], dots, jnp.zeros((4, 128), F32)], axis=0)


def chain(ready, bounds, vecs, mats, rhs, fac, beside, ups, downs, out, ys, vs, wb, ws, wc):
    slab = lax.axis_index("slab")
    group, place = slab // GROUP, slab % GROUP
    groups = 4
    psi = [unpack(bounds[g, 0:32, :]) for g in range(groups)]
    lead = [unpack(bounds[g, 32:64, :]) for g in range(groups)]
    ends_t = jnp.concatenate([v[0:1, :] for v in vecs] + [jnp.zeros((4, 128), F32)], axis=0).T
    ends = [as_col(ends_t, g) for g in range(groups)]
    starts = []
    lasts = []
    for g in range(groups):
        begins = jnp.where(lane_of((1, 128)) < 64, vecs[g][2:3, :], 0.0)
        if g:
            begins = begins + down(lead[g], lasts[g - 1])
        starts.append(begins)
        ys[g : g + 1, :] = begins
        lasts.append(across(psi[g], begins) + ends[g])
    grown = []
    for g in range(groups):
        packed = bounds[g, 64:96, :]
        gram = jnp.concatenate([packed[:, :64], packed[:, 64:]], axis=0)
        part = jnp.dot(
            jnp.broadcast_to(starts[g][:, :64], (8, 64)), gram, precision=HIGH, preferred_element_type=F32
        )[0:1, :]
        part = part * (1.0 / SCALE) * (1.0 / SCALE)
        grown.append(jnp.concatenate([part, jnp.zeros((1, 64), F32)], axis=1) + vecs[g][1:2, :])
    vs[...] = jnp.zeros((8, 128), F32)
    wb[0] = jnp.zeros((64, 128), F32)
    wb[groups] = lasts[groups - 1]
    head = grown[groups - 1]
    vs[groups - 1 : groups, :] = head
    for g in range(groups - 2, -1, -1):
        back = across(lead[g + 1], head)
        wb[g + 1] = lasts[g] + back
        head = grown[g] + down(psi[g], back)
        vs[g : g + 1, :] = head
    rows_t = rhs[...].T
    row = ys[pl.ds(group, 1), :]
    held = {0: row}
    col = None
    for k in range(1, GROUP):
        if k % 2:
            col = across(mats[k], row) + as_col(rows_t, k)
            held[k] = col
        else:
            row = down(mats[k], col) + rhs[k : k + 1, :]
            held[k] = row
    wc[0] = wb[group]
    col = wb[group + 1]
    wc[GROUP] = col
    ws[GROUP + 1 : GROUP + 2, :] = vs[pl.ds(group + 1, 1), :]
    for k in range(GROUP - 1, 0, -1):
        if k % 2:
            row = down(mats[k], col) + held[k - 1]
            ws[k : k + 1, :] = row
        else:
            col = across(mats[k], row) + held[k - 1]
            wc[k] = col
    ready(*range(len(vecs) + 10))
    shares = ((0, fac[...]), (-1, beside[0]), (1, beside[1]))
    for j, (shift, table) in enumerate(shares):
        at = place + shift + 1
        from_row = ws[pl.ds(at, 1), :]
        from_col = wc[at].T[0:1, :]
        is_row = jnp.broadcast_to(at % 2, (1, 64)) == 1
        w = jnp.where(is_row, from_row[:, :64], from_col[:, :64])
        part = jnp.dot(jnp.broadcast_to(w, (8, 64)), table, precision=HIGH, preferred_element_type=F32)
        for q in range(4):
            out[q, 2 * j : 2 * j + 1, :] = part[0:1, :128]
            out[q, 2 * j + 1 : 2 * j + 2, :] = part[0:1, 128:]
    for q in range(4):
        out[q, 6:8, :] = jnp.zeros((2, 128), F32)
        spread(out.at[q], 8, face_for(q, ups[...], downs[...]))


def chain_first(ready, bounds, own, other, rhs, fac, beside, ups, downs, out, *work):
    mats = local_mats(own, other)
    vecs = [bounds[g, 96:104, :] for g in range(4)]
    chain(ready, bounds, vecs, mats, rhs, fac, beside, ups, downs, out, *work)


def chain_second(ready, bounds, got, own, other, rhs, fac, beside, ups, downs, out, dots, *work):
    mats = local_mats(own, other)
    vecs = [got[g] for g in range(4)]
    total = vecs[0][3:4, :] + vecs[1][3:4, :] + vecs[2][3:4, :] + vecs[3][3:4, :]
    dots[...] = jnp.broadcast_to(total, (8, 128))
    chain(ready, bounds, vecs, mats, rhs, fac, beside, ups, downs, out, *work)


def tables(got):
    quad = lax.axis_index("quad")
    total = got[0, 0:8, :] + got[1, 0:8, :] + got[2, 0:8, :] + got[3, 0:8, :]
    near = pltpu.roll(total, 1, 1)
    far = pltpu.roll(total, 65, 1)
    lane = lane_of((1, 128))
    valid = (lane >= 1) & (lane <= 64)

    def table(base, q):
        first = jnp.where(jnp.broadcast_to(q % 2, (1, 128)) == 1, far[base : base + 1, :], near[base : base + 1, :])
        second = jnp.where(
            jnp.broadcast_to(q % 2, (1, 128)) == 1, far[base + 1 : base + 2, :], near[base + 1 : base + 2, :]
        )
        picked = jnp.where(jnp.broadcast_to(q, (1, 128)) >= 2, second, first)
        return jnp.where(valid, picked, 0.0)

    return (
        table(0, quad),
        table(0, jnp.maximum(quad - 1, 0)),
        table(0, jnp.minimum(quad + 1, 3)),
        table(2, quad),
        table(4, quad),
    )


def apply(got, field, core, near, sub, zsub, ysub, kz, ky, kyt, kx, kxe, inv):
    odd = parity()
    quad = lax.axis_index("quad")
    own, t_yl, t_yh, t_zl, t_zh = tables(got)
    bj = solve_lines([kz[z] for z in range(5)], [inv[z] for z in range(4)], [field[z] for z in range(4)])
    planes = [bj[z] + look_up(own, sub[z]) for z in range(4)]
    below = choose(odd, core[...], near[...]) + look_up(t_zl, zsub[0])
    above = choose(odd, near[...], core[...]) + look_up(t_zh, zsub[1])
    before = gather_rows(got[jnp.maximum(quad - 1, 0)], 8, 4)
    after = gather_rows(got[jnp.minimum(quad + 1, 3)], 8, 4)
    before = jnp.where(jnp.broadcast_to(quad, before.shape) > 0, before, 0.0) + look_up(t_yl, ysub[...])[0:4, :]
    after = jnp.where(jnp.broadcast_to(quad, after.shape) < 3, after, 0.0) + look_up(t_yh, ysub[...])[4:8, :]
    line = [below] + planes + [above]
    rise = [kz[j] * (line[j + 1] - line[j]) for j in range(5)]
    images = []
    for z in range(4):
        v = planes[z]
        y_low = ky[z] * (v - y_before(v, before[z : z + 1, :]))
        y_high = y_after(y_low, kyt[z : z + 1, :] * (after[z : z + 1, :] - v[15:16, :]))
        x_low = kx[z] * (v - x_before(v))
        x_high = x_after(x_low)
        x_high = jnp.concatenate([x_high[:, :896], x_high[:, 896:] - kxe[z] * v[:, 896:]], axis=1)
        images.append((rise[z] - rise[z + 1]) + (y_low - y_high) + (x_low - x_high))
    return planes, images


def total_of(lefts, rights):
    acc = lefts[0] * rights[0]
    for a, b in zip(lefts[1:], rights[1:]):
        acc = acc + a * b
    return jnp.sum(jnp.sum(acc, axis=0, keepdims=True), axis=1, keepdims=True)


def first(
    ready, got, core, near, sub, zsub, ysub, kz, ky, kyt, kx, kxe, inv, rs, cols,
    z_out, q_out, to_core, to_near, ups, downs, pay, rows,
):
    ready(4)
    planes, images = apply(got, rs, core, near, sub, zsub, ysub, kz, ky, kyt, kx, kxe, inv)
    for z in range(4):
        z_out[z] = planes[z]
        q_out[z] = images[z]
    send_faces(
        solve_lines([kz[z] for z in range(5)], [inv[z] for z in range(4)], images), to_core, to_near, ups, downs
    )
    cin = jnp.broadcast_to(restrict(sub, q_out, rows, 1), (8, 64))
    ready(12)
    rz = total_of([rs[z] for z in range(4)], planes)
    pq = total_of(planes, images)
    lane = lane_of((1, 128))
    parts = []
    for q in range(4):
        part = lax.dot_general(
            cin, cols[q // 2][:, q % 2 * 64 : q % 2 * 64 + 64], (((1,), (1,)), ((), ())), precision=HIGH, preferred_element_type=F32
        )[0:1, :]
        part = jnp.concatenate([part, part], axis=1)
        parts.append(jnp.where(lane < 64, part, jnp.where(lane == 64, rz, jnp.where(lane == 65, pq, 0.0))))
    pay[...] = jnp.concatenate(parts + parts, axis=0)


def second(
    ready, got, core, near, sub, zsub, ysub, kz, ky, kyt, kx, kxe, inv, rs, z0, q0, dots,
    z_out, g_out, r_out, pay,
):
    ready(4)
    planes, images = apply(got, q0, core, near, sub, zsub, ysub, kz, ky, kyt, kx, kxe, inv)
    alpha = dots[0:1, 64:65] / dots[0:1, 65:66]
    ready(12)
    zs, gs, rr = [], [], []
    for z in range(4):
        rr.append(rs[z] - alpha * q0[z])
        zs.append(z0[z] - alpha * planes[z])
        gs.append(q0[z] - alpha * images[z])
        z_out[z] = zs[z]
        g_out[z] = gs[z]
        r_out[z] = rr[z]
    new = total_of(rr, zs)
    own = total_of(zs, gs)
    cross = total_of([z0[z] for z in range(4)], gs)
    lane = lane_of((8, 128))
    pay[...] = jnp.where(lane == 0, new, jnp.where(lane == 1, own, jnp.where(lane == 2, cross, 0.0)))


def last(ready, got, dots, z0, q0, z1, g1, r1, x_out, r_out):
    total = jnp.sum(got[...], axis=0, keepdims=True)
    new, own, cross = total[:, 0:1], total[:, 1:2], total[:, 2:3]
    rz, pq = dots[0:1, 64:65], dots[0:1, 65:66]
    alpha = rz / pq
    beta = new / rz
    step = new / (own + 2.0 * beta * cross + beta * beta * pq)
    for z in range(4):
        x_out[z] = alpha * z0[z] + step * (z1[z] + beta * z0[z])
        r_out[z] = r1[z] - step * (g1[z] + beta * q0[z])


def body(right_side, phase_label, density_gain, subdomain, block_factor, coupling):
    slabs = lax.axis_size("slab")
    fac, cou = block_factor[0], coupling[0]
    grid, plane, edge = sds(4, 16, 1024), sds(16, 1024), sds(4, 1024)
    quads = lax.axis_size("quad")
    within = [list(range(g + c, g + GROUP, 2)) for g in range(0, slabs, GROUP) for c in range(2)]
    planes = [list(range(g, g + GROUP * quads)) for g in range(0, slabs * quads, GROUP * quads)]
    between = [list(range(i, slabs, GROUP)) for i in range(GROUP)]
    with_core = [(i, i ^ 1) for i in range(slabs)]
    with_near = [(i, i + 1 if i % 2 else i - 1) for i in range(1, slabs - 1)]

    def exchange(value, axis, groups=None):
        return lax.all_to_all(value, axis, 0, 0, tiled=True, axis_index_groups=groups)

    def swap(to_core, to_near):
        return lax.ppermute(to_core, "slab", with_core), lax.ppermute(to_near, "slab", with_near)

    mob, core, near, rs, sub, fac, cou, pay = call(
        begin,
        (grid, sds(384, 128), sds(384, 128), grid, jax.ShapeDtypeStruct((4, 16, 1024), jnp.int32))
        + (sds(64, 256), sds(32, 128), sds(4, 128, 128)),
        [pltpu.VMEM((64, 128), F32)],
        (3, 0, 1, 2, 4, 5),
        (-8,),
    )(right_side, phase_label, density_gain, subdomain, fac, cou)
    core, near = swap(core, near)
    got = exchange(pay, "quad")
    cols, pay = call(share, (sds(2, 64, 128), sds(GROUP // 2, 40, 128)), (), (), (1,))(got, fac, cou)
    pay, core, near = lax.optimization_barrier((pay, core, near))
    own = exchange(pay, "slab", within)
    kz, ky, kyt, kx, kxe, inv, to_core, to_near, ups, downs, zsub, ysub, beside = call(
        setup,
        (sds(5, 16, 1024), grid, edge, grid, sds(4, 16, 128), grid, plane, plane, edge, edge)
        + (jax.ShapeDtypeStruct((2, 16, 1024), jnp.int32), jax.ShapeDtypeStruct((8, 1024), jnp.int32), sds(2, 64, 256)),
        (),
        (),
        (-9, -10),
    )(rs, mob, core, near, got)
    own, to_core, to_near = lax.optimization_barrier((own, to_core, to_near))
    other = lax.ppermute(own, "slab", with_core)
    pay, rhs = call(
        condense_first,
        (sds(4, 104, 128), sds(GROUP, 128)),
        [pltpu.VMEM((64, GROUP * 64), F32)],
        (),
        (0,),
    )(own, other)
    pay, to_core, to_near = lax.optimization_barrier((pay, to_core, to_near))
    bj_core, bj_near = swap(to_core, to_near)
    bounds = exchange(pay, "slab", between)
    bounds, bj_core, bj_near = lax.optimization_barrier((bounds, bj_core, bj_near))
    work = [
        pltpu.VMEM((8, 128), F32),
        pltpu.VMEM((8, 128), F32),
        pltpu.VMEM((5, 64, 128), F32),
        pltpu.VMEM((GROUP + 8, 128), F32),
        pltpu.VMEM((GROUP + 2, 64, 128), F32),
    ]
    part = call(chain_first, sds(4, 40, 128), work, (6, 7), (-1,))(
        bounds, own, other, rhs, fac, beside, ups, downs
    )
    coarse = exchange(part, "quad")
    stencil = (sub, zsub, ysub, kz, ky, kyt, kx, kxe, inv, rs)
    z0, q0, to_core, to_near, ups, downs, pay = call(
        first,
        (grid, grid, plane, plane, edge, edge, sds(8, 8, 128)),
        [pltpu.VMEM((64, 128), F32)],
        (),
        (-5, -6, 6),
    )(coarse, bj_core, bj_near, *stencil, cols)
    plane_rows = exchange(pay.reshape(64, 1, 128), BOTH, planes).reshape(64, 128)
    bj_core, bj_near = swap(to_core, to_near)
    pay, rhs = call(condense_second, (sds(4, 8, 128), sds(GROUP, 128)), (), (), (0,))(plane_rows, own, other)
    vecs = exchange(pay, "slab", between)
    part, dots = call(chain_second, (sds(4, 40, 128), sds(8, 128)), work, (7, 8), (-1,))(
        bounds, vecs, own, other, rhs, fac, beside, ups, downs
    )
    coarse = exchange(part, "quad")
    z1, g1, r1, pay = call(second, (grid, grid, grid, sds(32, 8, 128)), (), (), (3,))(
        coarse, bj_core, bj_near, *stencil, z0, q0, dots
    )
    everyone = exchange(pay.reshape(256, 1, 128), BOTH).reshape(256, 128)
    return tuple(call(last, (grid, grid))(everyone, dots, z0, q0, z1, g1, r1))


def solution(mesh):
    spec = P("slab", "quad", None)
    return jax.shard_map(body, mesh=mesh, in_specs=(spec,) * 6, out_specs=(spec, spec), check_vma=False)
```

```python
import jax
import jax.numpy as jnp
from jax import lax
from jax.experimental import pallas as pl
from jax.experimental.pallas import tpu as pltpu
from jax.sharding import PartitionSpec as P

F32 = jnp.float32
HIGH = lax.Precision.HIGHEST
BOTH = ("slab", "quad")
PIECES = 4
GROUP = 16
SCALE = 2.0**-30


def sds(*shape):
    return jax.ShapeDtypeStruct(shape, F32)


def call(kernel, outs, scratch=(), far=(), spread_out=()):
    single = not isinstance(outs, tuple)
    shapes = (outs,) if single else outs
    whole = [-1 - i for i in spread_out if i < 0]
    copied = [i for i in spread_out if i >= 0]
    vmem, hbm = pl.BlockSpec(memory_space=pltpu.VMEM), pl.BlockSpec(memory_space=pltpu.HBM)

    def run(*args):
        count = len(args)
        extra = [pltpu.VMEM(args[i].shape, args[i].dtype) for i in far]
        extra += [pltpu.VMEM(shapes[i].shape, F32) for i in whole]
        extra += [pltpu.VMEM(shapes[i].shape[1:], F32) for i in copied]
        pieces_of = {i: PIECES if len(args[i].shape) == 3 and args[i].shape[0] % 8 == 0 else 1 for i in far}
        copies = sum(pieces_of.values()) + len(whole) + sum(shapes[i].shape[0] for i in copied)
        if copies:
            extra.append(pltpu.SemaphoreType.DMA((copies,)))

        def wrapped(*refs):
            ins, made = list(refs[:count]), list(refs[count : count + len(shapes)])
            rest = list(refs[count + len(shapes) : count + len(shapes) + len(scratch)])
            more = list(refs[count + len(shapes) + len(scratch) :])
            sems = more.pop() if copies else None
            coming, at = {}, 0
            for n, i in enumerate(far):
                size = ins[i].shape[0] // pieces_of[i]
                coming[i] = []
                for p in range(pieces_of[i]):
                    src, dst = ins[i], more[n]
                    if pieces_of[i] > 1:
                        src, dst = src.at[pl.ds(p * size, size)], dst.at[pl.ds(p * size, size)]
                    coming[i].append(pltpu.make_async_copy(src, dst, sems.at[at]))
                    coming[i][p].start()
                    at += 1
                ins[i] = more[n]
            targets = {}
            for n, i in enumerate(whole + copied):
                targets[i] = made[i]
                made[i] = more[len(far) + n]
            waited = set()

            def ready(*which, pieces=range(PIECES)):
                for i in which:
                    for p in pieces:
                        if i in coming and p < pieces_of[i] and (i, p) not in waited:
                            waited.add((i, p))
                            coming[i][p].wait()

            kernel(ready, *ins, *made, *rest)
            ready(*far)
            at = sum(pieces_of.values())
            going = []
            for i in whole:
                going.append(pltpu.make_async_copy(made[i], targets[i], sems.at[at]))
                at += 1
            for i in copied:
                for m in range(shapes[i].shape[0]):
                    going.append(pltpu.make_async_copy(made[i], targets[i].at[m], sems.at[at]))
                    at += 1
            for copy in going:
                copy.start()
            for copy in going:
                copy.wait()

        out = pl.pallas_call(
            wrapped,
            in_specs=[hbm if i in far else vmem for i in range(count)],
            out_specs=tuple(hbm if i in whole + copied else vmem for i in range(len(shapes))),
            out_shape=tuple(pltpu.HBM(s.shape, s.dtype) if i in whole + copied else s for i, s in enumerate(shapes)),
            scratch_shapes=list(scratch) + extra,
            compiler_params=pltpu.CompilerParams(vmem_limit_bytes=16 << 20),
            name=kernel.__name__,
        )(*[pltpu.with_memory_space_constraint(a, pltpu.HBM) if i in far else a for i, a in enumerate(args)])
        return out[0] if single else out

    return run


def harmonic(here, there):
    return jnp.where(there > 0, 2.0 * here * there / (here + there), here)


def x_before(plane):
    lane = lax.broadcasted_iota(jnp.int32, plane.shape, 1)
    return jnp.where(lane == 0, 0.0, pltpu.roll(plane, 1, 1))


def x_after(plane):
    width = plane.shape[1]
    lane = lax.broadcasted_iota(jnp.int32, plane.shape, 1)
    return jnp.where(lane == width - 1, 0.0, pltpu.roll(plane, width - 1, 1))


def y_before(plane, halo):
    row = lax.broadcasted_iota(jnp.int32, plane.shape, 0)
    return jnp.where(row == 0, halo, pltpu.roll(plane, 1, 0))


def y_after(plane, halo):
    height = plane.shape[0]
    row = lax.broadcasted_iota(jnp.int32, plane.shape, 0)
    return jnp.where(row == height - 1, halo, pltpu.roll(plane, height - 1, 0))


def lane_of(shape):
    return lax.broadcasted_iota(jnp.int32, shape, len(shape) - 1)


def restrict(sub_ref, field_ref, rows_ref, least=0):
    for base in range(0, 64, 16):

        def tile(t, totals):
            at = t // 2
            rows = pl.ds(pl.multiple_of((at % 2) * 8, 8), 8)
            lanes = pl.ds(pl.multiple_of((t % 2) * 512, 512), 512)
            sub = sub_ref[at // 2, rows, lanes]
            field = field_ref[at // 2, rows, lanes]
            out = []
            for label in range(16):
                picked = jnp.where(sub == base + label + least, field, 0.0)
                parts = [picked[:, j * 128 : (j + 1) * 128] for j in range(4)]
                out.append(totals[label] + ((parts[0] + parts[1]) + (parts[2] + parts[3])))
            return tuple(out)

        totals = lax.fori_loop(0, 16, tile, tuple(jnp.zeros((8, 128), F32) for _ in range(16)), unroll=4)
        for half in range(0, 16, 8):
            sums = [jnp.sum(t, axis=0, keepdims=True) for t in totals[half : half + 8]]
            rows_ref[base + half : base + half + 8, :] = jnp.concatenate(sums, axis=0)
    return jnp.sum(rows_ref[...].T, axis=0, keepdims=True)


def look_up(table, index):
    wide = jnp.broadcast_to(table, (8, 128))
    rows = []
    for r in range(index.shape[0] // 8):
        parts = []
        for c in range(index.shape[1] // 128):
            part = index[r * 8 : (r + 1) * 8, c * 128 : (c + 1) * 128]
            parts.append(jnp.take_along_axis(wide, part, axis=1, mode="promise_in_bounds"))
        rows.append(jnp.concatenate(parts, axis=1))
    return jnp.concatenate(rows, axis=0)


def solve_lines(kz, inv, rhs):
    rho = [rhs[0] * inv[0]]
    for j in range(1, 4):
        rho.append((rhs[j] + kz[j] * rho[j - 1]) * inv[j])
    out = [None] * 4
    out[3] = rho[3]
    for j in (2, 1, 0):
        out[j] = rho[j] + kz[j + 1] * inv[j] * out[j + 1]
    return out


def parity():
    return lax.axis_index("slab") % 2


def choose(flag, a, b):
    return jnp.where(jnp.broadcast_to(flag, a.shape) == 1, a, b)


def spread(out, at, plane):
    h = plane.shape[0]
    for c in range(8):
        out[at + c * h : at + (c + 1) * h, :] = plane[:, c * 128 : (c + 1) * 128]


def gather_rows(block, at, h):
    return jnp.concatenate([block[at + c * h : at + (c + 1) * h, :] for c in range(8)], axis=1)


def face_for(dest, upward, downward):
    return choose((lax.axis_index("quad") + 1 == dest).astype(jnp.int32), upward, downward)


def begin(ready, rs, ph, gain, sub, fac, cou, mob, core, near, rs_out, sub_out, fac_out, cou_out, pay, rows):
    odd = parity()
    ready(0, 3)
    cin = restrict(sub, rs, rows)
    rs_out[...] = rs[...]
    sub_out[...] = sub[...] + 1
    ready(1, 2, 4, 5)
    fac_out[...] = fac[...]
    cou_out[...] = pack(choose(odd, cou[...], cou[...].T))
    ms, ss = [], []
    for z in range(4):
        m = 1.0 / (gain[z] * (0.001 + 0.999 * ph[z].astype(F32)))
        mob[z] = m
        ms.append(m)
        ss.append((sub[z] + 1).astype(F32))
    spread(core, 0, choose(odd, ms[0], ms[3]))
    spread(core, 128, choose(odd, ss[0], ss[3]))
    spread(near, 0, choose(odd, ms[3], ms[0]))
    spread(near, 128, choose(odd, ss[3], ss[0]))
    for part in (core, near):
        part[256:320, :] = fac[:, :128]
        part[320:384, :] = fac[:, 128:]
    upward = jnp.concatenate([m[15:16, :] for m in ms] + [s[15:16, :] for s in ss], axis=0)
    downward = jnp.concatenate([m[0:1, :] for m in ms] + [s[0:1, :] for s in ss], axis=0)
    both = jnp.concatenate([cin, cin], axis=1)
    lane = lane_of((64, 128))
    row = lax.broadcasted_iota(jnp.int32, (64, 128), 0)
    tail = jnp.where(row == 0, both, 0.0)
    for q in range(4):
        block = fac[:, (q // 2) * 128 : (q // 2 + 1) * 128]
        if q % 2:
            block = pltpu.roll(block, 64, 1)
        pay[q, 0:64, :] = jnp.where(lane < 64, block, tail)
        spread(pay.at[q], 64, face_for(q, upward, downward))


def send_faces(out, to_core, to_near, ups, downs):
    odd = parity()
    to_core[...] = choose(odd, out[0], out[3])
    to_near[...] = choose(odd, out[3], out[0])
    for z in range(4):
        ups[z : z + 1, :] = out[z][15:16, :]
        downs[z : z + 1, :] = out[z][0:1, :]


def share(ready, got, fac, cou, cols, pay):
    low = lane_of((64, 128)) < 64
    for h in range(2):
        cols[h] = jnp.where(low, got[2 * h, 0:64, :], pltpu.roll(got[2 * h + 1, 0:64, :], 64, 1))
    cins = [pltpu.roll(got[q, 0:8, :], 64, 1)[0:1, :64] for q in range(4)]
    cin = jnp.concatenate(cins, axis=1)
    rhs = lax.dot_general(
        jnp.broadcast_to(cin, (8, 256)), fac[...], (((1,), (1,)), ((), ())), precision=HIGH, preferred_element_type=F32
    )
    pay[0:32, :] = cou[...]
    pay[32:40, :] = jnp.concatenate([rhs, rhs], axis=1)


def setup(
    ready, rs, mob, core, near, got, kz, ky, kyt, kx, kxe, inv, to_core, to_near, ups, downs, zsub, ysub, beside
):
    odd = parity()
    quad = lax.axis_index("quad")
    planes = [mob[z] for z in range(4)]
    c_mob, n_mob = gather_rows(core, 0, 16), gather_rows(near, 0, 16)
    c_sub, n_sub = gather_rows(core, 128, 16), gather_rows(near, 128, 16)
    below = [choose(odd, c_mob, n_mob)] + planes[:3]
    above = planes[1:] + [choose(odd, n_mob, c_mob)]
    zsub[0] = choose(odd, c_sub, n_sub).astype(jnp.int32)
    zsub[1] = choose(odd, n_sub, c_sub).astype(jnp.int32)
    c_fac = jnp.concatenate([core[256:320, :], core[320:384, :]], axis=1)
    n_fac = jnp.concatenate([near[256:320, :], near[320:384, :]], axis=1)
    beside[0] = choose(odd, c_fac, n_fac)
    beside[1] = choose(odd, n_fac, c_fac)
    before = gather_rows(got[jnp.maximum(quad - 1, 0)], 64, 8)
    after = gather_rows(got[jnp.minimum(quad + 1, 3)], 64, 8)
    ylo = jnp.where(jnp.broadcast_to(quad, before.shape) > 0, before, 0.0)
    yhi = jnp.where(jnp.broadcast_to(quad, after.shape) < 3, after, 0.0)
    ysub[...] = jnp.concatenate([ylo[4:8, :], yhi[4:8, :]], axis=0).astype(jnp.int32)
    faces = [harmonic(planes[z], below[z]) for z in range(4)]
    faces.append(harmonic(planes[3], above[3]))
    for z in range(5):
        kz[z] = faces[z]
    diags = []
    for z in range(4):
        m = planes[z]
        a = harmonic(m, y_before(m, ylo[z : z + 1, :]))
        b = harmonic(m, y_after(m, yhi[z : z + 1, :]))
        c = harmonic(m, x_before(m))
        d = harmonic(m, x_after(m))
        ky[z] = a
        kyt[z : z + 1, :] = b[15:16, :]
        kx[z] = c
        kxe[z] = jnp.where(lane_of((16, 128)) == 127, d[:, 896:], 0.0)
        diags.append(faces[z] + faces[z + 1] + a + b + c + d)
    invs = [1.0 / diags[0]]
    for j in range(1, 4):
        invs.append(1.0 / (diags[j] - faces[j] * faces[j] * invs[j - 1]))
    for j in range(4):
        inv[j] = invs[j]
    ready(0)
    out = solve_lines(faces, invs, [rs[z] for z in range(4)])
    send_faces(out, to_core, to_near, ups, downs)


def unpack(packed):
    low = lane_of((32, 128)) < 64
    return jnp.concatenate([jnp.where(low, packed, 0.0), jnp.where(low, pltpu.roll(packed, 64, 1), 0.0)], axis=0)


def pack(mat):
    return jnp.concatenate([mat[:32, :64], mat[32:, :64]], axis=1)


def across(mat, row):
    return jnp.broadcast_to(jnp.sum(mat * row, axis=1, keepdims=True), (64, 128))


def down(mat, col):
    return jnp.sum(mat * col, axis=0, keepdims=True)


def as_col(rows_t, k):
    return jnp.broadcast_to(rows_t[:64, k : k + 1], (64, 128))


def condense(mats, rhs):
    rows_t = rhs.T
    held = {}
    col = as_col(rows_t, 1)
    held[1] = col
    row = None
    for k in range(2, GROUP):
        if k % 2:
            col = across(mats[k], row) + as_col(rows_t, k)
            held[k] = col
        else:
            row = down(mats[k], col) + rhs[k : k + 1, :]
            held[k] = row
    end = col
    for k in range(GROUP - 1, 0, -1):
        if k % 2:
            row = down(mats[k], col)
            if k > 1:
                row = row + held[k - 1]
        else:
            col = across(mats[k], row) + held[k - 1]
    return jnp.concatenate([end.T[0:1, :], jnp.zeros((1, 64), F32)], axis=1), row


def of_slab(own, other, k, rows):
    at_even, at_odd = (other, own) if k % 2 else (own, other)
    return choose(parity(), at_odd[k // 2, rows, :], at_even[k // 2, rows, :])


def local_mats(own, other):
    return [unpack(of_slab(own, other, k, slice(0, 32))) for k in range(GROUP)]


def condense_first(ready, own, other, out, rhs_out, tall):
    rows = [of_slab(own, other, k, slice(32, 33)) for k in range(GROUP)]
    rhs = jnp.where(lane_of((GROUP, 128)) < 64, jnp.concatenate(rows, axis=0), 0.0)
    rhs_out[...] = rhs
    mats = local_mats(own, other)
    eye = lax.broadcasted_iota(jnp.int32, (64, 64), 0) == lax.broadcasted_iota(jnp.int32, (64, 64), 1)
    one = jnp.where(eye, 1.0, 0.0)
    runs = [[mats[b][:, :64] if b else one] for b in range(0, GROUP, 4)]
    for k in range(1, 4):
        for b, run in enumerate(runs):
            mat = mats[4 * b + k][:, :64]
            dims = (((1,), (1 if k % 2 else 0,)), ((), ()))
            run.append(lax.dot_general(run[-1], mat, dims, precision=HIGH, preferred_element_type=F32))
    psi = one * SCALE
    for b, run in enumerate(runs):
        wide = jnp.concatenate(run, axis=1)
        wide = wide * SCALE if b == 0 else jnp.dot(psi, wide, precision=HIGH, preferred_element_type=F32)
        tall[:, b * 256 : (b + 1) * 256] = wide
        psi = wide[:, 192:]
    gram = lax.dot_general(
        tall[...], tall[...], (((1,), (1,)), ((), ())), precision=HIGH, preferred_element_type=F32
    )
    end, start = condense(mats, rhs)
    out[0:32, :] = pack(psi.T * (1.0 / SCALE))
    out[32:64, :] = of_slab(own, other, 0, slice(0, 32))
    out[64:96, :] = pack(gram)
    out[96:104, :] = jnp.concatenate([end, start, rhs[0:1, :], jnp.zeros((5, 128), F32)], axis=0)


def condense_second(ready, got, own, other, out, rhs_out):
    mats = local_mats(own, other)
    total = got[pl.ds(0, GROUP, 4), :]
    for q in range(1, 4):
        total = total + got[pl.ds(q, GROUP, 4), :]
    rhs = jnp.where(lane_of((GROUP, 128)) < 64, total, 0.0)
    rhs_out[...] = rhs
    end, start = condense(mats, rhs)
    dots = jnp.sum(total, axis=0, keepdims=True)
    out[...] = jnp.concatenate([end, start, rhs[0:1, :], dots, jnp.zeros((4, 128), F32)], axis=0)


def chain(ready, bounds, vecs, mats, rhs, fac, beside, ups, downs, out, ys, vs, wb, ws, wc):
    slab = lax.axis_index("slab")
    group, place = slab // GROUP, slab % GROUP
    groups = 4
    psi = [unpack(bounds[g, 0:32, :]) for g in range(groups)]
    lead = [unpack(bounds[g, 32:64, :]) for g in range(groups)]
    ends_t = jnp.concatenate([v[0:1, :] for v in vecs] + [jnp.zeros((4, 128), F32)], axis=0).T
    ends = [as_col(ends_t, g) for g in range(groups)]
    starts = []
    lasts = []
    for g in range(groups):
        begins = jnp.where(lane_of((1, 128)) < 64, vecs[g][2:3, :], 0.0)
        if g:
            begins = begins + down(lead[g], lasts[g - 1])
        starts.append(begins)
        ys[g : g + 1, :] = begins
        lasts.append(across(psi[g], begins) + ends[g])
    grown = []
    for g in range(groups):
        packed = bounds[g, 64:96, :]
        gram = jnp.concatenate([packed[:, :64], packed[:, 64:]], axis=0)
        part = jnp.dot(
            jnp.broadcast_to(starts[g][:, :64], (8, 64)), gram, precision=HIGH, preferred_element_type=F32
        )[0:1, :]
        part = part * (1.0 / SCALE) * (1.0 / SCALE)
        grown.append(jnp.concatenate([part, jnp.zeros((1, 64), F32)], axis=1) + vecs[g][1:2, :])
    vs[...] = jnp.zeros((8, 128), F32)
    wb[0] = jnp.zeros((64, 128), F32)
    wb[groups] = lasts[groups - 1]
    head = grown[groups - 1]
    vs[groups - 1 : groups, :] = head
    for g in range(groups - 2, -1, -1):
        back = across(lead[g + 1], head)
        wb[g + 1] = lasts[g] + back
        head = grown[g] + down(psi[g], back)
        vs[g : g + 1, :] = head
    rows_t = rhs[...].T
    row = ys[pl.ds(group, 1), :]
    held = {0: row}
    col = None
    for k in range(1, GROUP):
        if k % 2:
            col = across(mats[k], row) + as_col(rows_t, k)
            held[k] = col
        else:
            row = down(mats[k], col) + rhs[k : k + 1, :]
            held[k] = row
    wc[0] = wb[group]
    col = wb[group + 1]
    wc[GROUP] = col
    ws[GROUP + 1 : GROUP + 2, :] = vs[pl.ds(group + 1, 1), :]
    for k in range(GROUP - 1, 0, -1):
        if k % 2:
            row = down(mats[k], col) + held[k - 1]
            ws[k : k + 1, :] = row
        else:
            col = across(mats[k], row) + held[k - 1]
            wc[k] = col
    ready(*range(len(vecs) + 10))
    shares = ((0, fac[...]), (-1, beside[0]), (1, beside[1]))
    for j, (shift, table) in enumerate(shares):
        at = place + shift + 1
        from_row = ws[pl.ds(at, 1), :]
        from_col = wc[at].T[0:1, :]
        is_row = jnp.broadcast_to(at % 2, (1, 64)) == 1
        w = jnp.where(is_row, from_row[:, :64], from_col[:, :64])
        part = jnp.dot(jnp.broadcast_to(w, (8, 64)), table, precision=HIGH, preferred_element_type=F32)
        for q in range(4):
            out[q, 2 * j : 2 * j + 1, :] = part[0:1, :128]
            out[q, 2 * j + 1 : 2 * j + 2, :] = part[0:1, 128:]
    for q in range(4):
        out[q, 6:8, :] = jnp.zeros((2, 128), F32)
        spread(out.at[q], 8, face_for(q, ups[...], downs[...]))


def chain_first(ready, bounds, own, other, rhs, fac, beside, ups, downs, out, *work):
    mats = local_mats(own, other)
    vecs = [bounds[g, 96:104, :] for g in range(4)]
    chain(ready, bounds, vecs, mats, rhs, fac, beside, ups, downs, out, *work)


def chain_second(ready, bounds, got, own, other, rhs, fac, beside, ups, downs, out, dots, *work):
    mats = local_mats(own, other)
    vecs = [got[g] for g in range(4)]
    total = vecs[0][3:4, :] + vecs[1][3:4, :] + vecs[2][3:4, :] + vecs[3][3:4, :]
    dots[...] = jnp.broadcast_to(total, (8, 128))
    chain(ready, bounds, vecs, mats, rhs, fac, beside, ups, downs, out, *work)


def tables(got):
    quad = lax.axis_index("quad")
    total = got[0, 0:8, :] + got[1, 0:8, :] + got[2, 0:8, :] + got[3, 0:8, :]
    near = pltpu.roll(total, 1, 1)
    far = pltpu.roll(total, 65, 1)
    lane = lane_of((1, 128))
    valid = (lane >= 1) & (lane <= 64)

    def table(base, q):
        first = jnp.where(jnp.broadcast_to(q % 2, (1, 128)) == 1, far[base : base + 1, :], near[base : base + 1, :])
        second = jnp.where(
            jnp.broadcast_to(q % 2, (1, 128)) == 1, far[base + 1 : base + 2, :], near[base + 1 : base + 2, :]
        )
        picked = jnp.where(jnp.broadcast_to(q, (1, 128)) >= 2, second, first)
        return jnp.where(valid, picked, 0.0)

    return (
        table(0, quad),
        table(0, jnp.maximum(quad - 1, 0)),
        table(0, jnp.minimum(quad + 1, 3)),
        table(2, quad),
        table(4, quad),
    )


def apply(got, field, core, near, sub, zsub, ysub, kz, ky, kyt, kx, kxe, inv):
    odd = parity()
    quad = lax.axis_index("quad")
    own, t_yl, t_yh, t_zl, t_zh = tables(got)
    bj = solve_lines([kz[z] for z in range(5)], [inv[z] for z in range(4)], [field[z] for z in range(4)])
    planes = [bj[z] + look_up(own, sub[z]) for z in range(4)]
    below = choose(odd, core[...], near[...]) + look_up(t_zl, zsub[0])
    above = choose(odd, near[...], core[...]) + look_up(t_zh, zsub[1])
    before = gather_rows(got[jnp.maximum(quad - 1, 0)], 8, 4)
    after = gather_rows(got[jnp.minimum(quad + 1, 3)], 8, 4)
    before = jnp.where(jnp.broadcast_to(quad, before.shape) > 0, before, 0.0) + look_up(t_yl, ysub[...])[0:4, :]
    after = jnp.where(jnp.broadcast_to(quad, after.shape) < 3, after, 0.0) + look_up(t_yh, ysub[...])[4:8, :]
    line = [below] + planes + [above]
    rise = [kz[j] * (line[j + 1] - line[j]) for j in range(5)]
    images = []
    for z in range(4):
        v = planes[z]
        y_low = ky[z] * (v - y_before(v, before[z : z + 1, :]))
        y_high = y_after(y_low, kyt[z : z + 1, :] * (after[z : z + 1, :] - v[15:16, :]))
        x_low = kx[z] * (v - x_before(v))
        x_high = x_after(x_low)
        x_high = jnp.concatenate([x_high[:, :896], x_high[:, 896:] - kxe[z] * v[:, 896:]], axis=1)
        images.append((rise[z] - rise[z + 1]) + (y_low - y_high) + (x_low - x_high))
    return planes, images


def total_of(lefts, rights):
    acc = lefts[0] * rights[0]
    for a, b in zip(lefts[1:], rights[1:]):
        acc = acc + a * b
    return jnp.sum(jnp.sum(acc, axis=0, keepdims=True), axis=1, keepdims=True)


def first(
    ready, got, core, near, sub, zsub, ysub, kz, ky, kyt, kx, kxe, inv, rs, cols,
    z_out, q_out, to_core, to_near, ups, downs, pay, rows,
):
    ready(4)
    planes, images = apply(got, rs, core, near, sub, zsub, ysub, kz, ky, kyt, kx, kxe, inv)
    for z in range(4):
        z_out[z] = planes[z]
        q_out[z] = images[z]
    send_faces(
        solve_lines([kz[z] for z in range(5)], [inv[z] for z in range(4)], images), to_core, to_near, ups, downs
    )
    cin = jnp.broadcast_to(restrict(sub, q_out, rows, 1), (8, 64))
    ready(12)
    rz = total_of([rs[z] for z in range(4)], planes)
    pq = total_of(planes, images)
    lane = lane_of((1, 128))
    parts = []
    for q in range(4):
        part = lax.dot_general(
            cin, cols[q // 2][:, q % 2 * 64 : q % 2 * 64 + 64], (((1,), (1,)), ((), ())), precision=HIGH, preferred_element_type=F32
        )[0:1, :]
        part = jnp.concatenate([part, part], axis=1)
        parts.append(jnp.where(lane < 64, part, jnp.where(lane == 64, rz, jnp.where(lane == 65, pq, 0.0))))
    pay[...] = jnp.concatenate(parts + parts, axis=0)


def second(
    ready, got, core, near, sub, zsub, ysub, kz, ky, kyt, kx, kxe, inv, rs, z0, q0, dots,
    z_out, g_out, r_out, pay,
):
    ready(4)
    planes, images = apply(got, q0, core, near, sub, zsub, ysub, kz, ky, kyt, kx, kxe, inv)
    alpha = dots[0:1, 64:65] / dots[0:1, 65:66]
    ready(12)
    zs, gs, rr = [], [], []
    for z in range(4):
        rr.append(rs[z] - alpha * q0[z])
        zs.append(z0[z] - alpha * planes[z])
        gs.append(q0[z] - alpha * images[z])
        z_out[z] = zs[z]
        g_out[z] = gs[z]
        r_out[z] = rr[z]
    new = total_of(rr, zs)
    own = total_of(zs, gs)
    cross = total_of([z0[z] for z in range(4)], gs)
    lane = lane_of((8, 128))
    pay[...] = jnp.where(lane == 0, new, jnp.where(lane == 1, own, jnp.where(lane == 2, cross, 0.0)))


def last(ready, got, dots, z0, q0, z1, g1, r1, x_out, r_out):
    total = jnp.sum(got[...], axis=0, keepdims=True)
    new, own, cross = total[:, 0:1], total[:, 1:2], total[:, 2:3]
    rz, pq = dots[0:1, 64:65], dots[0:1, 65:66]
    alpha = rz / pq
    beta = new / rz
    step = new / (own + 2.0 * beta * cross + beta * beta * pq)
    for z in range(4):
        x_out[z] = alpha * z0[z] + step * (z1[z] + beta * z0[z])
        r_out[z] = r1[z] - step * (g1[z] + beta * q0[z])


def body(right_side, phase_label, density_gain, subdomain, block_factor, coupling):
    slabs = lax.axis_size("slab")
    fac, cou = block_factor[0], coupling[0]
    grid, plane, edge = sds(4, 16, 1024), sds(16, 1024), sds(4, 1024)
    quads = lax.axis_size("quad")
    within = [list(range(g + c, g + GROUP, 2)) for g in range(0, slabs, GROUP) for c in range(2)]
    planes = [list(range(g, g + GROUP * quads)) for g in range(0, slabs * quads, GROUP * quads)]
    between = [list(range(i, slabs, GROUP)) for i in range(GROUP)]
    with_core = [(i, i ^ 1) for i in range(slabs)]
    with_near = [(i, i + 1 if i % 2 else i - 1) for i in range(1, slabs - 1)]

    def exchange(value, axis, groups=None):
        return lax.all_to_all(value, axis, 0, 0, tiled=True, axis_index_groups=groups)

    def swap(to_core, to_near):
        return lax.ppermute(to_core, "slab", with_core), lax.ppermute(to_near, "slab", with_near)

    mob, core, near, rs, sub, fac, cou, pay = call(
        begin,
        (grid, sds(384, 128), sds(384, 128), grid, jax.ShapeDtypeStruct((4, 16, 1024), jnp.int32))
        + (sds(64, 256), sds(32, 128), sds(4, 128, 128)),
        [pltpu.VMEM((64, 128), F32)],
        (3, 0, 1, 2, 4, 5),
        (-8,),
    )(right_side, phase_label, density_gain, subdomain, fac, cou)
    core, near = swap(core, near)
    got = exchange(pay, "quad")
    cols, pay = call(share, (sds(2, 64, 128), sds(GROUP // 2, 40, 128)), (), (), (1,))(got, fac, cou)
    pay, core, near = lax.optimization_barrier((pay, core, near))
    own = exchange(pay, "slab", within)
    kz, ky, kyt, kx, kxe, inv, to_core, to_near, ups, downs, zsub, ysub, beside = call(
        setup,
        (sds(5, 16, 1024), grid, edge, grid, sds(4, 16, 128), grid, plane, plane, edge, edge)
        + (jax.ShapeDtypeStruct((2, 16, 1024), jnp.int32), jax.ShapeDtypeStruct((8, 1024), jnp.int32), sds(2, 64, 256)),
        (),
        (),
        (-9, -10),
    )(rs, mob, core, near, got)
    own, to_core, to_near = lax.optimization_barrier((own, to_core, to_near))
    other = lax.ppermute(own, "slab", with_core)
    pay, rhs = call(
        condense_first,
        (sds(4, 104, 128), sds(GROUP, 128)),
        [pltpu.VMEM((64, GROUP * 64), F32)],
        (),
        (0,),
    )(own, other)
    pay, to_core, to_near = lax.optimization_barrier((pay, to_core, to_near))
    bj_core, bj_near = swap(to_core, to_near)
    bounds = exchange(pay, "slab", between)
    work = [
        pltpu.VMEM((8, 128), F32),
        pltpu.VMEM((8, 128), F32),
        pltpu.VMEM((5, 64, 128), F32),
        pltpu.VMEM((GROUP + 8, 128), F32),
        pltpu.VMEM((GROUP + 2, 64, 128), F32),
    ]
    part = call(chain_first, sds(4, 40, 128), work, (6, 7), (-1,))(
        bounds, own, other, rhs, fac, beside, ups, downs
    )
    coarse = exchange(part, "quad")
    stencil = (sub, zsub, ysub, kz, ky, kyt, kx, kxe, inv, rs)
    z0, q0, to_core, to_near, ups, downs, pay = call(
        first,
        (grid, grid, plane, plane, edge, edge, sds(8, 8, 128)),
        [pltpu.VMEM((64, 128), F32)],
        (),
        (-5, -6, 6),
    )(coarse, bj_core, bj_near, *stencil, cols)
    plane_rows = exchange(pay.reshape(64, 1, 128), BOTH, planes).reshape(64, 128)
    bj_core, bj_near = swap(to_core, to_near)
    pay, rhs = call(condense_second, (sds(4, 8, 128), sds(GROUP, 128)), (), (), (0,))(plane_rows, own, other)
    vecs = exchange(pay, "slab", between)
    part, dots = call(chain_second, (sds(4, 40, 128), sds(8, 128)), work, (7, 8), (-1,))(
        bounds, vecs, own, other, rhs, fac, beside, ups, downs
    )
    coarse = exchange(part, "quad")
    z1, g1, r1, pay = call(second, (grid, grid, grid, sds(32, 8, 128)), (), (), (3,))(
        coarse, bj_core, bj_near, *stencil, z0, q0, dots
    )
    everyone = exchange(pay.reshape(256, 1, 128), BOTH).reshape(256, 128)
    return tuple(call(last, (grid, grid))(everyone, dots, z0, q0, z1, g1, r1))


def solution(mesh):
    spec = P("slab", "quad", None)
    return jax.shard_map(body, mesh=mesh, in_specs=(spec,) * 6, out_specs=(spec, spec), check_vma=False)
```
